32 devices in a mesh: shard: 8 (over y, x, core), replica: 4 (over z).
Axes of the slice: x: 2, y: 2, z: 4, core: 2. Of those that a mesh axis runs over, the one named last changes fastest.
Arguments:
- hidden: bfloat16 [8192, 768], P(('replica', 'shard')), may hold values from -6 to 6
- segment_ids: int32 [8192], P(('replica', 'shard')), may hold values from 0 to 63, as said below
- w_qkv: bfloat16 [768, 2304], P('shard'), may hold values from -0.21875 to 0.21875
- b_qv: bfloat16 [2, 768], P(None, 'shard'), may hold values from -3 to 3
- w_out: bfloat16 [768, 768], P('shard'), may hold values from -3 to 3
- b_out: bfloat16 [768], P('shard'), may hold values from -3 to 3
- gain1: bfloat16 [768], P('shard'), may hold values from 0.5 to 1.5
- shift1: bfloat16 [768], P('shard'), may hold values from -3 to 3
- w_in: bfloat16 [768, 3072], P('shard'), may hold values from -0.21875 to 0.21875
- b_in: bfloat16 [3072], P('shard'), may hold values from -3 to 3
- w_back: bfloat16 [3072, 768], P('shard'), may hold values from -0.21875 to 0.21875
- b_back: bfloat16 [768], P('shard'), may hold values from -3 to 3
- gain2: bfloat16 [768], P('shard'), may hold values from 0.5 to 1.5
- shift2: bfloat16 [768], P('shard'), may hold values from -3 to 3
- cotangent: float32 [8192, 768], P(('replica', 'shard')), may hold values from -6 to 6
Outputs:
- output: bfloat16 [8192, 768], P(('replica', 'shard'))
- d_hidden: float32 [8192, 768], P(('replica', 'shard'))
- grad_w_qkv: float32 [768, 2304], P('shard')
- grad_b_qv: float32 [2, 768], P(None, 'shard')
- grad_w_out: float32 [768, 768], P('shard')
- grad_b_out: float32 [768], P('shard')
- grad_gain1: float32 [768], P('shard')
- grad_shift1: float32 [768], P('shard')
- grad_w_in: float32 [768, 3072], P('shard')
- grad_b_in: float32 [3072], P('shard')
- grad_w_back: float32 [3072, 768], P('shard')
- grad_b_back: float32 [768], P('shard')
- grad_gain2: float32 [768], P('shard')
- grad_shift2: float32 [768], P('shard')
The draws below stay inside these ranges and needn't reach their ends.
Inputs may be any that keep to these rules, and one draw needn't show every extreme that they name: `segment_ids`: ids never fall along the tokens. Sequence s (tokens s * 2048 to (s + 1) * 2048 - 1) holds exactly 16 documents with ids s * 16 to s * 16 + 15, one of them 1280 tokens long.
All inputs are finite; a program needn't handle non-finite values.
Results may differ from the reference program's by a relative error of at most 0.023.
Values may be sent and summed in bfloat16 or wider, within the bound.
A program may use at most 192 MiB of HBM per device.

```python
import math
import jax
import jax.numpy as jnp
from jax import lax

D = 768
HEADS = 12
HEAD_DIM = 64
FF = 3072
SEGS = 16
SEQ_LEN = 2048
SEQS = 4
TOKENS = 8192
LONG = 1280


def draw_segment_ids(key, part):
    rest = SEQ_LEN - LONG
    cut_keys = jax.random.split(jax.random.fold_in(key, 11), SEQS)

    def cuts_of(one_key):
        return jax.random.permutation(one_key, rest - 1)[:SEGS - 2] + 1
    cuts = jax.vmap(cuts_of)(cut_keys).astype(jnp.int32)
    choose = jax.random.randint(jax.random.fold_in(key, 12), (SEQS, 1), 0, SEGS).astype(jnp.int32)
    bounds = jnp.concatenate([jnp.zeros((SEQS, 1), jnp.int32), cuts, jnp.full((SEQS, 1), rest, jnp.int32)], axis=1)
    insert = jnp.take_along_axis(bounds, choose, axis=1)
    positions = jnp.arange(SEQ_LEN, dtype=jnp.int32)[None, :]
    before = positions < insert
    inside = jnp.logical_and(jnp.logical_not(before), positions < insert + LONG)
    rest_pos = jnp.where(before, positions, positions - LONG)
    rank = jnp.sum((cuts[:, :, None] <= rest_pos[:, None, :]).astype(jnp.int32), axis=1)
    long_id = jnp.sum((cuts <= insert).astype(jnp.int32), axis=1, keepdims=True) + (insert == rest).astype(jnp.int32)
    local_ids = jnp.where(before, rank, jnp.where(inside, long_id, rank + 1))
    ids = local_ids + jnp.arange(SEQS, dtype=jnp.int32)[:, None] * SEGS
    return ids.reshape(TOKENS).astype(jnp.int32)


def block_scale(own_key, extent, cuts, smallest, largest):
    loudness, own = 1.0, jax.random.fold_in(own_key, 6)
    for dim, shards_of in cuts:
        steps = jnp.exp(jax.random.uniform(jax.random.fold_in(own, dim), (shards_of,), jnp.float32, smallest / len(cuts), largest / len(cuts)))
        loudness = loudness * jnp.repeat(steps, extent[dim] // shards_of).reshape([-1 if axis == dim else 1 for axis in range(len(extent))])
    return loudness


def bell_draw(own_key, dims, width, limit, shards=(), kind=jnp.bfloat16):
    values = jax.random.normal(own_key, dims, jnp.float32) * width
    if len(shards) > 0:
        values = block_scale(own_key, dims, shards, -0.22, 0.18) * values
    return jnp.clip(values, min=-limit, max=limit).astype(kind)


def setup_inputs(seed: int = 0) -> dict:
    key_of = jax.random.split(jax.random.key(seed), 16)
    return {
        "hidden": bell_draw(key_of[0], (TOKENS, D), 1.0, 6.0, ((0, 32),)),
        "segment_ids": draw_segment_ids(jax.random.fold_in(key_of[15], 71), 0),
        "w_qkv": bell_draw(key_of[2], (D, 3 * D), D ** -0.5, 0.21875, ((0, 8),)),
        "b_qv": bell_draw(key_of[3], (2, D), 0.5, 3.0, ((1, 8),)),
        "w_out": bell_draw(key_of[4], (D, D), 4 ** -0.5, 3.0, ((0, 8),)),
        "b_out": bell_draw(key_of[5], (D,), 0.5, 3.0, ((0, 8),)),
        "gain1": jnp.clip(1.0 + 0.1 * jax.random.normal(key_of[6], (D,), jnp.float32), 0.5, 1.5).astype(jnp.bfloat16),
        "shift1": bell_draw(key_of[7], (D,), 0.5, 3.0, ((0, 8),)),
        "w_in": bell_draw(key_of[8], (D, FF), D ** -0.5, 0.21875, ((0, 8),)),
        "b_in": bell_draw(key_of[9], (FF,), 0.5, 3.0, ((0, 8),)),
        "w_back": bell_draw(key_of[10], (FF, D), (FF // 4) ** -0.5, 0.21875, ((0, 8),)),
        "b_back": bell_draw(key_of[11], (D,), 0.5, 3.0, ((0, 8),)),
        "gain2": jnp.clip(1.0 + 0.1 * jax.random.normal(key_of[12], (D,), jnp.float32), 0.5, 1.5).astype(jnp.bfloat16),
        "shift2": bell_draw(key_of[13], (D,), 0.5, 3.0, ((0, 8),)),
        "cotangent": bell_draw(key_of[14], (TOKENS, D), 1.0, 6.0, ((0, 32),), jnp.float32),
    }


highest = lax.Precision.HIGHEST
norm_epsilon = 1e-05

@jax.custom_vjp
def low(v):
    return lax.optimization_barrier(v.astype(jnp.bfloat16)).astype(jnp.float32)

@jax.custom_vjp
def low_back(v):
    return v

def low_keep(v):
    return (low(v), None)

def low_pass(kept, grad):
    return (grad,)

def back_keep(v):
    return (v, None)

def back_low(kept, grad):
    return (low(grad),)
low.defvjp(low_keep, low_pass)
low_back.defvjp(back_keep, back_low)

def matmul(left, right):
    return jnp.dot(left, right, precision=highest, preferred_element_type=jnp.float32)

def normalize(resid, gain, shift):
    mean_value = lax.optimization_barrier(jnp.mean(resid, axis=-1, keepdims=True))
    centered = resid - mean_value
    variance = lax.optimization_barrier(jnp.mean(centered * centered, axis=-1, keepdims=True))
    return centered * lax.rsqrt(variance + norm_epsilon) * gain + shift

def attend_block(query_block, seg_block, key_seq, value_seq, seg_keys):
    scores = low_back(jnp.einsum('qhd,khd->hqk', query_block, key_seq, precision=highest) * 0.125)
    allowed = (seg_block[:, None] == seg_keys[None, :])[None]
    scores = jnp.where(allowed, scores, -1e+30)
    top_score = lax.optimization_barrier(jnp.max(scores, axis=-1, keepdims=True))
    weights = jnp.exp(scores - top_score)
    probs = low(weights / lax.optimization_barrier(jnp.sum(weights, axis=-1, keepdims=True)))
    return jnp.einsum('hqk,khd->qhd', probs, value_seq, precision=highest)

def attend(query, key_all, value_all, segment_ids):
    block = math.gcd(SEQ_LEN, 512)
    query_blocks = query.reshape(SEQS, SEQ_LEN // block, block, HEADS, HEAD_DIM)
    seg_blocks = segment_ids.reshape(SEQS, SEQ_LEN // block, block)
    key_seqs = key_all.reshape(SEQS, SEQ_LEN, HEADS, HEAD_DIM)
    value_seqs = value_all.reshape(SEQS, SEQ_LEN, HEADS, HEAD_DIM)
    seg_seqs = segment_ids.reshape(SEQS, SEQ_LEN)

    def one_sequence(items):
        query_seq, seg_query, key_seq, value_seq, seg_keys = items

        def one_block(pair):
            return attend_block(pair[0], pair[1], key_seq, value_seq, seg_keys)
        return lax.map(jax.checkpoint(one_block), (query_seq, seg_query))
    result = lax.map(one_sequence, (query_blocks, seg_blocks, key_seqs, value_seqs, seg_seqs))
    return result.reshape(TOKENS, D)

def layer(hidden, w_qkv, b_qv, w_out, b_out, gain1, shift1, w_in, b_in, w_back, b_back, gain2, shift2, segment_ids):
    qkv = low_back(matmul(hidden, w_qkv))
    query = low(qkv[:, :D] + b_qv[0])
    key_all = low(qkv[:, D:2 * D])
    value_all = low(qkv[:, 2 * D:] + b_qv[1])
    context = attend(query, key_all, value_all, segment_ids)
    context = low_back(low(context))
    resid1 = hidden + low_back(matmul(context, w_out)) + b_out
    normed1 = normalize(resid1, gain1, shift1)
    pre = low_back(matmul(low(normed1), w_in)) + b_in
    act = low(jax.nn.gelu(pre, approximate=False))
    resid2 = normed1 + low_back(matmul(act, w_back)) + b_back
    return normalize(resid2, gain2, shift2)

def reference(hidden, segment_ids, w_qkv, b_qv, w_out, b_out, gain1, shift1, w_in, b_in, w_back, b_back, gain2, shift2, cotangent):
    floats = [param.astype(jnp.float32) for param in (hidden, w_qkv, b_qv, w_out, b_out, gain1, shift1, w_in, b_in, w_back, b_back, gain2, shift2)]

    def forward(*params):
        return layer(*params, segment_ids)
    out32, pull = jax.vjp(forward, *floats)
    grads = pull(cotangent.astype(jnp.float32))
    return (out32.astype(jnp.bfloat16), grads[0], grads[1], grads[2], grads[3], grads[4], grads[5], grads[6], grads[7], grads[8], grads[9], grads[10], grads[11], grads[12])
```

```python
import functools
import math

import jax
import jax.numpy as jnp
from jax import lax
from jax.experimental import pallas as pl
from jax.experimental.pallas import tpu as pltpu
from jax.sharding import PartitionSpec as P

HEADS = 12


scale_factor = 0.125
norm_epsilon = 1e-05
masked_value = -1e30


def normalize(resid, gain, shift):
    mean_value = jnp.mean(resid, axis=-1, keepdims=True)
    centered = resid - mean_value
    variance = jnp.mean(centered * centered, axis=-1, keepdims=True)
    return centered * lax.rsqrt(variance + norm_epsilon) * gain + shift


def gelu_exact(values):
    return jax.nn.gelu(values, approximate=False)


def keep_state(state):
    return state


def block_size(count):
    return math.gcd(count, 512)


def masked_scores(query_heads, key_heads, query_segs, key_segs):
    scores = (
        jnp.einsum("qhd,khd->hqk", query_heads, key_heads, preferred_element_type=jnp.float32)
        * scale_factor
    )
    allowed = query_segs[:, None] == key_segs[None, :]
    return (scores, allowed[None])


def grad_block(
    query_heads, dctx_heads, log_total, delta, query_segs, key_heads, value_heads, key_segs
):
    scores, allowed = masked_scores(query_heads, key_heads, query_segs, key_segs)
    probs = jnp.where(allowed, jnp.exp(scores - log_total[:, :, None]), 0.0)
    d_prob = jnp.einsum("qhd,khd->hqk", dctx_heads, value_heads, preferred_element_type=jnp.float32)
    d_scores = (probs * (d_prob - delta[:, :, None])).astype(jnp.bfloat16)
    return (probs.astype(jnp.bfloat16), d_scores)


def plain_body(
    hidden,
    segment_ids,
    w_qkv,
    b_qv,
    w_out,
    b_out,
    gain1,
    shift1,
    w_in,
    b_in,
    w_back,
    b_back,
    gain2,
    shift2,
    cotangent,
):
    tok_rows, width = hidden.shape
    heads = HEADS
    head_dim = width // heads
    seg_low = segment_ids[0]
    seg_high = segment_ids[-1]
    wq_full, wo_full, bqv_full, bo_full, g1_full, s1_full = (
        lax.all_gather(w_qkv, "shard", axis=0, tiled=True),
        lax.all_gather(w_out, "shard", axis=0, tiled=True),
        lax.all_gather(b_qv, "shard", axis=1, tiled=True),
        lax.all_gather(b_out, "shard", axis=0, tiled=True),
        lax.all_gather(gain1, "shard", axis=0, tiled=True),
        lax.all_gather(shift1, "shard", axis=0, tiled=True),
    )
    qkv = jnp.dot(hidden, wq_full, preferred_element_type=jnp.float32)
    bqv_wide = bqv_full.astype(jnp.float32)
    query = (qkv[:, :width] + bqv_wide[0]).astype(jnp.bfloat16)
    keys = qkv[:, width : 2 * width].astype(jnp.bfloat16)
    values = (qkv[:, 2 * width :] + bqv_wide[1]).astype(jnp.bfloat16)
    query_heads = query.reshape(tok_rows, heads, head_dim)
    key_local = keys.reshape(tok_rows, heads, head_dim)
    value_local = values.reshape(tok_rows, heads, head_dim)
    start_state = (
        jnp.full((heads, tok_rows), masked_value, jnp.float32),
        jnp.zeros((heads, tok_rows), jnp.float32),
        jnp.zeros((tok_rows, heads, head_dim), jnp.float32),
    )
    key_piece = lax.all_gather(keys, "shard", axis=0, tiled=True)
    value_piece = lax.all_gather(values, "shard", axis=0, tiled=True)
    seg_piece = lax.all_gather(segment_ids, "shard", axis=0, tiled=True)
    count = key_piece.shape[0]
    block = block_size(count)

    def forward_step(index, state):
        offset = index * block
        key_heads = lax.dynamic_slice_in_dim(key_piece, offset, block, 0).reshape(
            block, heads, head_dim
        )
        value_heads = lax.dynamic_slice_in_dim(value_piece, offset, block, 0).reshape(
            block, heads, head_dim
        )
        key_segs = lax.dynamic_slice_in_dim(seg_piece, offset, block, 0)

        def forward_update(state):
            running_max, running_sum, accum = state
            scores, allowed = masked_scores(query_heads, key_heads, segment_ids, key_segs)
            new_max = jnp.maximum(
                running_max, jnp.max(jnp.where(allowed, scores, masked_value), axis=-1)
            )
            factor = jnp.exp(running_max - new_max)
            weights = jnp.where(allowed, jnp.exp(scores - new_max[:, :, None]), 0.0)
            running_sum = running_sum * factor + jnp.sum(weights, axis=-1)
            accum = accum * factor.T[:, :, None] + jnp.einsum(
                "hqk,khd->qhd",
                weights.astype(jnp.bfloat16),
                value_heads,
                preferred_element_type=jnp.float32,
            )
            return (new_max, running_sum, accum)

        touches = jnp.logical_and(key_segs[0] <= seg_high, key_segs[-1] >= seg_low)
        return lax.cond(touches, forward_update, keep_state, state)

    running_max, running_sum, accum = lax.fori_loop(0, count // block, forward_step, start_state)
    context32 = accum / running_sum.T[:, :, None]
    log_total = running_max + jnp.log(running_sum)
    context = context32.reshape(tok_rows, width).astype(jnp.bfloat16)
    resid1 = (
        hidden.astype(jnp.float32)
        + jnp.dot(context, wo_full, preferred_element_type=jnp.float32)
        + bo_full.astype(jnp.float32)
    )
    normed1, norm1_pull = jax.vjp(
        normalize, resid1, g1_full.astype(jnp.float32), s1_full.astype(jnp.float32)
    )
    wi_full, bi_full, wb_full, bb_full, g2_full, s2_full = (
        lax.all_gather(w_in, "shard", axis=0, tiled=True),
        lax.all_gather(b_in, "shard", axis=0, tiled=True),
        lax.all_gather(w_back, "shard", axis=0, tiled=True),
        lax.all_gather(b_back, "shard", axis=0, tiled=True),
        lax.all_gather(gain2, "shard", axis=0, tiled=True),
        lax.all_gather(shift2, "shard", axis=0, tiled=True),
    )
    normed1_low = normed1.astype(jnp.bfloat16)
    pre = jnp.dot(normed1_low, wi_full, preferred_element_type=jnp.float32) + bi_full.astype(
        jnp.float32
    )
    act, gelu_pull = jax.vjp(gelu_exact, pre)
    act_low = act.astype(jnp.bfloat16)
    resid2 = (
        normed1
        + jnp.dot(act_low, wb_full, preferred_element_type=jnp.float32)
        + bb_full.astype(jnp.float32)
    )
    out32, norm2_pull = jax.vjp(
        normalize, resid2, g2_full.astype(jnp.float32), s2_full.astype(jnp.float32)
    )
    output = out32.astype(jnp.bfloat16)
    d_resid2, grad_gain2, grad_shift2 = norm2_pull(cotangent)
    d_branch2 = d_resid2.astype(jnp.bfloat16)
    grad_b_back = jnp.sum(d_resid2, axis=0)
    grad_w_back = jnp.einsum("tf,td->fd", act_low, d_branch2, preferred_element_type=jnp.float32)
    d_act = jnp.einsum("td,fd->tf", d_branch2, wb_full, preferred_element_type=jnp.float32)
    (d_pre,) = gelu_pull(d_act)
    grad_b_in = jnp.sum(d_pre, axis=0)
    d_pre_low = d_pre.astype(jnp.bfloat16)
    grad_w_in = jnp.einsum("td,tf->df", normed1_low, d_pre_low, preferred_element_type=jnp.float32)
    d_normed1 = d_resid2 + jnp.einsum(
        "tf,df->td", d_pre_low, wi_full, preferred_element_type=jnp.float32
    )
    d_resid1, grad_gain1, grad_shift1 = norm1_pull(d_normed1)
    grad_b_out = jnp.sum(d_resid1, axis=0)
    d_branch1 = d_resid1.astype(jnp.bfloat16)
    grad_w_out = jnp.einsum("tc,td->cd", context, d_branch1, preferred_element_type=jnp.float32)
    d_context = jnp.einsum(
        "td,cd->tc", d_branch1, wo_full, preferred_element_type=jnp.float32
    ).astype(jnp.bfloat16)
    dctx_heads = d_context.reshape(tok_rows, heads, head_dim)
    delta = jnp.einsum("qhd,qhd->hq", dctx_heads.astype(jnp.float32), context32)
    zero_heads = jnp.zeros((tok_rows, heads, head_dim), jnp.float32)
    query_key_piece = lax.all_gather(keys, "shard", axis=0, tiled=True)
    query_value_piece = lax.all_gather(values, "shard", axis=0, tiled=True)
    query_seg_piece = lax.all_gather(segment_ids, "shard", axis=0, tiled=True)
    count = query_key_piece.shape[0]
    query_block = block_size(count)

    def query_step(index, summed):
        offset = index * query_block
        key_heads = lax.dynamic_slice_in_dim(query_key_piece, offset, query_block, 0).reshape(
            query_block, heads, head_dim
        )
        value_heads = lax.dynamic_slice_in_dim(query_value_piece, offset, query_block, 0).reshape(
            query_block, heads, head_dim
        )
        key_segs = lax.dynamic_slice_in_dim(query_seg_piece, offset, query_block, 0)

        def query_update(summed):
            probs, d_scores = grad_block(
                query_heads,
                dctx_heads,
                log_total,
                delta,
                segment_ids,
                key_heads,
                value_heads,
                key_segs,
            )
            return (
                summed
                + jnp.einsum(
                    "hqk,khd->qhd", d_scores, key_heads, preferred_element_type=jnp.float32
                )
                * scale_factor
            )

        touches = jnp.logical_and(key_segs[0] <= seg_high, key_segs[-1] >= seg_low)
        return lax.cond(touches, query_update, keep_state, summed)

    d_query = lax.fori_loop(0, count // query_block, query_step, zero_heads)
    all_log_total, all_delta = (
        lax.all_gather(log_total, "shard", axis=1, tiled=True),
        lax.all_gather(delta, "shard", axis=1, tiled=True),
    )
    query_piece = lax.all_gather(query, "shard", axis=0, tiled=True)
    dctx_piece = lax.all_gather(d_context, "shard", axis=0, tiled=True)
    key_seg_piece = lax.all_gather(segment_ids, "shard", axis=0, tiled=True)
    count = query_piece.shape[0]
    key_block = block_size(count)

    def key_step(index, state):
        offset = index * key_block
        piece_query = lax.dynamic_slice_in_dim(query_piece, offset, key_block, 0).reshape(
            key_block, heads, head_dim
        )
        piece_dctx = lax.dynamic_slice_in_dim(dctx_piece, offset, key_block, 0).reshape(
            key_block, heads, head_dim
        )
        piece_segs = lax.dynamic_slice_in_dim(key_seg_piece, offset, key_block, 0)
        piece_log = lax.dynamic_slice_in_dim(all_log_total, offset, key_block, 1)
        piece_delta = lax.dynamic_slice_in_dim(all_delta, offset, key_block, 1)

        def key_update(state):
            d_key, d_value = state
            probs, d_scores = grad_block(
                piece_query,
                piece_dctx,
                piece_log,
                piece_delta,
                piece_segs,
                key_local,
                value_local,
                segment_ids,
            )
            d_key = (
                d_key
                + jnp.einsum(
                    "hqk,qhd->khd", d_scores, piece_query, preferred_element_type=jnp.float32
                )
                * scale_factor
            )
            d_value = d_value + jnp.einsum(
                "hqk,qhd->khd", probs, piece_dctx, preferred_element_type=jnp.float32
            )
            return (d_key, d_value)

        touches = jnp.logical_and(piece_segs[0] <= seg_high, piece_segs[-1] >= seg_low)
        return lax.cond(touches, key_update, keep_state, state)

    d_key_heads, d_value_heads = lax.fori_loop(
        0, count // key_block, key_step, (zero_heads, zero_heads)
    )
    d_keys = d_key_heads.reshape(tok_rows, width)
    d_values = d_value_heads.reshape(tok_rows, width)
    d_query = d_query.reshape(tok_rows, width)
    grad_b_qv = jnp.stack([jnp.sum(d_query, axis=0), jnp.sum(d_values, axis=0)], axis=0)
    d_qkv = jnp.concatenate([d_query, d_keys, d_values], axis=1).astype(jnp.bfloat16)
    grad_w_qkv = jnp.einsum("td,te->de", hidden, d_qkv, preferred_element_type=jnp.float32)
    d_hidden = d_resid1 + jnp.einsum(
        "te,de->td", d_qkv, wq_full, preferred_element_type=jnp.float32
    )
    local_grads = (
        grad_w_qkv,
        grad_b_qv,
        grad_w_out,
        grad_b_out,
        grad_gain1,
        grad_shift1,
        grad_w_in,
        grad_b_in,
        grad_w_back,
        grad_b_back,
        grad_gain2,
        grad_shift2,
    )
    shard_grads = (
        lax.psum_scatter(
            local_grads[0].astype(jnp.bfloat16), "shard", scatter_dimension=0, tiled=True
        ).astype(jnp.float32),
        lax.psum_scatter(
            local_grads[1].astype(jnp.bfloat16), "shard", scatter_dimension=1, tiled=True
        ).astype(jnp.float32),
        lax.psum_scatter(
            local_grads[2].astype(jnp.bfloat16), "shard", scatter_dimension=0, tiled=True
        ).astype(jnp.float32),
        lax.psum_scatter(
            local_grads[3].astype(jnp.bfloat16), "shard", scatter_dimension=0, tiled=True
        ).astype(jnp.float32),
        lax.psum_scatter(
            local_grads[4].astype(jnp.bfloat16), "shard", scatter_dimension=0, tiled=True
        ).astype(jnp.float32),
        lax.psum_scatter(
            local_grads[5].astype(jnp.bfloat16), "shard", scatter_dimension=0, tiled=True
        ).astype(jnp.float32),
        lax.psum_scatter(
            local_grads[6].astype(jnp.bfloat16), "shard", scatter_dimension=0, tiled=True
        ).astype(jnp.float32),
        lax.psum_scatter(
            local_grads[7].astype(jnp.bfloat16), "shard", scatter_dimension=0, tiled=True
        ).astype(jnp.float32),
        lax.psum_scatter(
            local_grads[8].astype(jnp.bfloat16), "shard", scatter_dimension=0, tiled=True
        ).astype(jnp.float32),
        lax.psum_scatter(
            local_grads[9].astype(jnp.bfloat16), "shard", scatter_dimension=0, tiled=True
        ).astype(jnp.float32),
        lax.psum_scatter(
            local_grads[10].astype(jnp.bfloat16), "shard", scatter_dimension=0, tiled=True
        ).astype(jnp.float32),
        lax.psum_scatter(
            local_grads[11].astype(jnp.bfloat16), "shard", scatter_dimension=0, tiled=True
        ).astype(jnp.float32),
    )
    total_grads = (
        lax.psum(shard_grads[0].astype(jnp.bfloat16), "replica").astype(jnp.float32),
        lax.psum(shard_grads[1].astype(jnp.bfloat16), "replica").astype(jnp.float32),
        lax.psum(shard_grads[2].astype(jnp.bfloat16), "replica").astype(jnp.float32),
        lax.psum(shard_grads[3].astype(jnp.bfloat16), "replica").astype(jnp.float32),
        lax.psum(shard_grads[4].astype(jnp.bfloat16), "replica").astype(jnp.float32),
        lax.psum(shard_grads[5].astype(jnp.bfloat16), "replica").astype(jnp.float32),
        lax.psum(shard_grads[6].astype(jnp.bfloat16), "replica").astype(jnp.float32),
        lax.psum(shard_grads[7].astype(jnp.bfloat16), "replica").astype(jnp.float32),
        lax.psum(shard_grads[8].astype(jnp.bfloat16), "replica").astype(jnp.float32),
        lax.psum(shard_grads[9].astype(jnp.bfloat16), "replica").astype(jnp.float32),
        lax.psum(shard_grads[10].astype(jnp.bfloat16), "replica").astype(jnp.float32),
        lax.psum(shard_grads[11].astype(jnp.bfloat16), "replica").astype(jnp.float32),
    )
    return (output, d_hidden) + tuple(total_grads)


PLANE = 8
LINE = 4
CHIPS = 4
MESH = pl.DeviceIdType.MESH
VMEM = pltpu.VMEM
ANY = pl.ANY
f32 = jnp.float32
bf16 = jnp.bfloat16


class Wires:
    def __init__(self, send, recv):
        self.send, self.recv, self.used = send, recv, 0
        me = lax.axis_index("shard")
        self.me = me
        self.core = me % 2
        self.chip = me // 2
        self.mate = me + 1 - 2 * self.core
        self.xn = me + 2 - 4 * (self.chip % 2)
        self.yn = me + 4 - 8 * (me // 4)
        self.dn = self.xn + 4 - 8 * (me // 4)
        self.cx = self.xn // 2
        self.cy = self.yn // 2
        self.cd = self.dn // 2

    def copy(self, src, dst, where):
        slot = self.used
        self.used += 1
        return pltpu.make_async_remote_copy(
            src_ref=src,
            dst_ref=dst,
            send_sem=self.send.at[slot],
            recv_sem=self.recv.at[slot],
            device_id=where if isinstance(where, dict) else {"shard": where},
            device_id_type=MESH,
        )

    def start(self, src, dst, where):
        made = self.copy(src, dst, where)
        made.start()
        return made


def greet(others):
    barrier = pltpu.get_barrier_semaphore()
    for other in others:
        pl.semaphore_signal(barrier, inc=1, device_id=other, device_id_type=MESH)
    pl.semaphore_wait(barrier, len(others))


def plane_others(me):
    return [{"shard": (me + step) % PLANE} for step in range(1, PLANE)]


def call(kernel, ins, outs, scratch, ident, in_spaces, out_spaces, name):
    return pl.pallas_call(
        kernel,
        out_shape=outs,
        in_specs=[pl.BlockSpec(memory_space=space) for space in in_spaces],
        out_specs=[pl.BlockSpec(memory_space=space) for space in out_spaces],
        scratch_shapes=scratch,
        compiler_params=pltpu.CompilerParams(
            collective_id=ident, has_side_effects=True, vmem_limit_bytes=60 << 20
        ),
        name=name,
    )(*ins)


def dma_sems(count):
    return [pltpu.SemaphoreType.DMA((count,)), pltpu.SemaphoreType.DMA((count,))]


class Gather:
    def __init__(self, wires, block, out, local_sem):
        w = self.w = wires
        self.out = out
        self.half = block.shape[0] // 2
        me = w.me
        self.own = pltpu.make_async_copy(block, out.at[me], local_sem)
        self.own.start()
        self.to_x = w.start(block, out.at[me], w.xn)
        self.to_y = w.start(block, out.at[me], w.yn)
        self.to_mate = w.start(block, out.at[me], w.mate)

    def relay(self):
        w, out, half = self.w, self.out, self.half
        low, high = pl.ds(0, half), pl.ds(half, half)
        self.to_x.wait_recv()
        self.x_on = w.start(out.at[w.xn, low], out.at[w.xn, low], w.yn)
        self.x_mate = w.start(out.at[w.xn], out.at[w.xn], w.mate)
        self.to_y.wait_recv()
        self.y_on = w.start(out.at[w.yn, high], out.at[w.yn, high], w.xn)
        self.y_mate = w.start(out.at[w.yn], out.at[w.yn], w.mate)

    def finish(self):
        w, out, half = self.w, self.out, self.half
        low, high = pl.ds(0, half), pl.ds(half, half)
        self.x_on.wait_recv()
        self.d_low = w.start(out.at[w.dn, low], out.at[w.dn, low], w.mate)
        self.y_on.wait_recv()
        self.d_high = w.start(out.at[w.dn, high], out.at[w.dn, high], w.mate)

    def done(self):
        for made in (self.to_mate, self.x_mate, self.y_mate, self.d_low, self.d_high):
            made.wait_recv()
        for made in (
            self.to_x,
            self.to_y,
            self.to_mate,
            self.x_on,
            self.x_mate,
            self.y_on,
            self.y_mate,
            self.d_low,
            self.d_high,
        ):
            made.wait_send()
        self.own.wait()


def gather_kernel(hid, wq, wo, wi, wb, small, hid_o, wq_o, wo_o, wi_o, wb_o, small_o, send, recv, loc):
    w = Wires(send, recv)
    greet(plane_others(w.me))
    me = w.me
    own_small = pltpu.make_async_copy(small, small_o.at[me], loc.at[0])
    own_small.start()
    smalls = [
        w.start(small, small_o.at[me], (me + step) % PLANE) for step in range(1, PLANE)
    ]
    first = Gather(w, hid, hid_o, loc.at[1])
    own_q = pltpu.make_async_copy(wq.at[w.chip], wq_o.at[me], loc.at[2])
    own_q.start()
    q_mate = w.start(wq.at[w.chip], wq_o.at[me], w.mate)
    q_x = w.start(wq.at[w.cx], wq_o.at[me], w.xn)
    q_y = w.start(wq.at[w.cy], wq_o.at[me], w.yn)
    q_d = w.start(wq.at[w.cd], wq_o.at[me], w.dn)
    rest = [
        Gather(w, block, out, loc.at[3 + slot])
        for slot, (block, out) in enumerate(((wo, wo_o), (wi, wi_o), (wb, wb_o)))
    ]
    first.relay()
    q_on = []
    for came, source in ((q_x, w.xn), (q_y, w.yn), (q_d, w.dn)):
        came.wait_recv()
        q_on.append(w.start(wq_o.at[source], wq_o.at[source], w.mate))
    first.finish()
    for one in rest:
        one.relay()
    for one in rest:
        one.finish()
    first.done()
    for one in rest:
        one.done()
    for made in [q_mate] + q_on + smalls:
        made.wait_recv()
    for made in [q_mate, q_x, q_y, q_d] + q_on + smalls:
        made.wait_send()
    own_small.wait()
    own_q.wait()


def gather_all(hid, wq, wo, wi, wb, small):
    outs = [
        jax.ShapeDtypeStruct((PLANE,) + one.shape, one.dtype) for one in (hid, wq, wo, wi, wb, small)
    ]
    outs[1] = jax.ShapeDtypeStruct((PLANE,) + wq.shape[1:], wq.dtype)
    return call(
        gather_kernel,
        (hid, wq, wo, wi, wb, small),
        outs,
        dma_sems(56) + [pltpu.SemaphoreType.DMA((8,))],
        1,
        [VMEM] * 6,
        [ANY] * 6,
        "gather_all",
    )


def swap_kernel(block, out, send, recv, loc):
    w = Wires(send, recv)
    greet([{"shard": one} for one in (w.xn, w.yn, w.dn)])
    own = pltpu.make_async_copy(block.at[w.chip], out.at[w.chip], loc.at[0])
    own.start()
    made = [
        w.start(block.at[chip], out.at[w.chip], who)
        for chip, who in ((w.cd, w.dn), (w.cx, w.xn), (w.cy, w.yn))
    ]
    for one in made:
        one.wait()
    own.wait()


def chip_swap(block, ident, name):
    return call(
        swap_kernel,
        (block,),
        [jax.ShapeDtypeStruct(block.shape, block.dtype)],
        dma_sems(4) + [pltpu.SemaphoreType.DMA((1,))],
        ident,
        [VMEM],
        [VMEM],
        name,
    )[0]


def mate_kernel(block, out, send, recv):
    w = Wires(send, recv)
    greet([{"shard": w.mate}])
    w.start(block.at[:, 1 - w.core], out, w.mate).wait()


def mate_swap(block, ident, name):
    shape = (block.shape[0],) + block.shape[2:]
    return call(
        mate_kernel,
        (block,),
        [jax.ShapeDtypeStruct(shape, block.dtype)],
        dma_sems(1),
        ident,
        [VMEM],
        [VMEM],
        name,
    )[0]


ROWS = 256


def attend_kernel(bound, q_ref, k_ref, v_ref, segq_ref, segk_ref, ctx_ref, low_ref, log_ref, *, hd):
    block = pl.program_id(0)
    heads = q_ref.shape[2] // hd
    query = q_ref[0]
    segq = segq_ref[0][:, 0:1]

    def step(index, state):
        rows = pl.ds(pl.multiple_of(index * ROWS, ROWS), ROWS)
        keys = k_ref[rows, :]
        values = v_ref[rows, :]
        allowed = segq == segk_ref[index]
        made = []
        for head in range(heads):
            top, total, acc = state[head]
            cols = slice(head * hd, (head + 1) * hd)
            scores = (
                lax.dot_general(
                    query[:, cols], keys[:, cols], (((1,), (1,)), ((), ())), preferred_element_type=f32
                )
                * scale_factor
            )
            scores = jnp.where(allowed, scores, masked_value)
            new = jnp.maximum(top, jnp.max(scores, axis=1, keepdims=True))
            weights = jnp.where(allowed, jnp.exp(scores - new), 0.0)
            factor = jnp.exp(top - new)
            total = total * factor + jnp.sum(weights, axis=1, keepdims=True)
            acc = acc * factor + lax.dot_general(
                weights.astype(bf16), values[:, cols], (((1,), (0,)), ((), ())), preferred_element_type=f32
            )
            made.append((new, total, acc))
        return tuple(made)

    zero = tuple(
        (
            jnp.full((ROWS, 1), masked_value, f32),
            jnp.zeros((ROWS, 1), f32),
            jnp.zeros((ROWS, hd), f32),
        )
        for _ in range(heads)
    )
    state = lax.fori_loop(bound[0, block], bound[1, block], step, zero)
    context = jnp.concatenate([acc / total for _, total, acc in state], axis=1)
    ctx_ref[0] = context
    low_ref[0] = context.astype(bf16)
    for head in range(heads):
        top, total, _ = state[head]
        log_ref[0, :, head : head + 1] = top + jnp.log(total)


def attend(bound, query, keys, values, segq, segk, hd):
    blocks, rows, wide = query.shape
    whole = lambda one: pl.BlockSpec(one.shape, lambda i, b: (0,) * one.ndim)
    per = lambda last: pl.BlockSpec((1, rows, last), lambda i, b: (i, 0, 0))
    return pl.pallas_call(
        functools.partial(attend_kernel, hd=hd),
        grid_spec=pltpu.PrefetchScalarGridSpec(
            num_scalar_prefetch=1,
            grid=(blocks,),
            in_specs=[per(wide), whole(keys), whole(values), per(128), whole(segk)],
            out_specs=[per(wide), per(wide), per(128)],
        ),
        out_shape=[
            jax.ShapeDtypeStruct((blocks, rows, wide), f32),
            jax.ShapeDtypeStruct((blocks, rows, wide), bf16),
            jax.ShapeDtypeStruct((blocks, rows, 128), f32),
        ],
        compiler_params=pltpu.CompilerParams(vmem_limit_bytes=48 << 20),
        name="attend",
    )(bound, query, keys, values, segq, segk)


def attend_back_kernel(
    bound, q_ref, k_ref, v_ref, segq_ref, segk_ref, ctx_ref, dctx_ref, log_ref, dq_ref, dk_ref, dv_ref, *, hd
):
    block = pl.program_id(0)
    heads = q_ref.shape[2] // hd

    @pl.when(block == 0)
    def _():
        dk_ref[...] = jnp.zeros_like(dk_ref)
        dv_ref[...] = jnp.zeros_like(dv_ref)

    query = q_ref[0]
    dctx = dctx_ref[0]
    segq = segq_ref[0][:, 0:1]
    product = dctx.astype(f32) * ctx_ref[0]
    delta = [
        jnp.sum(product[:, head * hd : (head + 1) * hd], axis=1, keepdims=True) for head in range(heads)
    ]

    def step(index, state):
        rows = pl.ds(pl.multiple_of(index * ROWS, ROWS), ROWS)
        keys = k_ref[rows, :]
        values = v_ref[rows, :]
        allowed = segq == segk_ref[index]
        made, dks, dvs = [], [], []
        for head in range(heads):
            cols = slice(head * hd, (head + 1) * hd)
            scores = (
                lax.dot_general(
                    query[:, cols], keys[:, cols], (((1,), (1,)), ((), ())), preferred_element_type=f32
                )
                * scale_factor
            )
            probs = jnp.where(allowed, jnp.exp(scores - log_ref[0, :, head : head + 1]), 0.0)
            d_prob = lax.dot_general(
                dctx[:, cols], values[:, cols], (((1,), (1,)), ((), ())), preferred_element_type=f32
            )
            d_scores = (probs * (d_prob - delta[head])).astype(bf16)
            made.append(
                state[head]
                + lax.dot_general(
                    d_scores, keys[:, cols], (((1,), (0,)), ((), ())), preferred_element_type=f32
                )
            )
            dks.append(
                lax.dot_general(
                    d_scores, query[:, cols], (((0,), (0,)), ((), ())), preferred_element_type=f32
                )
            )
            dvs.append(
                lax.dot_general(
                    probs.astype(bf16), dctx[:, cols], (((0,), (0,)), ((), ())), preferred_element_type=f32
                )
            )
        dk_ref[rows, :] += jnp.concatenate(dks, axis=1) * scale_factor
        dv_ref[rows, :] += jnp.concatenate(dvs, axis=1)
        return tuple(made)

    zero = tuple(jnp.zeros((ROWS, hd), f32) for _ in range(heads))
    state = lax.fori_loop(bound[0, block], bound[1, block], step, zero)
    dq_ref[0] = jnp.concatenate(state, axis=1) * scale_factor


def attend_back(bound, query, keys, values, segq, segk, ctx, dctx, log, hd):
    blocks, rows, wide = query.shape
    whole = lambda one: pl.BlockSpec(one.shape, lambda i, b: (0,) * len(one.shape))
    per = lambda last: pl.BlockSpec((1, rows, last), lambda i, b: (i, 0, 0))
    total = jax.ShapeDtypeStruct(keys.shape, f32)
    return pl.pallas_call(
        functools.partial(attend_back_kernel, hd=hd),
        grid_spec=pltpu.PrefetchScalarGridSpec(
            num_scalar_prefetch=1,
            grid=(blocks,),
            in_specs=[
                per(wide),
                whole(keys),
                whole(values),
                per(128),
                whole(segk),
                per(wide),
                per(wide),
                per(128),
            ],
            out_specs=[per(wide), whole(total), whole(total)],
        ),
        out_shape=[jax.ShapeDtypeStruct((blocks, rows, wide), f32), total, total],
        compiler_params=pltpu.CompilerParams(vmem_limit_bytes=48 << 20),
        name="attend_back",
    )(bound, query, keys, values, segq, segk, ctx, dctx, log)


def add_into(dst, other, out=None):
    out = dst if out is None else out
    lead = dst.shape[0] if len(dst.shape) == 3 else 0
    rows = dst.shape[-2]

    def go(index, carry):
        if lead:
            at = (index // (rows // 16), pl.ds(pl.multiple_of((index % (rows // 16)) * 16, 16), 16))
        else:
            at = (pl.ds(pl.multiple_of(index * 16, 16), 16),)
        out[at] = (dst[at].astype(f32) + other[at].astype(f32)).astype(out.dtype)
        return carry

    lax.fori_loop(0, max(lead, 1) * (rows // 16), go, 0)


class Reduce:
    def __init__(self, wires, full, pair, land, pick):
        self.w, self.full, self.pair, self.land = wires, full, pair, land
        self.half = pair.shape[1] // 2
        self.pick = pick
        if full is not None:
            self.meet = wires.start(pick(full, 1 - wires.core), pair, wires.mate)

    def first(self):
        w, pair, land = self.w, self.pair, self.land
        low, high = pl.ds(0, self.half), pl.ds(self.half, self.half)
        if self.full is not None:
            self.meet.wait_recv()
            add_into(pair, self.pick(self.full, w.core))
        self.x0 = w.start(pair.at[w.cd, low], land.at[1], w.xn)
        self.y0 = w.start(pair.at[w.cd, high], land.at[3], w.yn)
        self.x1 = w.start(pair.at[w.cx, low], land.at[0], w.xn)
        self.y1 = w.start(pair.at[w.cy, high], land.at[2], w.yn)

    def second(self):
        w, pair, land = self.w, self.pair, self.land
        low, high = pl.ds(0, self.half), pl.ds(self.half, self.half)
        self.x0.wait_recv()
        add_into(pair.at[w.cy, low], land.at[1])
        self.y2 = w.start(pair.at[w.cy, low], land.at[4], w.yn)
        self.y0.wait_recv()
        add_into(pair.at[w.cx, high], land.at[3])
        self.x2 = w.start(pair.at[w.cx, high], land.at[5], w.xn)
        self.x1.wait_recv()
        add_into(pair.at[w.chip, low], land.at[0])
        self.y1.wait_recv()
        add_into(pair.at[w.chip, high], land.at[2])

    def third(self, out):
        w, pair, land = self.w, self.pair, self.land
        low, high = pl.ds(0, self.half), pl.ds(self.half, self.half)
        self.y2.wait_recv()
        add_into(pair.at[w.chip, low], land.at[4], out.at[low])
        self.x2.wait_recv()
        add_into(pair.at[w.chip, high], land.at[5], out.at[high])

    def done(self):
        made = [self.x0, self.x1, self.y0, self.y1, self.x2, self.y2]
        if self.full is not None:
            made.append(self.meet)
        for one in made:
            one.wait_send()


class Line:
    def __init__(self, wires, z, block, land, out):
        self.w, self.z, self.block, self.land, self.out = wires, z, block, land, out
        self.edge = (z == 0) | (z == LINE - 1)
        self.inner = {"replica": 1 + z // 2}
        self.outer = {"replica": 3 * (z // 2)}
        self.across = {"replica": 2 - z // 2}
        self.up = wires.copy(block, land.at[0], self.inner)
        self.over = wires.copy(block, land.at[1], {"replica": 3 - z})
        self.back = wires.copy(out, out, self.outer)

    def first(self):
        @pl.when(self.edge)
        def _():
            self.up.start()

    def second(self):
        @pl.when(jnp.logical_not(self.edge))
        def _():
            self.up.wait_recv()
            add_into(self.block, self.land.at[0])
            self.over.start()

    def third(self):
        @pl.when(jnp.logical_not(self.edge))
        def _():
            self.over.wait_recv()
            add_into(self.block, self.land.at[1], self.out)
            self.back.start()

    def done(self):
        @pl.when(self.edge)
        def _():
            self.up.wait_send()
            self.back.wait_recv()

        @pl.when(jnp.logical_not(self.edge))
        def _():
            self.over.wait_send()
            self.back.wait_send()


def reduce_kernel(
    gq,
    gb,
    gi,
    go,
    dh,
    small,
    dq_o,
    db_o,
    di_o,
    do_o,
    dh_o,
    small_o,
    q_pair,
    q_all,
    pair,
    land,
    dh_land,
    part,
    s_land,
    s_sum,
    zq_land,
    z_land,
    zs_land,
    send,
    recv,
    loc,
):
    w = Wires(send, recv)
    z = lax.axis_index("replica")
    me = w.me
    barrier = pltpu.get_barrier_semaphore()
    for other in plane_others(me):
        pl.semaphore_signal(barrier, inc=1, device_id=other, device_id_type=MESH)
    edge = (z == 0) | (z == LINE - 1)

    @pl.when(edge)
    def _():
        pl.semaphore_signal(barrier, inc=1, device_id={"replica": 1 + z // 2}, device_id_type=MESH)
        pl.semaphore_wait(barrier, PLANE)

    @pl.when(jnp.logical_not(edge))
    def _():
        pl.semaphore_signal(barrier, inc=1, device_id={"replica": 3 * (z // 2)}, device_id_type=MESH)
        pl.semaphore_signal(barrier, inc=1, device_id={"replica": 3 - z}, device_id_type=MESH)
        pl.semaphore_wait(barrier, PLANE + 1)

    rows, cols = go.shape[2], go.shape[3]
    smalls = [
        w.start(small.at[(me + step) % PLANE], s_land.at[me], (me + step) % PLANE)
        for step in range(1, PLANE)
    ]
    own = pltpu.make_async_copy(small.at[me], s_land.at[me], loc.at[0])
    own.start()
    q_meet = w.start(gq.at[:, 1 - w.core], q_pair, w.mate)
    picks = []
    for slot in range(gb.shape[2] // rows):
        at = pl.ds(slot * rows, rows)
        picks.append((gb, lambda ref, core, at=at: ref.at[:, core, at], db_o.at[at]))
    for slot in range(gi.shape[3] // cols):
        at = pl.ds(slot * cols, cols)
        picks.append((gi, lambda ref, core, at=at: ref.at[:, core, :, at], di_o.at[:, at]))
    picks.append((go, lambda ref, core: ref.at[:, core], do_o))
    count = len(picks)
    chunks = [
        Reduce(w, full, pair.at[slot], land.at[slot], pick)
        for slot, (full, pick, _) in enumerate(picks)
    ]
    lines = [
        Line(w, z, part.at[slot], z_land.at[slot], out) for slot, (_, _, out) in enumerate(picks)
    ]
    q_meet.wait_recv()
    add_into(q_pair, gq.at[:, w.core])
    q_made = [
        w.start(q_pair.at[chip], q_all.at[w.chip], who)
        for chip, who in ((w.cd, w.dn), (w.cx, w.xn), (w.cy, w.yn))
    ]
    q_own = pltpu.make_async_copy(q_pair.at[w.chip], q_all.at[w.chip], loc.at[1])
    q_own.start()
    chunks[0].first()
    for one in q_made:
        one.wait_recv()
    q_own.wait()
    q_line = Line(w, z, q_all, zq_land, dq_o)
    q_line.first()
    hidden = Reduce(w, None, dh, dh_land, None)
    for one in smalls:
        one.wait_recv()
    own.wait()
    s_sum[...] = jnp.sum(s_land[...], axis=0)
    s_line = Line(w, z, s_sum, zs_land, small_o)
    s_line.first()
    for tick in range(1, count + 5):
        if tick < count:
            chunks[tick].first()
        if tick == count:
            hidden.first()
        if 0 <= tick - 1 < count:
            chunks[tick - 1].second()
        if tick - 1 == count:
            hidden.second()
        if 0 <= tick - 2 < count:
            chunks[tick - 2].third(part.at[tick - 2])
            lines[tick - 2].first()
        if tick - 2 == count:
            hidden.third(dh_o)
        if tick == 2:
            q_line.second()
            s_line.second()
        if 0 <= tick - 3 < count:
            lines[tick - 3].second()
        if tick == 3:
            q_line.third()
            s_line.third()
        if 0 <= tick - 4 < count:
            lines[tick - 4].third()
    for one in smalls + q_made + [q_meet]:
        one.wait_send()
    for one in chunks + [hidden]:
        one.done()
    for one in lines + [q_line, s_line]:
        one.done()


def reduce_all(gq, gb, gi, go, dh, small):
    rows, cols = go.shape[2:]
    count = gb.shape[2] // rows + gi.shape[3] // cols + 1
    q_block = (CHIPS,) + gq.shape[2:]
    tail = small.shape[1:]
    outs = [
        jax.ShapeDtypeStruct(q_block, bf16),
        jax.ShapeDtypeStruct(gb.shape[2:], bf16),
        jax.ShapeDtypeStruct(gi.shape[2:], bf16),
        jax.ShapeDtypeStruct(go.shape[2:], bf16),
        jax.ShapeDtypeStruct(dh.shape[1:], bf16),
        jax.ShapeDtypeStruct(tail, f32),
    ]
    scratch = [
        VMEM(q_block, bf16),
        VMEM(q_block, bf16),
        VMEM((count, CHIPS, rows, cols), bf16),
        VMEM((count, 6, rows // 2, cols), bf16),
        VMEM((6, dh.shape[1] // 2, dh.shape[2]), bf16),
        VMEM((count, rows, cols), bf16),
        VMEM(small.shape, f32),
        VMEM(tail, f32),
        VMEM((2,) + q_block, bf16),
        VMEM((count, 2, rows, cols), bf16),
        VMEM((2,) + tail, f32),
    ]
    wires = 8 + 4 + count * 10 + 6 + 6
    return call(
        reduce_kernel,
        (gq, gb, gi, go, dh, small),
        outs,
        scratch + dma_sems(wires) + [pltpu.SemaphoreType.DMA((2,))],
        7,
        [VMEM] * 6,
        [VMEM] * 6,
        "reduce_all",
    )


def fast_body(
    hidden,
    segment_ids,
    w_qkv,
    b_qv,
    w_out,
    b_out,
    gain1,
    shift1,
    w_in,
    b_in,
    w_back,
    b_back,
    gain2,
    shift2,
    cotangent,
):
    tok, width = hidden.shape
    hd = width // HEADS
    part = w_qkv.shape[0]
    wide = width // CHIPS
    ff = w_in.shape[1]
    core = lax.axis_index("shard") % 2
    fold = ff // width
    pad = lambda rows: jnp.pad(rows, ((0, 0), (0, 128 - rows.shape[1])))
    small = jnp.concatenate(
        [
            pad(
                jnp.concatenate(
                    [b_qv]
                    + [one.reshape(1, part) for one in (b_out, gain1, shift1, b_back, gain2, shift2)]
                    + [b_in.reshape(fold, part)],
                    axis=0,
                )
            ),
            segment_ids.astype(bf16).reshape(tok // 128, 128),
        ],
        axis=0,
    )
    small = jnp.pad(small, ((0, 16 - small.shape[0]), (0, 0)))
    wq_send = w_qkv.reshape(part, 3, CHIPS, wide).transpose(2, 0, 1, 3).reshape(CHIPS, part, 3 * wide)
    hid_all, wq_all, wo_all, wi_all, wb_all, small_all = gather_all(
        hidden, wq_send, w_out, w_in, w_back, small
    )
    wq_mine = wq_all.reshape(width, 3 * wide)
    wo_full = wo_all.reshape(width, width)
    wi_full = wi_all.reshape(width, ff)
    wb_full = wb_all.reshape(ff, width)
    vec = lambda row: small_all[:, row, :part].reshape(width).astype(f32)
    bo_full, g1_full, s1_full, bb_full, g2_full, s2_full = (vec(row) for row in range(2, 8))
    bi_full = small_all[:, 8 : 8 + fold, :part].reshape(ff).astype(f32)
    segs = small_all[:, 8 + fold : 8 + fold + tok // 128, :].astype(jnp.int32).reshape(PLANE, tok)
    chip = lax.axis_index("shard") // 2
    bias = lax.dynamic_slice_in_dim(small_all[:, 0:2, :part], 2 * chip, 2, 0)
    bias_q = bias[:, 0].reshape(wide).astype(f32)
    bias_v = bias[:, 1].reshape(wide).astype(f32)

    hid_mine = lax.dynamic_index_in_dim(
        hid_all.reshape(CHIPS, 2, tok, width), core, axis=1, keepdims=False
    ).reshape(CHIPS * tok, width)
    query = (
        (jnp.dot(hid_mine, wq_mine[:, :wide], preferred_element_type=f32) + bias_q)
        .astype(bf16)
        .reshape(CHIPS, tok, wide)
    )
    kv = jnp.dot(hid_all.reshape(PLANE * tok, width), wq_mine[:, wide:], preferred_element_type=f32)
    keys = kv[:, :wide].astype(bf16)
    values = (kv[:, wide:] + bias_v).astype(bf16)
    seg_mine = lax.dynamic_index_in_dim(segs.reshape(CHIPS, 2, tok), core, axis=1, keepdims=False)
    touch = jnp.logical_and(
        segs[None, :, 0] <= seg_mine[:, -1:], segs[None, :, -1] >= seg_mine[:, :1]
    )
    place = jnp.arange(PLANE, dtype=jnp.int32)[None]
    bound = jnp.stack(
        [
            jnp.min(jnp.where(touch, place, PLANE), axis=1),
            jnp.max(jnp.where(touch, place, -1), axis=1) + 1,
        ]
    ).astype(jnp.int32)
    segq = jnp.broadcast_to(seg_mine[:, :, None], (CHIPS, tok, 128))
    segk = segs.reshape(PLANE, 1, tok)
    ctx32, ctx_low, log_total = attend(bound, query, keys, values, segq, segk, hd)
    ctx_parts = chip_swap(ctx_low, 2, "ctx_swap")
    context = ctx_parts.transpose(1, 0, 2).reshape(tok, width)

    resid1 = hidden.astype(f32) + jnp.dot(context, wo_full, preferred_element_type=f32) + bo_full
    normed1, norm1_pull = jax.vjp(normalize, resid1, g1_full, s1_full)
    normed1_low = normed1.astype(bf16)
    pre = jnp.dot(normed1_low, wi_full, preferred_element_type=f32) + bi_full
    act, gelu_pull = jax.vjp(gelu_exact, pre)
    act_low = act.astype(bf16)
    resid2 = normed1 + jnp.dot(act_low, wb_full, preferred_element_type=f32) + bb_full
    out32, norm2_pull = jax.vjp(normalize, resid2, g2_full, s2_full)
    output = out32.astype(bf16)
    d_resid2, grad_gain2, grad_shift2 = norm2_pull(cotangent)
    d_branch2 = d_resid2.astype(bf16)
    grad_b_back = jnp.sum(d_resid2, axis=0)
    grad_w_back = jnp.einsum("tf,td->fd", act_low, d_branch2, preferred_element_type=f32)
    d_act = jnp.einsum("td,fd->tf", d_branch2, wb_full, preferred_element_type=f32)
    (d_pre,) = gelu_pull(d_act)
    grad_b_in = jnp.sum(d_pre, axis=0)
    d_pre_low = d_pre.astype(bf16)
    grad_w_in = jnp.einsum("td,tf->df", normed1_low, d_pre_low, preferred_element_type=f32)
    d_normed1 = d_resid2 + jnp.einsum("tf,df->td", d_pre_low, wi_full, preferred_element_type=f32)
    d_resid1, grad_gain1, grad_shift1 = norm1_pull(d_normed1)
    grad_b_out = jnp.sum(d_resid1, axis=0)
    d_branch1 = d_resid1.astype(bf16)
    grad_w_out = jnp.einsum("tc,td->cd", context, d_branch1, preferred_element_type=f32)
    d_context = jnp.einsum("td,cd->tc", d_branch1, wo_full, preferred_element_type=f32).astype(bf16)

    dctx_mine = chip_swap(d_context.reshape(tok, CHIPS, wide).transpose(1, 0, 2), 3, "dctx_swap")
    d_query, dk_part, dv_part = attend_back(
        bound, query, keys, values, segq, segk, ctx32, dctx_mine, log_total, hd
    )
    dkv = jnp.concatenate([dk_part, dv_part], axis=1).reshape(CHIPS, 2, tok, 2 * wide)
    dkv_other = mate_swap(dkv.astype(bf16), 4, "dkv_swap")
    dkv_mine = lax.dynamic_index_in_dim(dkv, core, axis=1, keepdims=False) + dkv_other.astype(f32)
    d_qkv = jnp.concatenate([d_query, dkv_mine], axis=2).reshape(CHIPS * tok, 3 * wide)
    bias_grads = jnp.stack([jnp.sum(d_qkv[:, :wide], axis=0), jnp.sum(d_qkv[:, 2 * wide :], axis=0)])
    d_qkv_low = d_qkv.astype(bf16)
    gq = (
        jnp.einsum("td,te->de", hid_mine, d_qkv_low, preferred_element_type=f32)
        .astype(bf16)
        .reshape(CHIPS, 2, part, 3 * wide)
    )
    dh = (
        jnp.einsum("te,de->td", d_qkv_low, wq_mine, preferred_element_type=f32)
        .astype(bf16)
        .reshape(CHIPS, tok, width)
    )
    mine = (jnp.arange(CHIPS) == chip).astype(f32)[:, None, None, None]
    bias_pack = (mine * bias_grads.reshape(1, 2, 2, part).transpose(0, 2, 1, 3)).reshape(PLANE, 2, part)
    stack = jnp.concatenate(
        [bias_pack]
        + [
            one.reshape(PLANE, 1, part)
            for one in (grad_b_out, grad_gain1, grad_shift1, grad_b_back, grad_gain2, grad_shift2)
        ]
        + [grad_b_in.reshape(PLANE, fold, part)],
        axis=1,
    )
    stack = jnp.pad(stack, ((0, 0), (0, 16 - stack.shape[1]), (0, 128 - part)))
    dq, db, di, do, dh_sum, tiny = reduce_all(
        gq,
        grad_w_back.astype(bf16).reshape(CHIPS, 2, ff // PLANE, width),
        grad_w_in.astype(bf16).reshape(CHIPS, 2, part, ff),
        grad_w_out.astype(bf16).reshape(CHIPS, 2, part, width),
        dh,
        stack,
    )
    d_hidden = d_resid1 + dh_sum.astype(f32)
    g_qkv = dq.astype(f32).reshape(CHIPS, part, 3, wide).transpose(1, 2, 0, 3).reshape(part, 3 * width)
    tiny = tiny[:, :part]
    return (
        output,
        d_hidden,
        g_qkv,
        tiny[0:2],
        do.astype(f32),
        tiny[2],
        tiny[3],
        tiny[4],
        di.astype(f32),
        tiny[8 : 8 + fold].reshape(ff // PLANE),
        db.astype(f32),
        tiny[5],
        tiny[6],
        tiny[7],
    )


def solution(mesh):
    in_specs = (
        P(("replica", "shard"), None),
        P(("replica", "shard")),
        P("shard", None),
        P(None, "shard"),
        P("shard", None),
        P("shard"),
        P("shard"),
        P("shard"),
        P("shard", None),
        P("shard"),
        P("shard", None),
        P("shard"),
        P("shard"),
        P("shard"),
        P(("replica", "shard"), None),
    )
    out_specs = (
        P(("replica", "shard"), None),
        P(("replica", "shard"), None),
        P("shard", None),
        P(None, "shard"),
        P("shard", None),
        P("shard"),
        P("shard"),
        P("shard"),
        P("shard", None),
        P("shard"),
        P("shard", None),
        P("shard"),
        P("shard"),
        P("shard"),
    )
    paired = mesh.shape["shard"] == PLANE and mesh.shape["replica"] == LINE
    body = fast_body if paired else plain_body
    return jax.shard_map(body, mesh=mesh, in_specs=in_specs, out_specs=out_specs, check_vma=False)
```

```python
import functools
import math

import jax
import jax.numpy as jnp
from jax import lax
from jax.experimental import pallas as pl
from jax.experimental.pallas import tpu as pltpu
from jax.sharding import PartitionSpec as P

HEADS = 12


scale_factor = 0.125
norm_epsilon = 1e-05
masked_value = -1e30


def normalize(resid, gain, shift):
    mean_value = jnp.mean(resid, axis=-1, keepdims=True)
    centered = resid - mean_value
    variance = jnp.mean(centered * centered, axis=-1, keepdims=True)
    return centered * lax.rsqrt(variance + norm_epsilon) * gain + shift


def gelu_exact(values):
    return jax.nn.gelu(values, approximate=False)


def keep_state(state):
    return state


def block_size(count):
    return math.gcd(count, 512)


def masked_scores(query_heads, key_heads, query_segs, key_segs):
    scores = (
        jnp.einsum("qhd,khd->hqk", query_heads, key_heads, preferred_element_type=jnp.float32)
        * scale_factor
    )
    allowed = query_segs[:, None] == key_segs[None, :]
    return (scores, allowed[None])


def grad_block(
    query_heads, dctx_heads, log_total, delta, query_segs, key_heads, value_heads, key_segs
):
    scores, allowed = masked_scores(query_heads, key_heads, query_segs, key_segs)
    probs = jnp.where(allowed, jnp.exp(scores - log_total[:, :, None]), 0.0)
    d_prob = jnp.einsum("qhd,khd->hqk", dctx_heads, value_heads, preferred_element_type=jnp.float32)
    d_scores = (probs * (d_prob - delta[:, :, None])).astype(jnp.bfloat16)
    return (probs.astype(jnp.bfloat16), d_scores)


def plain_body(
    hidden,
    segment_ids,
    w_qkv,
    b_qv,
    w_out,
    b_out,
    gain1,
    shift1,
    w_in,
    b_in,
    w_back,
    b_back,
    gain2,
    shift2,
    cotangent,
):
    tok_rows, width = hidden.shape
    heads = HEADS
    head_dim = width // heads
    seg_low = segment_ids[0]
    seg_high = segment_ids[-1]
    wq_full, wo_full, bqv_full, bo_full, g1_full, s1_full = (
        lax.all_gather(w_qkv, "shard", axis=0, tiled=True),
        lax.all_gather(w_out, "shard", axis=0, tiled=True),
        lax.all_gather(b_qv, "shard", axis=1, tiled=True),
        lax.all_gather(b_out, "shard", axis=0, tiled=True),
        lax.all_gather(gain1, "shard", axis=0, tiled=True),
        lax.all_gather(shift1, "shard", axis=0, tiled=True),
    )
    qkv = jnp.dot(hidden, wq_full, preferred_element_type=jnp.float32)
    bqv_wide = bqv_full.astype(jnp.float32)
    query = (qkv[:, :width] + bqv_wide[0]).astype(jnp.bfloat16)
    keys = qkv[:, width : 2 * width].astype(jnp.bfloat16)
    values = (qkv[:, 2 * width :] + bqv_wide[1]).astype(jnp.bfloat16)
    query_heads = query.reshape(tok_rows, heads, head_dim)
    key_local = keys.reshape(tok_rows, heads, head_dim)
    value_local = values.reshape(tok_rows, heads, head_dim)
    start_state = (
        jnp.full((heads, tok_rows), masked_value, jnp.float32),
        jnp.zeros((heads, tok_rows), jnp.float32),
        jnp.zeros((tok_rows, heads, head_dim), jnp.float32),
    )
    key_piece = lax.all_gather(keys, "shard", axis=0, tiled=True)
    value_piece = lax.all_gather(values, "shard", axis=0, tiled=True)
    seg_piece = lax.all_gather(segment_ids, "shard", axis=0, tiled=True)
    count = key_piece.shape[0]
    block = block_size(count)

    def forward_step(index, state):
        offset = index * block
        key_heads = lax.dynamic_slice_in_dim(key_piece, offset, block, 0).reshape(
            block, heads, head_dim
        )
        value_heads = lax.dynamic_slice_in_dim(value_piece, offset, block, 0).reshape(
            block, heads, head_dim
        )
        key_segs = lax.dynamic_slice_in_dim(seg_piece, offset, block, 0)

        def forward_update(state):
            running_max, running_sum, accum = state
            scores, allowed = masked_scores(query_heads, key_heads, segment_ids, key_segs)
            new_max = jnp.maximum(
                running_max, jnp.max(jnp.where(allowed, scores, masked_value), axis=-1)
            )
            factor = jnp.exp(running_max - new_max)
            weights = jnp.where(allowed, jnp.exp(scores - new_max[:, :, None]), 0.0)
            running_sum = running_sum * factor + jnp.sum(weights, axis=-1)
            accum = accum * factor.T[:, :, None] + jnp.einsum(
                "hqk,khd->qhd",
                weights.astype(jnp.bfloat16),
                value_heads,
                preferred_element_type=jnp.float32,
            )
            return (new_max, running_sum, accum)

        touches = jnp.logical_and(key_segs[0] <= seg_high, key_segs[-1] >= seg_low)
        return lax.cond(touches, forward_update, keep_state, state)

    running_max, running_sum, accum = lax.fori_loop(0, count // block, forward_step, start_state)
    context32 = accum / running_sum.T[:, :, None]
    log_total = running_max + jnp.log(running_sum)
    context = context32.reshape(tok_rows, width).astype(jnp.bfloat16)
    resid1 = (
        hidden.astype(jnp.float32)
        + jnp.dot(context, wo_full, preferred_element_type=jnp.float32)
        + bo_full.astype(jnp.float32)
    )
    normed1, norm1_pull = jax.vjp(
        normalize, resid1, g1_full.astype(jnp.float32), s1_full.astype(jnp.float32)
    )
    wi_full, bi_full, wb_full, bb_full, g2_full, s2_full = (
        lax.all_gather(w_in, "shard", axis=0, tiled=True),
        lax.all_gather(b_in, "shard", axis=0, tiled=True),
        lax.all_gather(w_back, "shard", axis=0, tiled=True),
        lax.all_gather(b_back, "shard", axis=0, tiled=True),
        lax.all_gather(gain2, "shard", axis=0, tiled=True),
        lax.all_gather(shift2, "shard", axis=0, tiled=True),
    )
    normed1_low = normed1.astype(jnp.bfloat16)
    pre = jnp.dot(normed1_low, wi_full, preferred_element_type=jnp.float32) + bi_full.astype(
        jnp.float32
    )
    act, gelu_pull = jax.vjp(gelu_exact, pre)
    act_low = act.astype(jnp.bfloat16)
    resid2 = (
        normed1
        + jnp.dot(act_low, wb_full, preferred_element_type=jnp.float32)
        + bb_full.astype(jnp.float32)
    )
    out32, norm2_pull = jax.vjp(
        normalize, resid2, g2_full.astype(jnp.float32), s2_full.astype(jnp.float32)
    )
    output = out32.astype(jnp.bfloat16)
    d_resid2, grad_gain2, grad_shift2 = norm2_pull(cotangent)
    d_branch2 = d_resid2.astype(jnp.bfloat16)
    grad_b_back = jnp.sum(d_resid2, axis=0)
    grad_w_back = jnp.einsum("tf,td->fd", act_low, d_branch2, preferred_element_type=jnp.float32)
    d_act = jnp.einsum("td,fd->tf", d_branch2, wb_full, preferred_element_type=jnp.float32)
    (d_pre,) = gelu_pull(d_act)
    grad_b_in = jnp.sum(d_pre, axis=0)
    d_pre_low = d_pre.astype(jnp.bfloat16)
    grad_w_in = jnp.einsum("td,tf->df", normed1_low, d_pre_low, preferred_element_type=jnp.float32)
    d_normed1 = d_resid2 + jnp.einsum(
        "tf,df->td", d_pre_low, wi_full, preferred_element_type=jnp.float32
    )
    d_resid1, grad_gain1, grad_shift1 = norm1_pull(d_normed1)
    grad_b_out = jnp.sum(d_resid1, axis=0)
    d_branch1 = d_resid1.astype(jnp.bfloat16)
    grad_w_out = jnp.einsum("tc,td->cd", context, d_branch1, preferred_element_type=jnp.float32)
    d_context = jnp.einsum(
        "td,cd->tc", d_branch1, wo_full, preferred_element_type=jnp.float32
    ).astype(jnp.bfloat16)
    dctx_heads = d_context.reshape(tok_rows, heads, head_dim)
    delta = jnp.einsum("qhd,qhd->hq", dctx_heads.astype(jnp.float32), context32)
    zero_heads = jnp.zeros((tok_rows, heads, head_dim), jnp.float32)
    query_key_piece = lax.all_gather(keys, "shard", axis=0, tiled=True)
    query_value_piece = lax.all_gather(values, "shard", axis=0, tiled=True)
    query_seg_piece = lax.all_gather(segment_ids, "shard", axis=0, tiled=True)
    count = query_key_piece.shape[0]
    query_block = block_size(count)

    def query_step(index, summed):
        offset = index * query_block
        key_heads = lax.dynamic_slice_in_dim(query_key_piece, offset, query_block, 0).reshape(
            query_block, heads, head_dim
        )
        value_heads = lax.dynamic_slice_in_dim(query_value_piece, offset, query_block, 0).reshape(
            query_block, heads, head_dim
        )
        key_segs = lax.dynamic_slice_in_dim(query_seg_piece, offset, query_block, 0)

        def query_update(summed):
            probs, d_scores = grad_block(
                query_heads,
                dctx_heads,
                log_total,
                delta,
                segment_ids,
                key_heads,
                value_heads,
                key_segs,
            )
            return (
                summed
                + jnp.einsum(
                    "hqk,khd->qhd", d_scores, key_heads, preferred_element_type=jnp.float32
                )
                * scale_factor
            )

        touches = jnp.logical_and(key_segs[0] <= seg_high, key_segs[-1] >= seg_low)
        return lax.cond(touches, query_update, keep_state, summed)

    d_query = lax.fori_loop(0, count // query_block, query_step, zero_heads)
    all_log_total, all_delta = (
        lax.all_gather(log_total, "shard", axis=1, tiled=True),
        lax.all_gather(delta, "shard", axis=1, tiled=True),
    )
    query_piece = lax.all_gather(query, "shard", axis=0, tiled=True)
    dctx_piece = lax.all_gather(d_context, "shard", axis=0, tiled=True)
    key_seg_piece = lax.all_gather(segment_ids, "shard", axis=0, tiled=True)
    count = query_piece.shape[0]
    key_block = block_size(count)

    def key_step(index, state):
        offset = index * key_block
        piece_query = lax.dynamic_slice_in_dim(query_piece, offset, key_block, 0).reshape(
            key_block, heads, head_dim
        )
        piece_dctx = lax.dynamic_slice_in_dim(dctx_piece, offset, key_block, 0).reshape(
            key_block, heads, head_dim
        )
        piece_segs = lax.dynamic_slice_in_dim(key_seg_piece, offset, key_block, 0)
        piece_log = lax.dynamic_slice_in_dim(all_log_total, offset, key_block, 1)
        piece_delta = lax.dynamic_slice_in_dim(all_delta, offset, key_block, 1)

        def key_update(state):
            d_key, d_value = state
            probs, d_scores = grad_block(
                piece_query,
                piece_dctx,
                piece_log,
                piece_delta,
                piece_segs,
                key_local,
                value_local,
                segment_ids,
            )
            d_key = (
                d_key
                + jnp.einsum(
                    "hqk,qhd->khd", d_scores, piece_query, preferred_element_type=jnp.float32
                )
                * scale_factor
            )
            d_value = d_value + jnp.einsum(
                "hqk,qhd->khd", probs, piece_dctx, preferred_element_type=jnp.float32
            )
            return (d_key, d_value)

        touches = jnp.logical_and(piece_segs[0] <= seg_high, piece_segs[-1] >= seg_low)
        return lax.cond(touches, key_update, keep_state, state)

    d_key_heads, d_value_heads = lax.fori_loop(
        0, count // key_block, key_step, (zero_heads, zero_heads)
    )
    d_keys = d_key_heads.reshape(tok_rows, width)
    d_values = d_value_heads.reshape(tok_rows, width)
    d_query = d_query.reshape(tok_rows, width)
    grad_b_qv = jnp.stack([jnp.sum(d_query, axis=0), jnp.sum(d_values, axis=0)], axis=0)
    d_qkv = jnp.concatenate([d_query, d_keys, d_values], axis=1).astype(jnp.bfloat16)
    grad_w_qkv = jnp.einsum("td,te->de", hidden, d_qkv, preferred_element_type=jnp.float32)
    d_hidden = d_resid1 + jnp.einsum(
        "te,de->td", d_qkv, wq_full, preferred_element_type=jnp.float32
    )
    local_grads = (
        grad_w_qkv,
        grad_b_qv,
        grad_w_out,
        grad_b_out,
        grad_gain1,
        grad_shift1,
        grad_w_in,
        grad_b_in,
        grad_w_back,
        grad_b_back,
        grad_gain2,
        grad_shift2,
    )
    shard_grads = (
        lax.psum_scatter(
            local_grads[0].astype(jnp.bfloat16), "shard", scatter_dimension=0, tiled=True
        ).astype(jnp.float32),
        lax.psum_scatter(
            local_grads[1].astype(jnp.bfloat16), "shard", scatter_dimension=1, tiled=True
        ).astype(jnp.float32),
        lax.psum_scatter(
            local_grads[2].astype(jnp.bfloat16), "shard", scatter_dimension=0, tiled=True
        ).astype(jnp.float32),
        lax.psum_scatter(
            local_grads[3].astype(jnp.bfloat16), "shard", scatter_dimension=0, tiled=True
        ).astype(jnp.float32),
        lax.psum_scatter(
            local_grads[4].astype(jnp.bfloat16), "shard", scatter_dimension=0, tiled=True
        ).astype(jnp.float32),
        lax.psum_scatter(
            local_grads[5].astype(jnp.bfloat16), "shard", scatter_dimension=0, tiled=True
        ).astype(jnp.float32),
        lax.psum_scatter(
            local_grads[6].astype(jnp.bfloat16), "shard", scatter_dimension=0, tiled=True
        ).astype(jnp.float32),
        lax.psum_scatter(
            local_grads[7].astype(jnp.bfloat16), "shard", scatter_dimension=0, tiled=True
        ).astype(jnp.float32),
        lax.psum_scatter(
            local_grads[8].astype(jnp.bfloat16), "shard", scatter_dimension=0, tiled=True
        ).astype(jnp.float32),
        lax.psum_scatter(
            local_grads[9].astype(jnp.bfloat16), "shard", scatter_dimension=0, tiled=True
        ).astype(jnp.float32),
        lax.psum_scatter(
            local_grads[10].astype(jnp.bfloat16), "shard", scatter_dimension=0, tiled=True
        ).astype(jnp.float32),
        lax.psum_scatter(
            local_grads[11].astype(jnp.bfloat16), "shard", scatter_dimension=0, tiled=True
        ).astype(jnp.float32),
    )
    total_grads = (
        lax.psum(shard_grads[0].astype(jnp.bfloat16), "replica").astype(jnp.float32),
        lax.psum(shard_grads[1].astype(jnp.bfloat16), "replica").astype(jnp.float32),
        lax.psum(shard_grads[2].astype(jnp.bfloat16), "replica").astype(jnp.float32),
        lax.psum(shard_grads[3].astype(jnp.bfloat16), "replica").astype(jnp.float32),
        lax.psum(shard_grads[4].astype(jnp.bfloat16), "replica").astype(jnp.float32),
        lax.psum(shard_grads[5].astype(jnp.bfloat16), "replica").astype(jnp.float32),
        lax.psum(shard_grads[6].astype(jnp.bfloat16), "replica").astype(jnp.float32),
        lax.psum(shard_grads[7].astype(jnp.bfloat16), "replica").astype(jnp.float32),
        lax.psum(shard_grads[8].astype(jnp.bfloat16), "replica").astype(jnp.float32),
        lax.psum(shard_grads[9].astype(jnp.bfloat16), "replica").astype(jnp.float32),
        lax.psum(shard_grads[10].astype(jnp.bfloat16), "replica").astype(jnp.float32),
        lax.psum(shard_grads[11].astype(jnp.bfloat16), "replica").astype(jnp.float32),
    )
    return (output, d_hidden) + tuple(total_grads)


PLANE = 8
LINE = 4
CHIPS = 4
MESH = pl.DeviceIdType.MESH
VMEM = pltpu.VMEM
ANY = pl.ANY
f32 = jnp.float32
bf16 = jnp.bfloat16


class Wires:
    def __init__(self, send, recv):
        self.send, self.recv, self.used = send, recv, 0
        me = lax.axis_index("shard")
        self.me = me
        self.core = me % 2
        self.chip = me // 2
        self.mate = me + 1 - 2 * self.core
        self.xn = me + 2 - 4 * (self.chip % 2)
        self.yn = me + 4 - 8 * (me // 4)
        self.dn = self.xn + 4 - 8 * (me // 4)
        self.cx = self.xn // 2
        self.cy = self.yn // 2
        self.cd = self.dn // 2

    def copy(self, src, dst, where):
        slot = self.used
        self.used += 1
        return pltpu.make_async_remote_copy(
            src_ref=src,
            dst_ref=dst,
            send_sem=self.send.at[slot],
            recv_sem=self.recv.at[slot],
            device_id=where if isinstance(where, dict) else {"shard": where},
            device_id_type=MESH,
        )

    def start(self, src, dst, where):
        made = self.copy(src, dst, where)
        made.start()
        return made


def greet(others):
    barrier = pltpu.get_barrier_semaphore()
    for other in others:
        pl.semaphore_signal(barrier, inc=1, device_id=other, device_id_type=MESH)
    pl.semaphore_wait(barrier, len(others))


def plane_others(me):
    return [{"shard": (me + step) % PLANE} for step in range(1, PLANE)]


def call(kernel, ins, outs, scratch, ident, in_spaces, out_spaces, name):
    return pl.pallas_call(
        kernel,
        out_shape=outs,
        in_specs=[pl.BlockSpec(memory_space=space) for space in in_spaces],
        out_specs=[pl.BlockSpec(memory_space=space) for space in out_spaces],
        scratch_shapes=scratch,
        compiler_params=pltpu.CompilerParams(
            collective_id=ident, has_side_effects=True, vmem_limit_bytes=60 << 20
        ),
        name=name,
    )(*ins)


def dma_sems(count):
    return [pltpu.SemaphoreType.DMA((count,)), pltpu.SemaphoreType.DMA((count,))]


class Gather:
    def __init__(self, wires, block, out, local_sem):
        w = self.w = wires
        self.out = out
        self.half = block.shape[0] // 2
        me = w.me
        self.own = pltpu.make_async_copy(block, out.at[me], local_sem)
        self.own.start()
        self.to_x = w.start(block, out.at[me], w.xn)
        self.to_y = w.start(block, out.at[me], w.yn)
        self.to_mate = w.start(block, out.at[me], w.mate)

    def relay(self):
        w, out, half = self.w, self.out, self.half
        low, high = pl.ds(0, half), pl.ds(half, half)
        self.to_x.wait_recv()
        self.x_on = w.start(out.at[w.xn, low], out.at[w.xn, low], w.yn)
        self.x_mate = w.start(out.at[w.xn], out.at[w.xn], w.mate)
        self.to_y.wait_recv()
        self.y_on = w.start(out.at[w.yn, high], out.at[w.yn, high], w.xn)
        self.y_mate = w.start(out.at[w.yn], out.at[w.yn], w.mate)

    def finish(self):
        w, out, half = self.w, self.out, self.half
        low, high = pl.ds(0, half), pl.ds(half, half)
        self.x_on.wait_recv()
        self.d_low = w.start(out.at[w.dn, low], out.at[w.dn, low], w.mate)
        self.y_on.wait_recv()
        self.d_high = w.start(out.at[w.dn, high], out.at[w.dn, high], w.mate)

    def done(self):
        for made in (self.to_mate, self.x_mate, self.y_mate, self.d_low, self.d_high):
            made.wait_recv()
        for made in (
            self.to_x,
            self.to_y,
            self.to_mate,
            self.x_on,
            self.x_mate,
            self.y_on,
            self.y_mate,
            self.d_low,
            self.d_high,
        ):
            made.wait_send()
        self.own.wait()


ROWS = 256


def dot(left, right, left_dim, right_dim):
    return lax.dot_general(
        left, right, (((left_dim,), (right_dim,)), ((), ())), preferred_element_type=f32
    )


def turn(block):
    return block.astype(f32).T


def whole_attend(query, k_ref, vt_ref, segk_ref, segq, hd):
    heads = k_ref.shape[0]
    rows = query.shape[1]
    segk = segk_ref[...]
    allowed = jnp.concatenate([segk] * (rows // 128), axis=1) == segq
    scores = [
        jnp.where(allowed, dot(k_ref[head], query[head * hd : (head + 1) * hd], 1, 0), masked_value)
        for head in range(heads)
    ]
    context, logs = [], []
    for head in range(heads):
        top = jnp.max(scores[head], axis=0, keepdims=True)
        weights = jnp.exp(scores[head] - top)
        total = jnp.sum(weights, axis=0, keepdims=True)
        acc = dot(vt_ref[head * hd : (head + 1) * hd, :], weights.astype(bf16), 1, 0)
        context.append(acc / total)
        logs.append(top + jnp.log(total))
    return jnp.concatenate(context, axis=0), jnp.concatenate(logs, axis=0)


def forward_kernel(
    hid,
    wq,
    small,
    wo,
    wi,
    wb,
    wo_o,
    wi_o,
    wb_o,
    small_o,
    wq_o,
    hidt_o,
    qt_o,
    k_o,
    v_o,
    kt_o,
    segk_o,
    segq_o,
    ctx32_o,
    log_o,
    ctx_o,
    hid_s,
    vt_s,
    ctx_s,
    send,
    recv,
    loc,
    *,
    hd,
    seg_row,
):
    w = Wires(send, recv)
    greet(plane_others(w.me))
    me, core = w.me, w.core
    tok, width = hid.shape
    wide = width // CHIPS
    own_small = pltpu.make_async_copy(small, small_o.at[me], loc.at[0])
    own_small.start()
    first = Gather(w, hid, hid_s, loc.at[1])
    own_q = pltpu.make_async_copy(wq.at[w.chip], wq_o.at[me], loc.at[2])
    own_q.start()
    q_mate = w.start(wq.at[w.chip], wq_o.at[me], w.mate)
    q_x = w.start(wq.at[w.cx], wq_o.at[me], w.xn)
    q_y = w.start(wq.at[w.cy], wq_o.at[me], w.yn)
    q_d = w.start(wq.at[w.cd], wq_o.at[me], w.dn)
    smalls = [w.start(small, small_o.at[me], (me + step) % PLANE) for step in range(1, PLANE)]
    first.relay()
    q_on = []
    for came, source in ((q_x, w.xn), (q_y, w.yn), (q_d, w.dn)):
        came.wait_recv()
        q_on.append(w.start(wq_o.at[source], wq_o.at[source], w.mate))
    rest = [
        Gather(w, block, out, loc.at[3 + slot])
        for slot, (block, out) in enumerate(((wo, wo_o), (wi, wi_o), (wb, wb_o)))
    ]
    for made in smalls:
        made.wait_recv()
    own_small.wait()
    for source in range(PLANE):
        ids = small_o[source].astype(f32)[seg_row : seg_row + tok // 128]
        segq_o[source] = jnp.concatenate([ids[part : part + 1] for part in range(tok // 128)], axis=1)
        for part in range(tok // 128):
            at = source * tok + part * 128
            segk_o[at : at + 128, :] = jnp.broadcast_to(ids[part : part + 1], (128, 128)).T
    first.finish()
    own_q.wait()
    for made in [q_mate] + q_on:
        made.wait_recv()
    first.done()

    names = [small_o[2 * w.chip + part].astype(f32).T for part in range(2)]
    span = wide // 2
    bias_q = jnp.concatenate([one[:span, 0:1] for one in names], axis=0)
    bias_v = jnp.concatenate([one[:span, 1:2] for one in names], axis=0)

    def project(index, carry):
        for mine in (True, False):
            source = 2 * index + (core if mine else 1 - core)
            block = hid_s[source]
            weight = wq_o[...].reshape(width, 3 * wide)
            rows = pl.ds(pl.multiple_of(source * tok, tok), tok)
            kv = dot(block, weight if mine else weight[:, : 2 * wide], 1, 0)
            kvt = kv.T
            low_v = (kvt[wide : 2 * wide] + bias_v).astype(bf16)
            kt_o[:, rows] = kvt[:wide].astype(bf16)
            vt_s[:, rows] = low_v
            back = turn(low_v).astype(bf16)
            for head in range(wide // hd):
                cols = slice(head * hd, (head + 1) * hd)
                k_o[head, rows, :] = kv[:, cols].astype(bf16)
                v_o[head, rows, :] = back[:, cols]
            if mine:
                query = kvt[2 * wide :] + bias_q
                qt_o[index] = (query.astype(bf16).astype(f32) * scale_factor).astype(bf16)
                hidt_o[index] = turn(block).astype(bf16)
        return carry

    lax.fori_loop(0, CHIPS, project, 0)
    rest[0].relay()

    def one_block(turn_no, carry):
        index = (
            (turn_no == 0) * w.cd + (turn_no == 1) * w.cx + (turn_no == 2) * w.cy + (turn_no == 3) * w.chip
        )
        context, logs = whole_attend(
            qt_o[index], k_o, vt_s, segk_o, segq_o[2 * index + core], hd
        )
        ctx32_o[index] = context
        ctx_s[index] = context.astype(bf16)
        log_o[index] = logs
        return carry

    lax.fori_loop(0, 2, one_block, 0)
    c_d = w.start(ctx_s.at[w.cd], ctx_o.at[w.chip], w.dn)
    c_x = w.start(ctx_s.at[w.cx], ctx_o.at[w.chip], w.xn)
    rest[1].relay()
    rest[0].finish()
    lax.fori_loop(2, 4, one_block, 0)
    c_y = w.start(ctx_s.at[w.cy], ctx_o.at[w.chip], w.yn)
    ctx_o[w.chip] = ctx_s[w.chip]
    rest[2].relay()
    rest[1].finish()
    rest[2].finish()
    for one in rest:
        one.done()
    for made in (c_d, c_x, c_y):
        made.wait()
    for made in [q_mate, q_x, q_y, q_d] + q_on + smalls:
        made.wait_send()


def forward_all(hid, wq, small, wo, wi, wb, hd, seg_row):
    tok, width = hid.shape
    wide = width // CHIPS
    seq = PLANE * tok
    shape = jax.ShapeDtypeStruct
    outs = [
        shape((PLANE,) + wo.shape, bf16),
        shape((PLANE,) + wi.shape, bf16),
        shape((PLANE,) + wb.shape, bf16),
        shape((PLANE,) + small.shape, bf16),
        shape((PLANE,) + wq.shape[1:], bf16),
        shape((CHIPS, width, tok), bf16),
        shape((CHIPS, wide, tok), bf16),
        shape((wide // hd, seq, hd), bf16),
        shape((wide // hd, seq, hd), bf16),
        shape((wide, seq), bf16),
        shape((seq, 128), f32),
        shape((PLANE, 1, tok), f32),
        shape((CHIPS, wide, tok), f32),
        shape((CHIPS, wide // hd, tok), f32),
        shape((CHIPS, wide, tok), bf16),
    ]
    scratch = [
        VMEM((PLANE, tok, width), bf16),
        VMEM((wide, seq), bf16),
        VMEM((CHIPS, wide, tok), bf16),
    ]
    return call(
        functools.partial(forward_kernel, hd=hd, seg_row=seg_row),
        (hid, wq, small, wo, wi, wb),
        outs,
        scratch + dma_sems(56) + [pltpu.SemaphoreType.DMA((8,))],
        1,
        [VMEM] * 6,
        [ANY] * 3 + [VMEM] * 12,
        "forward_all",
    )


def add_into(dst, other, out=None):
    out = dst if out is None else out
    lead = dst.shape[0] if len(dst.shape) == 3 else 0
    rows = dst.shape[-2]

    def go(index, carry):
        if lead:
            at = (index // (rows // 16), pl.ds(pl.multiple_of((index % (rows // 16)) * 16, 16), 16))
        else:
            at = (pl.ds(pl.multiple_of(index * 16, 16), 16),)
        out[at] = (dst[at].astype(f32) + other[at].astype(f32)).astype(out.dtype)
        return carry

    lax.fori_loop(0, max(lead, 1) * (rows // 16), go, 0)


class Reduce:
    def __init__(self, wires, full, pair, land, pick):
        self.w, self.full, self.pair, self.land = wires, full, pair, land
        self.half = pair.shape[1] // 2
        self.pick = pick
        if full is not None:
            self.meet = wires.start(pick(full, 1 - wires.core), pair, wires.mate)

    def first(self):
        w, pair, land = self.w, self.pair, self.land
        low, high = pl.ds(0, self.half), pl.ds(self.half, self.half)
        if self.full is not None:
            self.meet.wait_recv()
            add_into(pair, self.pick(self.full, w.core))
        self.x0 = w.start(pair.at[w.cd, low], land.at[1], w.xn)
        self.y0 = w.start(pair.at[w.cd, high], land.at[3], w.yn)
        self.x1 = w.start(pair.at[w.cx, low], land.at[0], w.xn)
        self.y1 = w.start(pair.at[w.cy, high], land.at[2], w.yn)

    def second(self):
        w, pair, land = self.w, self.pair, self.land
        low, high = pl.ds(0, self.half), pl.ds(self.half, self.half)
        self.x0.wait_recv()
        add_into(pair.at[w.cy, low], land.at[1])
        self.y2 = w.start(pair.at[w.cy, low], land.at[4], w.yn)
        self.y0.wait_recv()
        add_into(pair.at[w.cx, high], land.at[3])
        self.x2 = w.start(pair.at[w.cx, high], land.at[5], w.xn)
        self.x1.wait_recv()
        add_into(pair.at[w.chip, low], land.at[0])
        self.y1.wait_recv()
        add_into(pair.at[w.chip, high], land.at[2])

    def third(self, out):
        w, pair, land = self.w, self.pair, self.land
        low, high = pl.ds(0, self.half), pl.ds(self.half, self.half)
        self.y2.wait_recv()
        add_into(pair.at[w.chip, low], land.at[4], out.at[low])
        self.x2.wait_recv()
        add_into(pair.at[w.chip, high], land.at[5], out.at[high])

    def done(self):
        made = [self.x0, self.x1, self.y0, self.y1, self.x2, self.y2]
        if self.full is not None:
            made.append(self.meet)
        for one in made:
            one.wait_send()


class Line:
    def __init__(self, wires, z, block, land, out):
        self.w, self.z, self.block, self.land, self.out = wires, z, block, land, out
        self.edge = (z == 0) | (z == LINE - 1)
        self.inner = {"replica": 1 + z // 2}
        self.outer = {"replica": 3 * (z // 2)}
        self.across = {"replica": 2 - z // 2}
        self.up = wires.copy(block, land.at[0], self.inner)
        self.over = wires.copy(block, land.at[1], {"replica": 3 - z})
        self.back = wires.copy(out, out, self.outer)

    def first(self):
        @pl.when(self.edge)
        def _():
            self.up.start()

    def second(self):
        @pl.when(jnp.logical_not(self.edge))
        def _():
            self.up.wait_recv()
            add_into(self.block, self.land.at[0])
            self.over.start()

    def third(self):
        @pl.when(jnp.logical_not(self.edge))
        def _():
            self.over.wait_recv()
            add_into(self.block, self.land.at[1], self.out)
            self.back.start()

    def done(self):
        @pl.when(self.edge)
        def _():
            self.up.wait_send()
            self.back.wait_recv()

        @pl.when(jnp.logical_not(self.edge))
        def _():
            self.over.wait_send()
            self.back.wait_send()


def back_unit(qt, dt, log, delta, k_ref, v_ref, kt_ref, segk_ref, segq, dk_ref, dv_ref, start, stop, hd):
    heads = k_ref.shape[0]
    rows = qt.shape[1]

    def step(index, state):
        at = pl.ds(pl.multiple_of(index * SPAN, SPAN), SPAN)
        segk = segk_ref[at, :]
        allowed = jnp.concatenate([segk] * (rows // 128), axis=1) == segq
        low = []
        for head in range(heads):
            part = slice(head * hd, (head + 1) * hd)
            scores = dot(k_ref[head, at, :], qt[part], 1, 0)
            d_prob = dot(v_ref[head, at, :], dt[part], 1, 0)
            probs = jnp.where(allowed, jnp.exp(scores - log[head : head + 1]), 0.0)
            low.append((probs.astype(bf16), (probs * (d_prob - delta[head])).astype(bf16)))
        made = []
        for head in range(heads):
            part = slice(head * hd, (head + 1) * hd)
            probs, d_scores = low[head]
            dv_ref[head, at, :] += dot(probs, dt[part], 1, 1)
            dk_ref[head, at, :] += dot(d_scores, qt[part], 1, 1)
            made.append(state[head] + dot(kt_ref[part, at], d_scores, 1, 0))
        return tuple(made)

    zero = tuple(jnp.zeros((hd, rows), f32) for _ in range(heads))
    return jnp.concatenate(lax.fori_loop(start, stop, step, zero), axis=0)


SPAN = 512


def backward_kernel(
    gb,
    gi,
    go,
    dctx,
    qt,
    k,
    v,
    kt,
    segk,
    segq,
    ctx32,
    log,
    hidt,
    wq,
    small,
    dq_o,
    db_o,
    di_o,
    do_o,
    dh_o,
    small_o,
    dctx_s,
    dq_s,
    dk_s,
    dv_s,
    dkv_s,
    dkv_land,
    dqkv_s,
    gq_s,
    dh_s,
    tiny_s,
    q_pair,
    q_all,
    pair,
    land,
    dh_land,
    part,
    s_land,
    s_sum,
    zq_land,
    z_land,
    zs_land,
    send,
    recv,
    loc,
    *,
    hd,
):
    w = Wires(send, recv)
    z = lax.axis_index("replica")
    me, core = w.me, w.core
    barrier = pltpu.get_barrier_semaphore()
    for other in plane_others(me):
        pl.semaphore_signal(barrier, inc=1, device_id=other, device_id_type=MESH)
    edge = (z == 0) | (z == LINE - 1)

    @pl.when(edge)
    def _():
        pl.semaphore_signal(barrier, inc=1, device_id={"replica": 1 + z // 2}, device_id_type=MESH)
        pl.semaphore_wait(barrier, PLANE)

    @pl.when(jnp.logical_not(edge))
    def _():
        pl.semaphore_signal(barrier, inc=1, device_id={"replica": 3 * (z // 2)}, device_id_type=MESH)
        pl.semaphore_signal(barrier, inc=1, device_id={"replica": 3 - z}, device_id_type=MESH)
        pl.semaphore_wait(barrier, PLANE + 1)

    wide, tok = dctx.shape[1:]
    heads = wide // hd
    width = wq.shape[0] * wq.shape[1]
    rows, cols = go.shape[2], go.shape[3]
    dctx_made = [
        w.start(dctx.at[chip], dctx_s.at[w.chip], who)
        for chip, who in ((w.cx, w.xn), (w.cy, w.yn), (w.cd, w.dn))
    ]
    picks = []
    for slot in range(gb.shape[2] // rows):
        at = pl.ds(slot * rows, rows)
        picks.append((gb, lambda ref, core, at=at: ref.at[:, core, at], db_o.at[at]))
    for slot in range(gi.shape[3] // cols):
        at = pl.ds(slot * cols, cols)
        picks.append((gi, lambda ref, core, at=at: ref.at[:, core, :, at], di_o.at[:, at]))
    picks.append((go, lambda ref, core: ref.at[:, core], do_o))
    count = len(picks)
    chunks = [
        Reduce(w, full, pair.at[slot], land.at[slot], pick)
        for slot, (full, pick, _) in enumerate(picks)
    ]
    lines = [
        Line(w, z, part.at[slot], z_land.at[slot], out) for slot, (_, _, out) in enumerate(picks)
    ]

    def tick(now):
        if now < count:
            chunks[now].first()
        if 0 <= now - 1 < count:
            chunks[now - 1].second()
        if 0 <= now - 2 < count:
            chunks[now - 2].third(part.at[now - 2])
            lines[now - 2].first()
        if 0 <= now - 3 < count:
            lines[now - 3].second()
        if 0 <= now - 4 < count:
            lines[now - 4].third()

    dctx_s[w.chip] = dctx[w.chip]
    dk_s[...] = jnp.zeros_like(dk_s)
    dv_s[...] = jnp.zeros_like(dv_s)
    dq_s[...] = jnp.zeros_like(dq_s)
    ticks = 0
    tick(ticks)
    ticks += 1
    steps = PLANE * tok // SPAN
    for turn_no, index in enumerate((w.chip, w.cx, w.cy, w.cd)):
        if turn_no:
            dctx_made[turn_no - 1].wait_recv()
        for half in range(2):
            dt = dctx_s[index]
            product = dt.astype(f32) * ctx32[index]
            delta = [
                jnp.sum(product[head * hd : (head + 1) * hd], axis=0, keepdims=True)
                for head in range(heads)
            ]
            dq_s[index] += back_unit(
                qt[index],
                dt,
                log[index],
                delta,
                k,
                v,
                kt,
                segk,
                segq[2 * index + core],
                dk_s,
                dv_s,
                half * steps // 2,
                (half + 1) * steps // 2,
                hd,
            )
            tick(ticks)
            ticks += 1

    def gather_rows(source):
        at = pl.ds(pl.multiple_of(source * tok, tok), tok)
        return jnp.concatenate(
            [dk_s[head, at, :] for head in range(heads)] + [dv_s[head, at, :] for head in range(heads)],
            axis=1,
        )

    def away(index, carry):
        dkv_s[index] = gather_rows(2 * index + 1 - core).astype(bf16)
        return carry

    lax.fori_loop(0, CHIPS, away, 0)
    meet = w.start(dkv_s, dkv_land, w.mate)
    tick(ticks)
    ticks += 1
    meet.wait_recv()

    def join(index, sums):
        dkv = gather_rows(2 * index + core) + dkv_land[index].astype(f32)
        dq = (dq_s[index] * scale_factor).T
        dqkv = jnp.concatenate([dkv, dq], axis=1)
        low = dqkv.astype(bf16)
        dqkv_s[index] = low
        dh_s[index] = dot(low, wq[...].reshape(width, 3 * wide), 1, 1).astype(bf16)
        return sums + jnp.sum(dqkv, axis=0, keepdims=True)

    sums = lax.fori_loop(0, CHIPS, join, jnp.zeros((1, 3 * wide), f32))
    span = wide // 2
    tiny_s[...] = small[...]
    for side in range(2):
        slot = 2 * w.chip + side
        tiny_s[slot, 0:1, :span] = sums[:, 2 * wide + side * span : 2 * wide + (side + 1) * span]
        tiny_s[slot, 1:2, :span] = sums[:, wide + side * span : wide + (side + 1) * span]
    for half in range(2):
        at = slice(half * width // 2, (half + 1) * width // 2)
        total = sum(dot(hidt[index, at, :], dqkv_s[index], 1, 0) for index in range(CHIPS))
        gq_s[2 * half : 2 * half + 2] = total.astype(bf16).reshape(2, 2, width // PLANE, 3 * wide)
    q_meet = w.start(gq_s.at[:, 1 - core], q_pair, w.mate)
    smalls = [
        w.start(tiny_s.at[(me + step) % PLANE], s_land.at[me], (me + step) % PLANE)
        for step in range(1, PLANE)
    ]
    s_land[me] = tiny_s[me]
    hidden = Reduce(w, None, dh_s, dh_land, None)
    tick(ticks)
    ticks += 1
    q_meet.wait_recv()
    add_into(q_pair, gq_s.at[:, core])
    q_made = [
        w.start(q_pair.at[chip], q_all.at[w.chip], who)
        for chip, who in ((w.cd, w.dn), (w.cx, w.xn), (w.cy, w.yn))
    ]
    hidden.first()
    q_all[w.chip] = q_pair[w.chip]
    tick(ticks)
    ticks += 1
    for one in smalls:
        one.wait_recv()
    s_sum[...] = jnp.sum(s_land[...], axis=0)
    s_line = Line(w, z, s_sum, zs_land, small_o)
    s_line.first()
    for one in q_made:
        one.wait_recv()
    q_line = Line(w, z, q_all, zq_land, dq_o)
    q_line.first()
    hidden.second()
    s_line.second()
    q_line.second()
    while ticks < count + 4:
        tick(ticks)
        ticks += 1
    s_line.third()
    q_line.third()
    hidden.third(dh_o)
    for one in smalls + q_made + [q_meet, meet] + dctx_made:
        one.wait_send()
    for one in chunks + [hidden]:
        one.done()
    for one in lines + [q_line, s_line]:
        one.done()


def backward_all(gb, gi, go, dctx, qt, k, v, kt, segk, segq, ctx32, log, hidt, wq, small, hd):
    rows, cols = go.shape[2:]
    wide, tok = dctx.shape[1:]
    width = hidt.shape[1]
    count = gb.shape[2] // rows + gi.shape[3] // cols + 1
    q_block = (CHIPS, wq.shape[1], wq.shape[2])
    tail = small.shape[1:]
    shape = jax.ShapeDtypeStruct
    outs = [
        shape(q_block, bf16),
        shape(gb.shape[2:], bf16),
        shape(gi.shape[2:], bf16),
        shape(go.shape[2:], bf16),
        shape((tok, width), bf16),
        shape(tail, f32),
    ]
    scratch = [
        VMEM(dctx.shape, bf16),
        VMEM(dctx.shape, f32),
        VMEM(k.shape, f32),
        VMEM(k.shape, f32),
        VMEM((CHIPS, tok, 2 * wide), bf16),
        VMEM((CHIPS, tok, 2 * wide), bf16),
        VMEM((CHIPS, tok, 3 * wide), bf16),
        VMEM((CHIPS, 2) + wq.shape[1:], bf16),
        VMEM((CHIPS, tok, width), bf16),
        VMEM(small.shape, f32),
        VMEM(q_block, bf16),
        VMEM(q_block, bf16),
        VMEM((count, CHIPS, rows, cols), bf16),
        VMEM((count, 6, rows // 2, cols), bf16),
        VMEM((6, tok // 2, width), bf16),
        VMEM((count, rows, cols), bf16),
        VMEM(small.shape, f32),
        VMEM(tail, f32),
        VMEM((2,) + q_block, bf16),
        VMEM((count, 2, rows, cols), bf16),
        VMEM((2,) + tail, f32),
    ]
    return call(
        functools.partial(backward_kernel, hd=hd),
        (gb, gi, go, dctx, qt, k, v, kt, segk, segq, ctx32, log, hidt, wq, small),
        outs,
        scratch + dma_sems(count * 10 + 32) + [pltpu.SemaphoreType.DMA((2,))],
        2,
        [VMEM] * 15,
        [VMEM] * 6,
        "backward_all",
    )


def fast_body(
    hidden,
    segment_ids,
    w_qkv,
    b_qv,
    w_out,
    b_out,
    gain1,
    shift1,
    w_in,
    b_in,
    w_back,
    b_back,
    gain2,
    shift2,
    cotangent,
):
    tok, width = hidden.shape
    hd = width // HEADS
    part = w_qkv.shape[0]
    wide = width // CHIPS
    ff = w_in.shape[1]
    fold = ff // width
    pad = lambda rows: jnp.pad(rows, ((0, 0), (0, 128 - rows.shape[1])))
    small = jnp.concatenate(
        [
            pad(
                jnp.concatenate(
                    [b_qv]
                    + [one.reshape(1, part) for one in (b_out, gain1, shift1, b_back, gain2, shift2)]
                    + [b_in.reshape(fold, part)],
                    axis=0,
                )
            ),
            segment_ids.astype(bf16).reshape(tok // 128, 128),
        ],
        axis=0,
    )
    small = jnp.pad(small, ((0, 16 - small.shape[0]), (0, 0)))
    seg_row = 8 + fold
    wq_send = (
        w_qkv.reshape(part, 3, CHIPS, wide)[:, (1, 2, 0)]
        .transpose(2, 0, 1, 3)
        .reshape(CHIPS, part, 3 * wide)
    )
    (
        wo_all,
        wi_all,
        wb_all,
        small_all,
        wq_all,
        hidt,
        qt,
        k,
        v,
        kt,
        segk,
        segq,
        ctx32,
        log_total,
        ctx_parts,
    ) = forward_all(hidden, wq_send, small, w_out, w_in, w_back, hd, seg_row)
    wo_full = wo_all.reshape(width, width)
    wi_full = wi_all.reshape(width, ff)
    wb_full = wb_all.reshape(ff, width)
    vec = lambda row: small_all[:, row, :part].reshape(width).astype(f32)
    bo_full, g1_full, s1_full, bb_full, g2_full, s2_full = (vec(row) for row in range(2, 8))
    bi_full = small_all[:, 8 : 8 + fold, :part].reshape(ff).astype(f32)
    context = ctx_parts.reshape(width, tok)

    resid1 = hidden.astype(f32) + jnp.einsum("ct,cd->td", context, wo_full, preferred_element_type=f32) + bo_full
    normed1, norm1_pull = jax.vjp(normalize, resid1, g1_full, s1_full)
    normed1_low = normed1.astype(bf16)
    pre = jnp.dot(normed1_low, wi_full, preferred_element_type=f32) + bi_full
    act, gelu_pull = jax.vjp(gelu_exact, pre)
    act_low = act.astype(bf16)
    resid2 = normed1 + jnp.dot(act_low, wb_full, preferred_element_type=f32) + bb_full
    out32, norm2_pull = jax.vjp(normalize, resid2, g2_full, s2_full)
    output = out32.astype(bf16)
    d_resid2, grad_gain2, grad_shift2 = norm2_pull(cotangent)
    d_branch2 = d_resid2.astype(bf16)
    grad_b_back = jnp.sum(d_resid2, axis=0)
    grad_w_back = jnp.einsum("tf,td->fd", act_low, d_branch2, preferred_element_type=f32)
    d_act = jnp.einsum("td,fd->tf", d_branch2, wb_full, preferred_element_type=f32)
    (d_pre,) = gelu_pull(d_act)
    grad_b_in = jnp.sum(d_pre, axis=0)
    d_pre_low = d_pre.astype(bf16)
    grad_w_in = jnp.einsum("td,tf->df", normed1_low, d_pre_low, preferred_element_type=f32)
    d_normed1 = d_resid2 + jnp.einsum("tf,df->td", d_pre_low, wi_full, preferred_element_type=f32)
    d_resid1, grad_gain1, grad_shift1 = norm1_pull(d_normed1)
    grad_b_out = jnp.sum(d_resid1, axis=0)
    d_branch1 = d_resid1.astype(bf16)
    grad_w_out = jnp.einsum("ct,td->cd", context, d_branch1, preferred_element_type=f32)
    d_context = jnp.einsum("cd,td->ct", wo_full, d_branch1, preferred_element_type=f32).astype(bf16)

    stack = jnp.concatenate(
        [jnp.zeros((PLANE, 2, part), f32)]
        + [
            one.reshape(PLANE, 1, part)
            for one in (grad_b_out, grad_gain1, grad_shift1, grad_b_back, grad_gain2, grad_shift2)
        ]
        + [grad_b_in.reshape(PLANE, fold, part)],
        axis=1,
    )
    stack = jnp.pad(stack, ((0, 0), (0, 16 - stack.shape[1]), (0, 128 - part)))
    dq, db, di, do, dh_sum, tiny = backward_all(
        grad_w_back.astype(bf16).reshape(CHIPS, 2, ff // PLANE, width),
        grad_w_in.astype(bf16).reshape(CHIPS, 2, part, ff),
        grad_w_out.astype(bf16).reshape(CHIPS, 2, part, width),
        d_context.reshape(CHIPS, wide, tok),
        qt,
        k,
        v,
        kt,
        segk,
        segq,
        ctx32,
        log_total,
        hidt,
        wq_all,
        stack,
        hd,
    )
    d_hidden = d_resid1 + dh_sum.astype(f32)
    g_qkv = dq.astype(f32).reshape(CHIPS, part, 3, wide)[:, :, (2, 0, 1)].transpose(1, 2, 0, 3).reshape(part, 3 * width)
    tiny = tiny[:, :part]
    return (
        output,
        d_hidden,
        g_qkv,
        tiny[0:2],
        do.astype(f32),
        tiny[2],
        tiny[3],
        tiny[4],
        di.astype(f32),
        tiny[8 : 8 + fold].reshape(ff // PLANE),
        db.astype(f32),
        tiny[5],
        tiny[6],
        tiny[7],
    )


def solution(mesh):
    in_specs = (
        P(("replica", "shard"), None),
        P(("replica", "shard")),
        P("shard", None),
        P(None, "shard"),
        P("shard", None),
        P("shard"),
        P("shard"),
        P("shard"),
        P("shard", None),
        P("shard"),
        P("shard", None),
        P("shard"),
        P("shard"),
        P("shard"),
        P(("replica", "shard"), None),
    )
    out_specs = (
        P(("replica", "shard"), None),
        P(("replica", "shard"), None),
        P("shard", None),
        P(None, "shard"),
        P("shard", None),
        P("shard"),
        P("shard"),
        P("shard"),
        P("shard", None),
        P("shard"),
        P("shard", None),
        P("shard"),
        P("shard"),
        P("shard"),
    )
    paired = mesh.shape["shard"] == PLANE and mesh.shape["replica"] == LINE
    body = fast_body if paired else plain_body
    return jax.shard_map(body, mesh=mesh, in_specs=in_specs, out_specs=out_specs, check_vma=False)
```

```python
import functools
import math

import jax
import jax.numpy as jnp
from jax import lax
from jax.experimental import pallas as pl
from jax.experimental.pallas import tpu as pltpu
from jax.sharding import PartitionSpec as P

HEADS = 12


scale_factor = 0.125
norm_epsilon = 1e-05
masked_value = -1e30


def normalize(resid, gain, shift):
    mean_value = jnp.mean(resid, axis=-1, keepdims=True)
    centered = resid - mean_value
    variance = jnp.mean(centered * centered, axis=-1, keepdims=True)
    return centered * lax.rsqrt(variance + norm_epsilon) * gain + shift


def gelu_exact(values):
    return jax.nn.gelu(values, approximate=False)


def keep_state(state):
    return state


def block_size(count):
    return math.gcd(count, 512)


def masked_scores(query_heads, key_heads, query_segs, key_segs):
    scores = (
        jnp.einsum("qhd,khd->hqk", query_heads, key_heads, preferred_element_type=jnp.float32)
        * scale_factor
    )
    allowed = query_segs[:, None] == key_segs[None, :]
    return (scores, allowed[None])


def grad_block(
    query_heads, dctx_heads, log_total, delta, query_segs, key_heads, value_heads, key_segs
):
    scores, allowed = masked_scores(query_heads, key_heads, query_segs, key_segs)
    probs = jnp.where(allowed, jnp.exp(scores - log_total[:, :, None]), 0.0)
    d_prob = jnp.einsum("qhd,khd->hqk", dctx_heads, value_heads, preferred_element_type=jnp.float32)
    d_scores = (probs * (d_prob - delta[:, :, None])).astype(jnp.bfloat16)
    return (probs.astype(jnp.bfloat16), d_scores)


def plain_body(
    hidden,
    segment_ids,
    w_qkv,
    b_qv,
    w_out,
    b_out,
    gain1,
    shift1,
    w_in,
    b_in,
    w_back,
    b_back,
    gain2,
    shift2,
    cotangent,
):
    tok_rows, width = hidden.shape
    heads = HEADS
    head_dim = width // heads
    seg_low = segment_ids[0]
    seg_high = segment_ids[-1]
    wq_full, wo_full, bqv_full, bo_full, g1_full, s1_full = (
        lax.all_gather(w_qkv, "shard", axis=0, tiled=True),
        lax.all_gather(w_out, "shard", axis=0, tiled=True),
        lax.all_gather(b_qv, "shard", axis=1, tiled=True),
        lax.all_gather(b_out, "shard", axis=0, tiled=True),
        lax.all_gather(gain1, "shard", axis=0, tiled=True),
        lax.all_gather(shift1, "shard", axis=0, tiled=True),
    )
    qkv = jnp.dot(hidden, wq_full, preferred_element_type=jnp.float32)
    bqv_wide = bqv_full.astype(jnp.float32)
    query = (qkv[:, :width] + bqv_wide[0]).astype(jnp.bfloat16)
    keys = qkv[:, width : 2 * width].astype(jnp.bfloat16)
    values = (qkv[:, 2 * width :] + bqv_wide[1]).astype(jnp.bfloat16)
    query_heads = query.reshape(tok_rows, heads, head_dim)
    key_local = keys.reshape(tok_rows, heads, head_dim)
    value_local = values.reshape(tok_rows, heads, head_dim)
    start_state = (
        jnp.full((heads, tok_rows), masked_value, jnp.float32),
        jnp.zeros((heads, tok_rows), jnp.float32),
        jnp.zeros((tok_rows, heads, head_dim), jnp.float32),
    )
    key_piece = lax.all_gather(keys, "shard", axis=0, tiled=True)
    value_piece = lax.all_gather(values, "shard", axis=0, tiled=True)
    seg_piece = lax.all_gather(segment_ids, "shard", axis=0, tiled=True)
    count = key_piece.shape[0]
    block = block_size(count)

    def forward_step(index, state):
        offset = index * block
        key_heads = lax.dynamic_slice_in_dim(key_piece, offset, block, 0).reshape(
            block, heads, head_dim
        )
        value_heads = lax.dynamic_slice_in_dim(value_piece, offset, block, 0).reshape(
            block, heads, head_dim
        )
        key_segs = lax.dynamic_slice_in_dim(seg_piece, offset, block, 0)

        def forward_update(state):
            running_max, running_sum, accum = state
            scores, allowed = masked_scores(query_heads, key_heads, segment_ids, key_segs)
            new_max = jnp.maximum(
                running_max, jnp.max(jnp.where(allowed, scores, masked_value), axis=-1)
            )
            factor = jnp.exp(running_max - new_max)
            weights = jnp.where(allowed, jnp.exp(scores - new_max[:, :, None]), 0.0)
            running_sum = running_sum * factor + jnp.sum(weights, axis=-1)
            accum = accum * factor.T[:, :, None] + jnp.einsum(
                "hqk,khd->qhd",
                weights.astype(jnp.bfloat16),
                value_heads,
                preferred_element_type=jnp.float32,
            )
            return (new_max, running_sum, accum)

        touches = jnp.logical_and(key_segs[0] <= seg_high, key_segs[-1] >= seg_low)
        return lax.cond(touches, forward_update, keep_state, state)

    running_max, running_sum, accum = lax.fori_loop(0, count // block, forward_step, start_state)
    context32 = accum / running_sum.T[:, :, None]
    log_total = running_max + jnp.log(running_sum)
    context = context32.reshape(tok_rows, width).astype(jnp.bfloat16)
    resid1 = (
        hidden.astype(jnp.float32)
        + jnp.dot(context, wo_full, preferred_element_type=jnp.float32)
        + bo_full.astype(jnp.float32)
    )
    normed1, norm1_pull = jax.vjp(
        normalize, resid1, g1_full.astype(jnp.float32), s1_full.astype(jnp.float32)
    )
    wi_full, bi_full, wb_full, bb_full, g2_full, s2_full = (
        lax.all_gather(w_in, "shard", axis=0, tiled=True),
        lax.all_gather(b_in, "shard", axis=0, tiled=True),
        lax.all_gather(w_back, "shard", axis=0, tiled=True),
        lax.all_gather(b_back, "shard", axis=0, tiled=True),
        lax.all_gather(gain2, "shard", axis=0, tiled=True),
        lax.all_gather(shift2, "shard", axis=0, tiled=True),
    )
    normed1_low = normed1.astype(jnp.bfloat16)
    pre = jnp.dot(normed1_low, wi_full, preferred_element_type=jnp.float32) + bi_full.astype(
        jnp.float32
    )
    act, gelu_pull = jax.vjp(gelu_exact, pre)
    act_low = act.astype(jnp.bfloat16)
    resid2 = (
        normed1
        + jnp.dot(act_low, wb_full, preferred_element_type=jnp.float32)
        + bb_full.astype(jnp.float32)
    )
    out32, norm2_pull = jax.vjp(
        normalize, resid2, g2_full.astype(jnp.float32), s2_full.astype(jnp.float32)
    )
    output = out32.astype(jnp.bfloat16)
    d_resid2, grad_gain2, grad_shift2 = norm2_pull(cotangent)
    d_branch2 = d_resid2.astype(jnp.bfloat16)
    grad_b_back = jnp.sum(d_resid2, axis=0)
    grad_w_back = jnp.einsum("tf,td->fd", act_low, d_branch2, preferred_element_type=jnp.float32)
    d_act = jnp.einsum("td,fd->tf", d_branch2, wb_full, preferred_element_type=jnp.float32)
    (d_pre,) = gelu_pull(d_act)
    grad_b_in = jnp.sum(d_pre, axis=0)
    d_pre_low = d_pre.astype(jnp.bfloat16)
    grad_w_in = jnp.einsum("td,tf->df", normed1_low, d_pre_low, preferred_element_type=jnp.float32)
    d_normed1 = d_resid2 + jnp.einsum(
        "tf,df->td", d_pre_low, wi_full, preferred_element_type=jnp.float32
    )
    d_resid1, grad_gain1, grad_shift1 = norm1_pull(d_normed1)
    grad_b_out = jnp.sum(d_resid1, axis=0)
    d_branch1 = d_resid1.astype(jnp.bfloat16)
    grad_w_out = jnp.einsum("tc,td->cd", context, d_branch1, preferred_element_type=jnp.float32)
    d_context = jnp.einsum(
        "td,cd->tc", d_branch1, wo_full, preferred_element_type=jnp.float32
    ).astype(jnp.bfloat16)
    dctx_heads = d_context.reshape(tok_rows, heads, head_dim)
    delta = jnp.einsum("qhd,qhd->hq", dctx_heads.astype(jnp.float32), context32)
    zero_heads = jnp.zeros((tok_rows, heads, head_dim), jnp.float32)
    query_key_piece = lax.all_gather(keys, "shard", axis=0, tiled=True)
    query_value_piece = lax.all_gather(values, "shard", axis=0, tiled=True)
    query_seg_piece = lax.all_gather(segment_ids, "shard", axis=0, tiled=True)
    count = query_key_piece.shape[0]
    query_block = block_size(count)

    def query_step(index, summed):
        offset = index * query_block
        key_heads = lax.dynamic_slice_in_dim(query_key_piece, offset, query_block, 0).reshape(
            query_block, heads, head_dim
        )
        value_heads = lax.dynamic_slice_in_dim(query_value_piece, offset, query_block, 0).reshape(
            query_block, heads, head_dim
        )
        key_segs = lax.dynamic_slice_in_dim(query_seg_piece, offset, query_block, 0)

        def query_update(summed):
            probs, d_scores = grad_block(
                query_heads,
                dctx_heads,
                log_total,
                delta,
                segment_ids,
                key_heads,
                value_heads,
                key_segs,
            )
            return (
                summed
                + jnp.einsum(
                    "hqk,khd->qhd", d_scores, key_heads, preferred_element_type=jnp.float32
                )
                * scale_factor
            )

        touches = jnp.logical_and(key_segs[0] <= seg_high, key_segs[-1] >= seg_low)
        return lax.cond(touches, query_update, keep_state, summed)

    d_query = lax.fori_loop(0, count // query_block, query_step, zero_heads)
    all_log_total, all_delta = (
        lax.all_gather(log_total, "shard", axis=1, tiled=True),
        lax.all_gather(delta, "shard", axis=1, tiled=True),
    )
    query_piece = lax.all_gather(query, "shard", axis=0, tiled=True)
    dctx_piece = lax.all_gather(d_context, "shard", axis=0, tiled=True)
    key_seg_piece = lax.all_gather(segment_ids, "shard", axis=0, tiled=True)
    count = query_piece.shape[0]
    key_block = block_size(count)

    def key_step(index, state):
        offset = index * key_block
        piece_query = lax.dynamic_slice_in_dim(query_piece, offset, key_block, 0).reshape(
            key_block, heads, head_dim
        )
        piece_dctx = lax.dynamic_slice_in_dim(dctx_piece, offset, key_block, 0).reshape(
            key_block, heads, head_dim
        )
        piece_segs = lax.dynamic_slice_in_dim(key_seg_piece, offset, key_block, 0)
        piece_log = lax.dynamic_slice_in_dim(all_log_total, offset, key_block, 1)
        piece_delta = lax.dynamic_slice_in_dim(all_delta, offset, key_block, 1)

        def key_update(state):
            d_key, d_value = state
            probs, d_scores = grad_block(
                piece_query,
                piece_dctx,
                piece_log,
                piece_delta,
                piece_segs,
                key_local,
                value_local,
                segment_ids,
            )
            d_key = (
                d_key
                + jnp.einsum(
                    "hqk,qhd->khd", d_scores, piece_query, preferred_element_type=jnp.float32
                )
                * scale_factor
            )
            d_value = d_value + jnp.einsum(
                "hqk,qhd->khd", probs, piece_dctx, preferred_element_type=jnp.float32
            )
            return (d_key, d_value)

        touches = jnp.logical_and(piece_segs[0] <= seg_high, piece_segs[-1] >= seg_low)
        return lax.cond(touches, key_update, keep_state, state)

    d_key_heads, d_value_heads = lax.fori_loop(
        0, count // key_block, key_step, (zero_heads, zero_heads)
    )
    d_keys = d_key_heads.reshape(tok_rows, width)
    d_values = d_value_heads.reshape(tok_rows, width)
    d_query = d_query.reshape(tok_rows, width)
    grad_b_qv = jnp.stack([jnp.sum(d_query, axis=0), jnp.sum(d_values, axis=0)], axis=0)
    d_qkv = jnp.concatenate([d_query, d_keys, d_values], axis=1).astype(jnp.bfloat16)
    grad_w_qkv = jnp.einsum("td,te->de", hidden, d_qkv, preferred_element_type=jnp.float32)
    d_hidden = d_resid1 + jnp.einsum(
        "te,de->td", d_qkv, wq_full, preferred_element_type=jnp.float32
    )
    local_grads = (
        grad_w_qkv,
        grad_b_qv,
        grad_w_out,
        grad_b_out,
        grad_gain1,
        grad_shift1,
        grad_w_in,
        grad_b_in,
        grad_w_back,
        grad_b_back,
        grad_gain2,
        grad_shift2,
    )
    shard_grads = (
        lax.psum_scatter(
            local_grads[0].astype(jnp.bfloat16), "shard", scatter_dimension=0, tiled=True
        ).astype(jnp.float32),
        lax.psum_scatter(
            local_grads[1].astype(jnp.bfloat16), "shard", scatter_dimension=1, tiled=True
        ).astype(jnp.float32),
        lax.psum_scatter(
            local_grads[2].astype(jnp.bfloat16), "shard", scatter_dimension=0, tiled=True
        ).astype(jnp.float32),
        lax.psum_scatter(
            local_grads[3].astype(jnp.bfloat16), "shard", scatter_dimension=0, tiled=True
        ).astype(jnp.float32),
        lax.psum_scatter(
            local_grads[4].astype(jnp.bfloat16), "shard", scatter_dimension=0, tiled=True
        ).astype(jnp.float32),
        lax.psum_scatter(
            local_grads[5].astype(jnp.bfloat16), "shard", scatter_dimension=0, tiled=True
        ).astype(jnp.float32),
        lax.psum_scatter(
            local_grads[6].astype(jnp.bfloat16), "shard", scatter_dimension=0, tiled=True
        ).astype(jnp.float32),
        lax.psum_scatter(
            local_grads[7].astype(jnp.bfloat16), "shard", scatter_dimension=0, tiled=True
        ).astype(jnp.float32),
        lax.psum_scatter(
            local_grads[8].astype(jnp.bfloat16), "shard", scatter_dimension=0, tiled=True
        ).astype(jnp.float32),
        lax.psum_scatter(
            local_grads[9].astype(jnp.bfloat16), "shard", scatter_dimension=0, tiled=True
        ).astype(jnp.float32),
        lax.psum_scatter(
            local_grads[10].astype(jnp.bfloat16), "shard", scatter_dimension=0, tiled=True
        ).astype(jnp.float32),
        lax.psum_scatter(
            local_grads[11].astype(jnp.bfloat16), "shard", scatter_dimension=0, tiled=True
        ).astype(jnp.float32),
    )
    total_grads = (
        lax.psum(shard_grads[0].astype(jnp.bfloat16), "replica").astype(jnp.float32),
        lax.psum(shard_grads[1].astype(jnp.bfloat16), "replica").astype(jnp.float32),
        lax.psum(shard_grads[2].astype(jnp.bfloat16), "replica").astype(jnp.float32),
        lax.psum(shard_grads[3].astype(jnp.bfloat16), "replica").astype(jnp.float32),
        lax.psum(shard_grads[4].astype(jnp.bfloat16), "replica").astype(jnp.float32),
        lax.psum(shard_grads[5].astype(jnp.bfloat16), "replica").astype(jnp.float32),
        lax.psum(shard_grads[6].astype(jnp.bfloat16), "replica").astype(jnp.float32),
        lax.psum(shard_grads[7].astype(jnp.bfloat16), "replica").astype(jnp.float32),
        lax.psum(shard_grads[8].astype(jnp.bfloat16), "replica").astype(jnp.float32),
        lax.psum(shard_grads[9].astype(jnp.bfloat16), "replica").astype(jnp.float32),
        lax.psum(shard_grads[10].astype(jnp.bfloat16), "replica").astype(jnp.float32),
        lax.psum(shard_grads[11].astype(jnp.bfloat16), "replica").astype(jnp.float32),
    )
    return (output, d_hidden) + tuple(total_grads)


PLANE = 8
LINE = 4
CHIPS = 4
MESH = pl.DeviceIdType.MESH
VMEM = pltpu.VMEM
ANY = pl.ANY
f32 = jnp.float32
bf16 = jnp.bfloat16


class Wires:
    def __init__(self, send, recv):
        self.send, self.recv, self.used = send, recv, 0
        me = lax.axis_index("shard")
        self.me = me
        self.core = me % 2
        self.chip = me // 2
        self.mate = me + 1 - 2 * self.core
        self.xn = me + 2 - 4 * (self.chip % 2)
        self.yn = me + 4 - 8 * (me // 4)
        self.dn = self.xn + 4 - 8 * (me // 4)
        self.cx = self.xn // 2
        self.cy = self.yn // 2
        self.cd = self.dn // 2

    def copy(self, src, dst, where):
        slot = self.used
        self.used += 1
        return pltpu.make_async_remote_copy(
            src_ref=src,
            dst_ref=dst,
            send_sem=self.send.at[slot],
            recv_sem=self.recv.at[slot],
            device_id=where if isinstance(where, dict) else {"shard": where},
            device_id_type=MESH,
        )

    def start(self, src, dst, where):
        made = self.copy(src, dst, where)
        made.start()
        return made


def greet(others):
    barrier = pltpu.get_barrier_semaphore()
    for other in others:
        pl.semaphore_signal(barrier, inc=1, device_id=other, device_id_type=MESH)
    pl.semaphore_wait(barrier, len(others))


def plane_others(me):
    return [{"shard": (me + step) % PLANE} for step in range(1, PLANE)]


def call(kernel, ins, outs, scratch, ident, in_spaces, out_spaces, name):
    return pl.pallas_call(
        kernel,
        out_shape=outs,
        in_specs=[pl.BlockSpec(memory_space=space) for space in in_spaces],
        out_specs=[pl.BlockSpec(memory_space=space) for space in out_spaces],
        scratch_shapes=scratch,
        compiler_params=pltpu.CompilerParams(
            collective_id=ident, has_side_effects=True, vmem_limit_bytes=60 << 20
        ),
        name=name,
    )(*ins)


def dma_sems(count):
    return [pltpu.SemaphoreType.DMA((count,)), pltpu.SemaphoreType.DMA((count,))]


class Gather:
    def __init__(self, wires, block, out, local_sem):
        w = self.w = wires
        self.out = out
        self.half = block.shape[0] // 2
        me = w.me
        self.own = pltpu.make_async_copy(block, out.at[me], local_sem)
        self.own.start()
        self.to_x = w.start(block, out.at[me], w.xn)
        self.to_y = w.start(block, out.at[me], w.yn)
        self.to_mate = w.start(block, out.at[me], w.mate)

    def relay(self):
        w, out, half = self.w, self.out, self.half
        low, high = pl.ds(0, half), pl.ds(half, half)
        self.to_x.wait_recv()
        self.x_on = w.start(out.at[w.xn, low], out.at[w.xn, low], w.yn)
        self.x_mate = w.start(out.at[w.xn], out.at[w.xn], w.mate)
        self.to_y.wait_recv()
        self.y_on = w.start(out.at[w.yn, high], out.at[w.yn, high], w.xn)
        self.y_mate = w.start(out.at[w.yn], out.at[w.yn], w.mate)

    def finish(self):
        w, out, half = self.w, self.out, self.half
        low, high = pl.ds(0, half), pl.ds(half, half)
        self.x_on.wait_recv()
        self.d_low = w.start(out.at[w.dn, low], out.at[w.dn, low], w.mate)
        self.y_on.wait_recv()
        self.d_high = w.start(out.at[w.dn, high], out.at[w.dn, high], w.mate)

    def done(self):
        for made in (self.to_mate, self.x_mate, self.y_mate, self.d_low, self.d_high):
            made.wait_recv()
        for made in (
            self.to_x,
            self.to_y,
            self.to_mate,
            self.x_on,
            self.x_mate,
            self.y_on,
            self.y_mate,
            self.d_low,
            self.d_high,
        ):
            made.wait_send()
        self.own.wait()


ROWS = 256


def dot(left, right, left_dim, right_dim):
    return lax.dot_general(
        left, right, (((left_dim,), (right_dim,)), ((), ())), preferred_element_type=f32
    )


def turn(block):
    return block.astype(f32).T


def whole_attend(query, k_ref, vt_ref, segk_ref, segq, hd):
    heads = k_ref.shape[0]
    rows = query.shape[1]
    segk = segk_ref[...]
    allowed = jnp.concatenate([segk] * (rows // 128), axis=1) == segq
    scores = [
        jnp.where(allowed, dot(k_ref[head], query[head * hd : (head + 1) * hd], 1, 0), masked_value)
        for head in range(heads)
    ]
    context, logs = [], []
    for head in range(heads):
        top = jnp.max(scores[head], axis=0, keepdims=True)
        weights = jnp.exp(scores[head] - top)
        total = jnp.sum(weights, axis=0, keepdims=True)
        acc = dot(vt_ref[head * hd : (head + 1) * hd, :], weights.astype(bf16), 1, 0)
        context.append(acc / total)
        logs.append(top + jnp.log(total))
    return jnp.concatenate(context, axis=0), jnp.concatenate(logs, axis=0)


def forward_kernel(
    hid,
    wq,
    small,
    wo,
    wi,
    wb,
    wo_o,
    wi_o,
    wb_o,
    small_o,
    wq_o,
    hidt_o,
    qt_o,
    k_o,
    v_o,
    kt_o,
    segk_o,
    segq_o,
    ctx32_o,
    log_o,
    ctx_o,
    hid_s,
    wq_s,
    vt_s,
    ctx_s,
    send,
    recv,
    loc,
    *,
    hd,
    seg_row,
):
    w = Wires(send, recv)
    greet(plane_others(w.me))
    me, core = w.me, w.core
    tok, width = hid.shape
    wide = width // CHIPS
    own_small = pltpu.make_async_copy(small, small_o.at[me], loc.at[0])
    own_small.start()
    first = Gather(w, hid, hid_s, loc.at[1])
    for chip in range(CHIPS):
        for place, section in enumerate((1, 2, 0)):
            start = section * width + chip * wide
            wq_s[chip, :, place * wide : (place + 1) * wide] = wq[:, start : start + wide]
    wq_o[me] = wq_s[w.chip]
    q_mate = w.start(wq_s.at[w.chip], wq_o.at[me], w.mate)
    q_d = w.start(wq_s.at[w.cd], wq_o.at[me], w.dn)
    q_x = w.start(wq_s.at[w.cx], wq_o.at[me], w.xn)
    q_y = w.start(wq_s.at[w.cy], wq_o.at[me], w.yn)
    smalls = [w.start(small, small_o.at[me], (me + step) % PLANE) for step in range(1, PLANE)]
    first.relay()
    q_on = []
    for came, source in ((q_x, w.xn), (q_y, w.yn), (q_d, w.dn)):
        came.wait_recv()
        q_on.append(w.start(wq_o.at[source], wq_o.at[source], w.mate))
    rest = [
        Gather(w, block, out, loc.at[3 + slot])
        for slot, (block, out) in enumerate(((wo, wo_o), (wi, wi_o), (wb, wb_o)))
    ]
    for made in smalls:
        made.wait_recv()
    own_small.wait()
    for source in range(PLANE):
        ids = small_o[source].astype(f32)[seg_row : seg_row + tok // 128]
        segq_o[source] = jnp.concatenate([ids[part : part + 1] for part in range(tok // 128)], axis=1)
        for part in range(tok // 128):
            at = source * tok + part * 128
            segk_o[at : at + 128, :] = jnp.broadcast_to(ids[part : part + 1], (128, 128)).T
    first.finish()
    for made in [q_mate] + q_on:
        made.wait_recv()
    first.done()

    names = [small_o[2 * w.chip + part].astype(f32).T for part in range(2)]
    span = wide // 2
    bias_q = jnp.concatenate([one[:span, 0:1] for one in names], axis=0)
    bias_v = jnp.concatenate([one[:span, 1:2] for one in names], axis=0)

    def project(index, carry):
        for mine in (True, False):
            source = 2 * index + (core if mine else 1 - core)
            block = hid_s[source]
            weight = wq_o[...].reshape(width, 3 * wide)
            rows = pl.ds(pl.multiple_of(source * tok, tok), tok)
            kv = dot(block, weight if mine else weight[:, : 2 * wide], 1, 0)
            kvt = kv.T
            low_v = (kvt[wide : 2 * wide] + bias_v).astype(bf16)
            kt_o[:, rows] = kvt[:wide].astype(bf16)
            vt_s[:, rows] = low_v
            back = turn(low_v).astype(bf16)
            for head in range(wide // hd):
                cols = slice(head * hd, (head + 1) * hd)
                k_o[head, rows, :] = kv[:, cols].astype(bf16)
                v_o[head, rows, :] = back[:, cols]
            if mine:
                query = kvt[2 * wide :] + bias_q
                qt_o[index] = (query.astype(bf16).astype(f32) * scale_factor).astype(bf16)
                hidt_o[index] = turn(block).astype(bf16)
        return carry

    lax.fori_loop(0, CHIPS, project, 0)
    rest[0].relay()

    def one_block(turn_no, carry):
        index = (
            (turn_no == 0) * w.cd + (turn_no == 1) * w.cx + (turn_no == 2) * w.cy + (turn_no == 3) * w.chip
        )
        context, logs = whole_attend(
            qt_o[index], k_o, vt_s, segk_o, segq_o[2 * index + core], hd
        )
        ctx32_o[index] = context
        ctx_s[index] = context.astype(bf16)
        log_o[index] = logs
        return carry

    lax.fori_loop(0, 2, one_block, 0)
    c_d = w.start(ctx_s.at[w.cd], ctx_o.at[w.chip], w.dn)
    c_x = w.start(ctx_s.at[w.cx], ctx_o.at[w.chip], w.xn)
    rest[1].relay()
    rest[0].finish()
    lax.fori_loop(2, 4, one_block, 0)
    c_y = w.start(ctx_s.at[w.cy], ctx_o.at[w.chip], w.yn)
    ctx_o[w.chip] = ctx_s[w.chip]
    rest[2].relay()
    rest[1].finish()
    rest[2].finish()
    for one in rest:
        one.done()
    for made in (c_d, c_x, c_y):
        made.wait()
    for made in [q_mate, q_x, q_y, q_d] + q_on + smalls:
        made.wait_send()


def forward_all(hid, wq, small, wo, wi, wb, hd, seg_row):
    tok, width = hid.shape
    wide = width // CHIPS
    seq = PLANE * tok
    shape = jax.ShapeDtypeStruct
    outs = [
        shape((PLANE,) + wo.shape, bf16),
        shape((PLANE,) + wi.shape, bf16),
        shape((PLANE,) + wb.shape, bf16),
        shape((PLANE,) + small.shape, bf16),
        shape((PLANE, wq.shape[0], 3 * wide), bf16),
        shape((CHIPS, width, tok), bf16),
        shape((CHIPS, wide, tok), bf16),
        shape((wide // hd, seq, hd), bf16),
        shape((wide // hd, seq, hd), bf16),
        shape((wide, seq), bf16),
        shape((seq, 128), f32),
        shape((PLANE, 1, tok), f32),
        shape((CHIPS, wide, tok), f32),
        shape((CHIPS, wide // hd, tok), f32),
        shape((CHIPS, wide, tok), bf16),
    ]
    scratch = [
        VMEM((PLANE, tok, width), bf16),
        VMEM((CHIPS, wq.shape[0], 3 * wide), bf16),
        VMEM((wide, seq), bf16),
        VMEM((CHIPS, wide, tok), bf16),
    ]
    return call(
        functools.partial(forward_kernel, hd=hd, seg_row=seg_row),
        (hid, wq, small, wo, wi, wb),
        outs,
        scratch + dma_sems(56) + [pltpu.SemaphoreType.DMA((8,))],
        1,
        [VMEM] * 6,
        [ANY] * 3 + [VMEM] * 12,
        "forward_all",
    )


def add_into(dst, other, out=None):
    out = dst if out is None else out
    lead = dst.shape[0] if len(dst.shape) == 3 else 0
    rows = dst.shape[-2]

    def go(index, carry):
        if lead:
            at = (index // (rows // 16), pl.ds(pl.multiple_of((index % (rows // 16)) * 16, 16), 16))
        else:
            at = (pl.ds(pl.multiple_of(index * 16, 16), 16),)
        out[at] = (dst[at].astype(f32) + other[at].astype(f32)).astype(out.dtype)
        return carry

    lax.fori_loop(0, max(lead, 1) * (rows // 16), go, 0)


class Reduce:
    def __init__(self, wires, full, pair, land, pick):
        self.w, self.full, self.pair, self.land = wires, full, pair, land
        self.half = pair.shape[1] // 2
        self.pick = pick
        if full is not None:
            self.meet = wires.copy(pick(full, 1 - wires.core), pair, wires.mate)

    def first(self):
        w, pair, land = self.w, self.pair, self.land
        low, high = pl.ds(0, self.half), pl.ds(self.half, self.half)
        if self.full is not None:
            self.meet.wait_recv()
            add_into(pair, self.pick(self.full, w.core))
        self.x0 = w.start(pair.at[w.cd, low], land.at[1], w.xn)
        self.y0 = w.start(pair.at[w.cd, high], land.at[3], w.yn)
        self.x1 = w.start(pair.at[w.cx, low], land.at[0], w.xn)
        self.y1 = w.start(pair.at[w.cy, high], land.at[2], w.yn)

    def second(self):
        w, pair, land = self.w, self.pair, self.land
        low, high = pl.ds(0, self.half), pl.ds(self.half, self.half)
        self.x0.wait_recv()
        add_into(pair.at[w.cy, low], land.at[1])
        self.y2 = w.start(pair.at[w.cy, low], land.at[4], w.yn)
        self.y0.wait_recv()
        add_into(pair.at[w.cx, high], land.at[3])
        self.x2 = w.start(pair.at[w.cx, high], land.at[5], w.xn)
        self.x1.wait_recv()
        add_into(pair.at[w.chip, low], land.at[0])
        self.y1.wait_recv()
        add_into(pair.at[w.chip, high], land.at[2])

    def third(self, out):
        w, pair, land = self.w, self.pair, self.land
        low, high = pl.ds(0, self.half), pl.ds(self.half, self.half)
        self.y2.wait_recv()
        add_into(pair.at[w.chip, low], land.at[4], out.at[low])
        self.x2.wait_recv()
        add_into(pair.at[w.chip, high], land.at[5], out.at[high])

    def done(self):
        made = [self.x0, self.x1, self.y0, self.y1, self.x2, self.y2]
        if self.full is not None:
            made.append(self.meet)
        for one in made:
            one.wait_send()


class Line:
    def __init__(self, wires, z, block, land, out):
        self.w, self.z, self.block, self.land, self.out = wires, z, block, land, out
        self.edge = (z == 0) | (z == LINE - 1)
        self.inner = {"replica": 1 + z // 2}
        self.outer = {"replica": 3 * (z // 2)}
        self.across = {"replica": 2 - z // 2}
        self.up = wires.copy(block, land.at[0], self.inner)
        self.over = wires.copy(block, land.at[1], {"replica": 3 - z})
        self.back = wires.copy(out, out, self.outer)

    def first(self):
        @pl.when(self.edge)
        def _():
            self.up.start()

    def second(self):
        @pl.when(jnp.logical_not(self.edge))
        def _():
            self.up.wait_recv()
            add_into(self.block, self.land.at[0])
            self.over.start()

    def third(self):
        @pl.when(jnp.logical_not(self.edge))
        def _():
            self.over.wait_recv()
            add_into(self.block, self.land.at[1], self.out)
            self.back.start()

    def done(self):
        @pl.when(self.edge)
        def _():
            self.up.wait_send()
            self.back.wait_recv()

        @pl.when(jnp.logical_not(self.edge))
        def _():
            self.over.wait_send()
            self.back.wait_send()


def back_unit(qt, dt, log, delta, k_ref, v_ref, kt_ref, segk_ref, segq, dk_ref, dv_ref, start, stop, hd):
    heads = k_ref.shape[0]
    rows = qt.shape[1]

    def step(index, state):
        at = pl.ds(pl.multiple_of(index * SPAN, SPAN), SPAN)
        segk = segk_ref[at, :]
        allowed = jnp.concatenate([segk] * (rows // 128), axis=1) == segq
        low = []
        for head in range(heads):
            part = slice(head * hd, (head + 1) * hd)
            scores = dot(k_ref[head, at, :], qt[part], 1, 0)
            d_prob = dot(v_ref[head, at, :], dt[part], 1, 0)
            probs = jnp.where(allowed, jnp.exp(scores - log[head : head + 1]), 0.0)
            low.append((probs.astype(bf16), (probs * (d_prob - delta[head])).astype(bf16)))
        made = []
        for head in range(heads):
            part = slice(head * hd, (head + 1) * hd)
            probs, d_scores = low[head]
            dv_ref[head, at, :] += dot(probs, dt[part], 1, 1)
            dk_ref[head, at, :] += dot(d_scores, qt[part], 1, 1)
            made.append(state[head] + dot(kt_ref[part, at], d_scores, 1, 0))
        return tuple(made)

    zero = tuple(jnp.zeros((hd, rows), f32) for _ in range(heads))
    return jnp.concatenate(lax.fori_loop(start, stop, step, zero), axis=0)


SPAN = 512
AHEAD = 3


def backward_kernel(
    gb,
    gi,
    go,
    dctx,
    qt,
    k,
    v,
    kt,
    segk,
    segq,
    ctx32,
    log,
    hidt,
    wq,
    small,
    dq_o,
    db_o,
    di_o,
    do_o,
    dh_o,
    small_o,
    dctx_s,
    dq_s,
    dk_s,
    dv_s,
    dkv_s,
    dkv_land,
    dqkv_s,
    gq_s,
    dh_s,
    tiny_s,
    q_pair,
    q_all,
    pair,
    land,
    dh_land,
    part,
    s_land,
    s_sum,
    zq_land,
    z_land,
    zs_land,
    send,
    recv,
    loc,
    *,
    hd,
):
    w = Wires(send, recv)
    z = lax.axis_index("replica")
    me, core = w.me, w.core
    barrier = pltpu.get_barrier_semaphore()
    for other in plane_others(me):
        pl.semaphore_signal(barrier, inc=1, device_id=other, device_id_type=MESH)
    edge = (z == 0) | (z == LINE - 1)

    @pl.when(edge)
    def _():
        pl.semaphore_signal(barrier, inc=1, device_id={"replica": 1 + z // 2}, device_id_type=MESH)
        pl.semaphore_wait(barrier, PLANE)

    @pl.when(jnp.logical_not(edge))
    def _():
        pl.semaphore_signal(barrier, inc=1, device_id={"replica": 3 * (z // 2)}, device_id_type=MESH)
        pl.semaphore_signal(barrier, inc=1, device_id={"replica": 3 - z}, device_id_type=MESH)
        pl.semaphore_wait(barrier, PLANE + 1)

    wide, tok = dctx.shape[1:]
    heads = wide // hd
    width = wq.shape[0] * wq.shape[1]
    rows, cols = go.shape[2], go.shape[3]
    dctx_made = [
        w.start(dctx.at[chip], dctx_s.at[w.chip], who)
        for chip, who in ((w.cx, w.xn), (w.cy, w.yn), (w.cd, w.dn))
    ]
    picks = []
    for slot in range(gb.shape[2] // rows):
        at = pl.ds(slot * rows, rows)
        picks.append((gb, lambda ref, core, at=at: ref.at[:, core, at], db_o.at[at]))
    for slot in range(gi.shape[3] // cols):
        at = pl.ds(slot * cols, cols)
        picks.append((gi, lambda ref, core, at=at: ref.at[:, core, :, at], di_o.at[:, at]))
    picks.append((go, lambda ref, core: ref.at[:, core], do_o))
    count = len(picks)
    chunks = [
        Reduce(w, full, pair.at[slot], land.at[slot], pick)
        for slot, (full, pick, _) in enumerate(picks)
    ]
    lines = [
        Line(w, z, part.at[slot], z_land.at[slot], out) for slot, (_, _, out) in enumerate(picks)
    ]

    for one in chunks[:AHEAD]:
        one.meet.start()

    def tick(now):
        if now + AHEAD < count:
            chunks[now + AHEAD].meet.start()
        if now < count:
            chunks[now].first()
        if 0 <= now - 1 < count:
            chunks[now - 1].second()
        if 0 <= now - 2 < count:
            chunks[now - 2].third(part.at[now - 2])
            lines[now - 2].first()
        if 0 <= now - 3 < count:
            lines[now - 3].second()
        if 0 <= now - 4 < count:
            lines[now - 4].third()

    dctx_s[w.chip] = dctx[w.chip]
    dk_s[...] = jnp.zeros_like(dk_s)
    dv_s[...] = jnp.zeros_like(dv_s)
    dq_s[...] = jnp.zeros_like(dq_s)
    ticks = 0
    tick(ticks)
    ticks += 1
    steps = PLANE * tok // SPAN
    for turn_no, index in enumerate((w.chip, w.cx, w.cy, w.cd)):
        if turn_no:
            dctx_made[turn_no - 1].wait_recv()
        for half in range(2):
            dt = dctx_s[index]
            product = dt.astype(f32) * ctx32[index]
            delta = [
                jnp.sum(product[head * hd : (head + 1) * hd], axis=0, keepdims=True)
                for head in range(heads)
            ]
            dq_s[index] += back_unit(
                qt[index],
                dt,
                log[index],
                delta,
                k,
                v,
                kt,
                segk,
                segq[2 * index + core],
                dk_s,
                dv_s,
                half * steps // 2,
                (half + 1) * steps // 2,
                hd,
            )
            tick(ticks)
            ticks += 1

    def gather_rows(source):
        at = pl.ds(pl.multiple_of(source * tok, tok), tok)
        return jnp.concatenate(
            [dk_s[head, at, :] for head in range(heads)] + [dv_s[head, at, :] for head in range(heads)],
            axis=1,
        )

    def away(index, carry):
        dkv_s[index] = gather_rows(2 * index + 1 - core).astype(bf16)
        return carry

    lax.fori_loop(0, CHIPS, away, 0)
    meet = w.start(dkv_s, dkv_land, w.mate)
    tick(ticks)
    ticks += 1
    meet.wait_recv()

    def join(index, sums):
        dkv = gather_rows(2 * index + core) + dkv_land[index].astype(f32)
        dq = (dq_s[index] * scale_factor).T
        dqkv = jnp.concatenate([dkv, dq], axis=1)
        low = dqkv.astype(bf16)
        dqkv_s[index] = low
        return sums + jnp.sum(dqkv, axis=0, keepdims=True)

    sums = lax.fori_loop(0, CHIPS, join, jnp.zeros((1, 3 * wide), f32))
    span = wide // 2
    tiny_s[...] = small[...]
    for side in range(2):
        slot = 2 * w.chip + side
        tiny_s[slot, 0:1, :span] = sums[:, 2 * wide + side * span : 2 * wide + (side + 1) * span]
        tiny_s[slot, 1:2, :span] = sums[:, wide + side * span : wide + (side + 1) * span]
    for half in range(2):
        at = slice(half * width // 2, (half + 1) * width // 2)
        total = sum(dot(hidt[index, at, :], dqkv_s[index], 1, 0) for index in range(CHIPS))
        gq_s[2 * half : 2 * half + 2] = total.astype(bf16).reshape(2, 2, width // PLANE, 3 * wide)
    q_meet = w.start(gq_s.at[:, 1 - core], q_pair, w.mate)
    smalls = [
        w.start(tiny_s.at[(me + step) % PLANE], s_land.at[me], (me + step) % PLANE)
        for step in range(1, PLANE)
    ]
    s_land[me] = tiny_s[me]
    hidden = Reduce(w, None, dh_s, dh_land, None)

    def down(index, carry):
        dh_s[index] = dot(dqkv_s[index], wq[...].reshape(width, 3 * wide), 1, 1).astype(bf16)
        return carry

    q_meet.wait_recv()
    add_into(q_pair, gq_s.at[:, core])
    q_made = [
        w.start(q_pair.at[chip], q_all.at[w.chip], who)
        for chip, who in ((w.cx, w.xn), (w.cy, w.yn), (w.cd, w.dn))
    ]
    q_all[w.chip] = q_pair[w.chip]
    q_lines = [
        Line(w, z, q_all.at[chip], zq_land.at[chip], dq_o.at[chip]) for chip in (w.chip, w.cx, w.cy, w.cd)
    ]
    q_lines[0].first()
    lax.fori_loop(0, CHIPS, down, 0)
    hidden.first()
    tick(ticks)
    ticks += 1
    for one in smalls:
        one.wait_recv()
    s_sum[...] = jnp.sum(s_land[...], axis=0)
    s_line = Line(w, z, s_sum, zs_land, small_o)
    s_line.first()
    for slot in (1, 2, 3):
        q_made[slot - 1].wait_recv()
        q_lines[slot].first()
        q_lines[slot - 1].second()
        if slot > 1:
            q_lines[slot - 2].third()
    tick(ticks)
    ticks += 1
    s_line.second()
    q_lines[3].second()
    q_lines[2].third()
    hidden.second()
    while ticks < count + 4:
        tick(ticks)
        ticks += 1
    s_line.third()
    q_lines[3].third()
    hidden.third(dh_o)
    for one in smalls + q_made + [q_meet, meet] + dctx_made:
        one.wait_send()
    for one in chunks + [hidden]:
        one.done()
    for one in lines + q_lines + [s_line]:
        one.done()


def backward_all(gb, gi, go, dctx, qt, k, v, kt, segk, segq, ctx32, log, hidt, wq, small, hd):
    rows, cols = go.shape[2:]
    wide, tok = dctx.shape[1:]
    width = hidt.shape[1]
    count = gb.shape[2] // rows + gi.shape[3] // cols + 1
    q_block = (CHIPS, wq.shape[1], wq.shape[2])
    tail = small.shape[1:]
    shape = jax.ShapeDtypeStruct
    outs = [
        shape(q_block, bf16),
        shape(gb.shape[2:], bf16),
        shape(gi.shape[2:], bf16),
        shape(go.shape[2:], bf16),
        shape((tok, width), bf16),
        shape(tail, f32),
    ]
    scratch = [
        VMEM(dctx.shape, bf16),
        VMEM(dctx.shape, f32),
        VMEM(k.shape, f32),
        VMEM(k.shape, f32),
        VMEM((CHIPS, tok, 2 * wide), bf16),
        VMEM((CHIPS, tok, 2 * wide), bf16),
        VMEM((CHIPS, tok, 3 * wide), bf16),
        VMEM((CHIPS, 2) + wq.shape[1:], bf16),
        VMEM((CHIPS, tok, width), bf16),
        VMEM(small.shape, f32),
        VMEM(q_block, bf16),
        VMEM(q_block, bf16),
        VMEM((count, CHIPS, rows, cols), bf16),
        VMEM((count, 6, rows // 2, cols), bf16),
        VMEM((6, tok // 2, width), bf16),
        VMEM((count, rows, cols), bf16),
        VMEM(small.shape, f32),
        VMEM(tail, f32),
        VMEM((CHIPS, 2) + q_block[1:], bf16),
        VMEM((count, 2, rows, cols), bf16),
        VMEM((2,) + tail, f32),
    ]
    return call(
        functools.partial(backward_kernel, hd=hd),
        (gb, gi, go, dctx, qt, k, v, kt, segk, segq, ctx32, log, hidt, wq, small),
        outs,
        scratch + dma_sems(count * 10 + 42) + [pltpu.SemaphoreType.DMA((2,))],
        2,
        [VMEM] * 15,
        [VMEM] * 6,
        "backward_all",
    )


def each(rows, block, step, init):
    def go(index, carry):
        return step(pl.ds(pl.multiple_of(index * block, block), block), carry)

    return lax.fori_loop(0, rows // block, go, init)


def fold_rows(block):
    return jnp.sum(block.reshape(block.shape[0] // 8, 8, block.shape[1]), axis=0)


def settle(block):
    return jnp.sum(block, axis=0, keepdims=True)


def vector(small, row, part):
    return jnp.concatenate(
        [small[source, row : row + 1, :part].astype(f32) for source in range(PLANE)], axis=1
    )


def put_vector(stack, row, value, part):
    for source in range(PLANE):
        stack[source, row : row + 1, :part] = value[:, source * part : (source + 1) * part]


BAND = 32


def moments(block):
    mean_value = jnp.mean(block, axis=-1, keepdims=True)
    centered = block - mean_value
    scale = lax.rsqrt(jnp.mean(centered * centered, axis=-1, keepdims=True) + norm_epsilon)
    return centered * scale, scale


def norm_back(grad, gain, unit, scale):
    scaled = grad * gain
    return (
        scaled
        - jnp.mean(scaled, axis=-1, keepdims=True)
        - unit * jnp.mean(scaled * unit, axis=-1, keepdims=True)
    ) * scale


def middle_kernel(
    hid,
    ctxt,
    wo,
    wi,
    wb,
    small,
    cot,
    out_o,
    gb_o,
    gi_o,
    go_o,
    dctx_o,
    dresid_o,
    stack_o,
    acc_s,
    unit_s,
    scale_s,
    low_s,
    lowt_s,
    act_s,
    slope_s,
    wide_s,
    grad_s,
):
    tok, width = hid.shape
    ff = wi.shape[2]
    part = width // PLANE
    fold = ff // width
    lines = ff // PLANE // 128
    stack_o[...] = jnp.zeros_like(stack_o)
    wo_v = wo[...].reshape(width, width)
    bo, g1, s1, bb, g2, s2 = (vector(small, row, part) for row in range(2, 8))
    context = turn(ctxt[...].reshape(width, tok)).astype(bf16)
    acc_s[...] = dot(context, wo_v, 1, 0)

    def open_one(at, carry):
        unit, scale = moments(hid[at, :].astype(f32) + acc_s[at, :] + bo)
        unit_s[at, :] = unit
        scale_s[at, :] = jnp.broadcast_to(scale, (BAND, 128))
        normed = unit * g1 + s1
        low_s[at, :] = normed.astype(bf16)
        acc_s[at, :] = normed + bb
        return carry

    each(tok, BAND, open_one, 0)

    def up(chunk, carry):
        cols = pl.ds(pl.multiple_of(chunk * width, width), width)
        bias = jnp.concatenate(
            [
                small[2 * chunk + side, 8 + row : 9 + row, :].astype(f32)
                for side in range(2)
                for row in range(lines)
            ],
            axis=1,
        )
        wide_s[...] = dot(low_s[...], wi[:, :, cols].reshape(width, width), 1, 0)

        def gelu(at, carry):
            pre = wide_s[at, :] + bias
            phi = 0.5 * (1.0 + lax.erf(pre * math.sqrt(0.5)))
            act_s[chunk, at, :] = (pre * phi).astype(bf16)
            slope_s[chunk, at, :] = phi + pre * (
                jnp.exp(-0.5 * pre * pre) * (1.0 / math.sqrt(2.0 * math.pi))
            )
            return carry

        each(tok, BAND, gelu, 0)
        acc_s[...] += dot(act_s[chunk], wb[pl.ds(2 * chunk, 2)].reshape(width, width), 1, 0)
        return carry

    lax.fori_loop(0, fold, up, 0)
    zero = jnp.zeros((8, width), f32)

    def close(at, sums):
        unit, scale = moments(acc_s[at, :])
        out_o[at, :] = (unit * g2 + s2).astype(bf16)
        grad = cot[at, :]
        d_resid = norm_back(grad, g2, unit, scale)
        acc_s[at, :] = d_resid
        grad_s[at, :] = d_resid.astype(bf16)
        return (sums[0] + fold_rows(d_resid), sums[1] + fold_rows(grad * unit), sums[2] + fold_rows(grad))

    sums = each(tok, BAND, close, (zero, zero, zero))
    for row, value in zip((5, 6, 7), sums):
        put_vector(stack_o, row, settle(value), part)

    lowt_s[...] = turn(low_s[...]).astype(bf16)

    def down(chunk, carry):
        cols = pl.ds(pl.multiple_of(chunk * width, width), width)
        grad = grad_s[...]
        gb_o[chunk] = (
            dot(turn(act_s[chunk]).astype(bf16), grad, 1, 0)
            .astype(bf16)
            .reshape(2, ff // PLANE, width)
        )
        wide_s[...] = dot(grad, wb[pl.ds(2 * chunk, 2)].reshape(width, width), 1, 1)

        def through(at, sums):
            d_pre = wide_s[at, :] * slope_s[chunk, at, :]
            act_s[chunk, at, :] = d_pre.astype(bf16)
            return sums + fold_rows(d_pre)

        total = settle(each(tok, BAND, through, zero))
        for side in range(2):
            for row in range(lines):
                start = (side * lines + row) * 128
                stack_o[2 * chunk + side, 8 + row : 9 + row, :] = total[:, start : start + 128]
        d_low = act_s[chunk]
        gi_o[:, :, :, cols] = (
            dot(lowt_s[...], d_low, 1, 0).astype(bf16).reshape(CHIPS, 2, part, width)
        )
        acc_s[...] += dot(d_low, wi[:, :, cols].reshape(width, width), 1, 1)
        return carry

    lax.fori_loop(0, fold, down, 0)

    def finish(at, sums):
        unit = unit_s[at, :]
        grad = acc_s[at, :]
        d_resid = norm_back(grad, g1, unit, scale_s[at, 0:1])
        dresid_o[at, :] = d_resid
        grad_s[at, :] = d_resid.astype(bf16)
        return (sums[0] + fold_rows(d_resid), sums[1] + fold_rows(grad * unit), sums[2] + fold_rows(grad))

    sums = each(tok, BAND, finish, (zero, zero, zero))
    for row, value in zip((2, 3, 4), sums):
        put_vector(stack_o, row, settle(value), part)
    grad = grad_s[...]
    go_o[...] = (
        dot(ctxt[...].reshape(width, tok), grad, 1, 0).astype(bf16).reshape(CHIPS, 2, part, width)
    )
    dctx_o[...] = dot(wo_v, grad, 1, 1).astype(bf16).reshape(CHIPS, width // CHIPS, tok)


def middle_all(hid, ctxt, wo, wi, wb, small, cot):
    tok, width = hid.shape
    ff = wi.shape[2]
    part = width // PLANE
    fold = ff // width
    shape = jax.ShapeDtypeStruct
    outs = [
        shape((tok, width), bf16),
        shape((CHIPS, 2, ff // PLANE, width), bf16),
        shape((CHIPS, 2, part, ff), bf16),
        shape((CHIPS, 2, part, width), bf16),
        shape((CHIPS, width // CHIPS, tok), bf16),
        shape((tok, width), f32),
        shape((PLANE, 16, 128), f32),
    ]
    scratch = [
        VMEM((tok, width), f32),
        VMEM((tok, width), f32),
        VMEM((tok, 128), f32),
        VMEM((tok, width), bf16),
        VMEM((width, tok), bf16),
        VMEM((fold, tok, width), bf16),
        VMEM((fold, tok, width), f32),
        VMEM((tok, width), f32),
        VMEM((tok, width), bf16),
    ]
    return pl.pallas_call(
        middle_kernel,
        out_shape=outs,
        in_specs=[pl.BlockSpec(memory_space=VMEM)] * 7,
        out_specs=[pl.BlockSpec(memory_space=VMEM)] * 7,
        scratch_shapes=scratch,
        compiler_params=pltpu.CompilerParams(vmem_limit_bytes=56 << 20),
        name="middle_all",
    )(hid, ctxt, wo, wi, wb, small, cot)


def finish_kernel(dq, db, di, do, dh, resid, q_o, b_o, i_o, o_o, h_o):
    wide = dq.shape[2] // 3
    width = resid.shape[1]
    for chip in range(CHIPS):
        for place, section in enumerate((1, 2, 0)):
            start = section * width + chip * wide
            q_o[:, start : start + wide] = dq[chip, :, place * wide : (place + 1) * wide].astype(f32)
    b_o[...] = db[...].astype(f32)
    i_o[...] = di[...].astype(f32)
    o_o[...] = do[...].astype(f32)
    h_o[...] = resid[...] + dh[...].astype(f32)


def finish_all(dq, db, di, do, dh, resid):
    part, wide = dq.shape[1:]
    shape = jax.ShapeDtypeStruct
    outs = [shape((part, CHIPS * wide), f32)] + [shape(one.shape, f32) for one in (db, di, do, dh)]
    return pl.pallas_call(
        finish_kernel,
        out_shape=outs,
        in_specs=[pl.BlockSpec(memory_space=VMEM)] * 6,
        out_specs=[pl.BlockSpec(memory_space=VMEM)] * 5,
        compiler_params=pltpu.CompilerParams(vmem_limit_bytes=32 << 20),
        name="finish_all",
    )(dq, db, di, do, dh, resid)


def fast_body(
    hidden,
    segment_ids,
    w_qkv,
    b_qv,
    w_out,
    b_out,
    gain1,
    shift1,
    w_in,
    b_in,
    w_back,
    b_back,
    gain2,
    shift2,
    cotangent,
):
    tok, width = hidden.shape
    hd = width // HEADS
    part = w_qkv.shape[0]
    wide = width // CHIPS
    ff = w_in.shape[1]
    lines = b_in.shape[0] // 128
    narrow = jnp.concatenate(
        [b_qv] + [one[None] for one in (b_out, gain1, shift1, b_back, gain2, shift2)], axis=0
    )
    small = jnp.concatenate(
        [
            jnp.pad(narrow, ((0, 0), (0, 128 - part))),
            b_in.reshape(lines, 128),
            segment_ids.astype(bf16).reshape(tok // 128, 128),
            jnp.zeros((8 - lines - tok // 128, 128), bf16),
        ],
        axis=0,
    )
    (
        wo_all,
        wi_all,
        wb_all,
        small_all,
        wq_all,
        hidt,
        qt,
        k,
        v,
        kt,
        segk,
        segq,
        ctx32,
        log_total,
        ctx_parts,
    ) = forward_all(hidden, w_qkv, small, w_out, w_in, w_back, hd, 8 + lines)
    output, gb, gi, go, dctx, d_resid1, stack = middle_all(
        hidden, ctx_parts, wo_all, wi_all, wb_all, small_all, cotangent
    )
    dq, db, di, do, dh, tiny = backward_all(
        gb, gi, go, dctx, qt, k, v, kt, segk, segq, ctx32, log_total, hidt, wq_all, stack, hd
    )
    g_qkv, g_back, g_in, g_out, d_hidden = finish_all(dq, db, di, do, dh, d_resid1)
    return (
        output,
        d_hidden,
        g_qkv,
        tiny[0:2, :part],
        g_out,
        tiny[2, :part],
        tiny[3, :part],
        tiny[4, :part],
        g_in,
        tiny[8 : 8 + lines].reshape(ff // PLANE),
        g_back,
        tiny[5, :part],
        tiny[6, :part],
        tiny[7, :part],
    )


def solution(mesh):
    in_specs = (
        P(("replica", "shard"), None),
        P(("replica", "shard")),
        P("shard", None),
        P(None, "shard"),
        P("shard", None),
        P("shard"),
        P("shard"),
        P("shard"),
        P("shard", None),
        P("shard"),
        P("shard", None),
        P("shard"),
        P("shard"),
        P("shard"),
        P(("replica", "shard"), None),
    )
    out_specs = (
        P(("replica", "shard"), None),
        P(("replica", "shard"), None),
        P("shard", None),
        P(None, "shard"),
        P("shard", None),
        P("shard"),
        P("shard"),
        P("shard"),
        P("shard", None),
        P("shard"),
        P("shard", None),
        P("shard"),
        P("shard"),
        P("shard"),
    )
    paired = mesh.shape["shard"] == PLANE and mesh.shape["replica"] == LINE
    body = fast_body if paired else plain_body
    return jax.shard_map(body, mesh=mesh, in_specs=in_specs, out_specs=out_specs, check_vma=False)
```

```python
import functools
import math

import jax
import jax.numpy as jnp
from jax import lax
from jax.experimental import pallas as pl
from jax.experimental.pallas import tpu as pltpu
from jax.sharding import PartitionSpec as P

HEADS = 12


scale_factor = 0.125
norm_epsilon = 1e-05
masked_value = -1e30


def normalize(resid, gain, shift):
    mean_value = jnp.mean(resid, axis=-1, keepdims=True)
    centered = resid - mean_value
    variance = jnp.mean(centered * centered, axis=-1, keepdims=True)
    return centered * lax.rsqrt(variance + norm_epsilon) * gain + shift


def gelu_exact(values):
    return jax.nn.gelu(values, approximate=False)


def keep_state(state):
    return state


def block_size(count):
    return math.gcd(count, 512)


def masked_scores(query_heads, key_heads, query_segs, key_segs):
    scores = (
        jnp.einsum("qhd,khd->hqk", query_heads, key_heads, preferred_element_type=jnp.float32)
        * scale_factor
    )
    allowed = query_segs[:, None] == key_segs[None, :]
    return (scores, allowed[None])


def grad_block(
    query_heads, dctx_heads, log_total, delta, query_segs, key_heads, value_heads, key_segs
):
    scores, allowed = masked_scores(query_heads, key_heads, query_segs, key_segs)
    probs = jnp.where(allowed, jnp.exp(scores - log_total[:, :, None]), 0.0)
    d_prob = jnp.einsum("qhd,khd->hqk", dctx_heads, value_heads, preferred_element_type=jnp.float32)
    d_scores = (probs * (d_prob - delta[:, :, None])).astype(jnp.bfloat16)
    return (probs.astype(jnp.bfloat16), d_scores)


def plain_body(
    hidden,
    segment_ids,
    w_qkv,
    b_qv,
    w_out,
    b_out,
    gain1,
    shift1,
    w_in,
    b_in,
    w_back,
    b_back,
    gain2,
    shift2,
    cotangent,
):
    tok_rows, width = hidden.shape
    heads = HEADS
    head_dim = width // heads
    seg_low = segment_ids[0]
    seg_high = segment_ids[-1]
    wq_full, wo_full, bqv_full, bo_full, g1_full, s1_full = (
        lax.all_gather(w_qkv, "shard", axis=0, tiled=True),
        lax.all_gather(w_out, "shard", axis=0, tiled=True),
        lax.all_gather(b_qv, "shard", axis=1, tiled=True),
        lax.all_gather(b_out, "shard", axis=0, tiled=True),
        lax.all_gather(gain1, "shard", axis=0, tiled=True),
        lax.all_gather(shift1, "shard", axis=0, tiled=True),
    )
    qkv = jnp.dot(hidden, wq_full, preferred_element_type=jnp.float32)
    bqv_wide = bqv_full.astype(jnp.float32)
    query = (qkv[:, :width] + bqv_wide[0]).astype(jnp.bfloat16)
    keys = qkv[:, width : 2 * width].astype(jnp.bfloat16)
    values = (qkv[:, 2 * width :] + bqv_wide[1]).astype(jnp.bfloat16)
    query_heads = query.reshape(tok_rows, heads, head_dim)
    key_local = keys.reshape(tok_rows, heads, head_dim)
    value_local = values.reshape(tok_rows, heads, head_dim)
    start_state = (
        jnp.full((heads, tok_rows), masked_value, jnp.float32),
        jnp.zeros((heads, tok_rows), jnp.float32),
        jnp.zeros((tok_rows, heads, head_dim), jnp.float32),
    )
    key_piece = lax.all_gather(keys, "shard", axis=0, tiled=True)
    value_piece = lax.all_gather(values, "shard", axis=0, tiled=True)
    seg_piece = lax.all_gather(segment_ids, "shard", axis=0, tiled=True)
    count = key_piece.shape[0]
    block = block_size(count)

    def forward_step(index, state):
        offset = index * block
        key_heads = lax.dynamic_slice_in_dim(key_piece, offset, block, 0).reshape(
            block, heads, head_dim
        )
        value_heads = lax.dynamic_slice_in_dim(value_piece, offset, block, 0).reshape(
            block, heads, head_dim
        )
        key_segs = lax.dynamic_slice_in_dim(seg_piece, offset, block, 0)

        def forward_update(state):
            running_max, running_sum, accum = state
            scores, allowed = masked_scores(query_heads, key_heads, segment_ids, key_segs)
            new_max = jnp.maximum(
                running_max, jnp.max(jnp.where(allowed, scores, masked_value), axis=-1)
            )
            factor = jnp.exp(running_max - new_max)
            weights = jnp.where(allowed, jnp.exp(scores - new_max[:, :, None]), 0.0)
            running_sum = running_sum * factor + jnp.sum(weights, axis=-1)
            accum = accum * factor.T[:, :, None] + jnp.einsum(
                "hqk,khd->qhd",
                weights.astype(jnp.bfloat16),
                value_heads,
                preferred_element_type=jnp.float32,
            )
            return (new_max, running_sum, accum)

        touches = jnp.logical_and(key_segs[0] <= seg_high, key_segs[-1] >= seg_low)
        return lax.cond(touches, forward_update, keep_state, state)

    running_max, running_sum, accum = lax.fori_loop(0, count // block, forward_step, start_state)
    context32 = accum / running_sum.T[:, :, None]
    log_total = running_max + jnp.log(running_sum)
    context = context32.reshape(tok_rows, width).astype(jnp.bfloat16)
    resid1 = (
        hidden.astype(jnp.float32)
        + jnp.dot(context, wo_full, preferred_element_type=jnp.float32)
        + bo_full.astype(jnp.float32)
    )
    normed1, norm1_pull = jax.vjp(
        normalize, resid1, g1_full.astype(jnp.float32), s1_full.astype(jnp.float32)
    )
    wi_full, bi_full, wb_full, bb_full, g2_full, s2_full = (
        lax.all_gather(w_in, "shard", axis=0, tiled=True),
        lax.all_gather(b_in, "shard", axis=0, tiled=True),
        lax.all_gather(w_back, "shard", axis=0, tiled=True),
        lax.all_gather(b_back, "shard", axis=0, tiled=True),
        lax.all_gather(gain2, "shard", axis=0, tiled=True),
        lax.all_gather(shift2, "shard", axis=0, tiled=True),
    )
    normed1_low = normed1.astype(jnp.bfloat16)
    pre = jnp.dot(normed1_low, wi_full, preferred_element_type=jnp.float32) + bi_full.astype(
        jnp.float32
    )
    act, gelu_pull = jax.vjp(gelu_exact, pre)
    act_low = act.astype(jnp.bfloat16)
    resid2 = (
        normed1
        + jnp.dot(act_low, wb_full, preferred_element_type=jnp.float32)
        + bb_full.astype(jnp.float32)
    )
    out32, norm2_pull = jax.vjp(
        normalize, resid2, g2_full.astype(jnp.float32), s2_full.astype(jnp.float32)
    )
    output = out32.astype(jnp.bfloat16)
    d_resid2, grad_gain2, grad_shift2 = norm2_pull(cotangent)
    d_branch2 = d_resid2.astype(jnp.bfloat16)
    grad_b_back = jnp.sum(d_resid2, axis=0)
    grad_w_back = jnp.einsum("tf,td->fd", act_low, d_branch2, preferred_element_type=jnp.float32)
    d_act = jnp.einsum("td,fd->tf", d_branch2, wb_full, preferred_element_type=jnp.float32)
    (d_pre,) = gelu_pull(d_act)
    grad_b_in = jnp.sum(d_pre, axis=0)
    d_pre_low = d_pre.astype(jnp.bfloat16)
    grad_w_in = jnp.einsum("td,tf->df", normed1_low, d_pre_low, preferred_element_type=jnp.float32)
    d_normed1 = d_resid2 + jnp.einsum(
        "tf,df->td", d_pre_low, wi_full, preferred_element_type=jnp.float32
    )
    d_resid1, grad_gain1, grad_shift1 = norm1_pull(d_normed1)
    grad_b_out = jnp.sum(d_resid1, axis=0)
    d_branch1 = d_resid1.astype(jnp.bfloat16)
    grad_w_out = jnp.einsum("tc,td->cd", context, d_branch1, preferred_element_type=jnp.float32)
    d_context = jnp.einsum(
        "td,cd->tc", d_branch1, wo_full, preferred_element_type=jnp.float32
    ).astype(jnp.bfloat16)
    dctx_heads = d_context.reshape(tok_rows, heads, head_dim)
    delta = jnp.einsum("qhd,qhd->hq", dctx_heads.astype(jnp.float32), context32)
    zero_heads = jnp.zeros((tok_rows, heads, head_dim), jnp.float32)
    query_key_piece = lax.all_gather(keys, "shard", axis=0, tiled=True)
    query_value_piece = lax.all_gather(values, "shard", axis=0, tiled=True)
    query_seg_piece = lax.all_gather(segment_ids, "shard", axis=0, tiled=True)
    count = query_key_piece.shape[0]
    query_block = block_size(count)

    def query_step(index, summed):
        offset = index * query_block
        key_heads = lax.dynamic_slice_in_dim(query_key_piece, offset, query_block, 0).reshape(
            query_block, heads, head_dim
        )
        value_heads = lax.dynamic_slice_in_dim(query_value_piece, offset, query_block, 0).reshape(
            query_block, heads, head_dim
        )
        key_segs = lax.dynamic_slice_in_dim(query_seg_piece, offset, query_block, 0)

        def query_update(summed):
            probs, d_scores = grad_block(
                query_heads,
                dctx_heads,
                log_total,
                delta,
                segment_ids,
                key_heads,
                value_heads,
                key_segs,
            )
            return (
                summed
                + jnp.einsum(
                    "hqk,khd->qhd", d_scores, key_heads, preferred_element_type=jnp.float32
                )
                * scale_factor
            )

        touches = jnp.logical_and(key_segs[0] <= seg_high, key_segs[-1] >= seg_low)
        return lax.cond(touches, query_update, keep_state, summed)

    d_query = lax.fori_loop(0, count // query_block, query_step, zero_heads)
    all_log_total, all_delta = (
        lax.all_gather(log_total, "shard", axis=1, tiled=True),
        lax.all_gather(delta, "shard", axis=1, tiled=True),
    )
    query_piece = lax.all_gather(query, "shard", axis=0, tiled=True)
    dctx_piece = lax.all_gather(d_context, "shard", axis=0, tiled=True)
    key_seg_piece = lax.all_gather(segment_ids, "shard", axis=0, tiled=True)
    count = query_piece.shape[0]
    key_block = block_size(count)

    def key_step(index, state):
        offset = index * key_block
        piece_query = lax.dynamic_slice_in_dim(query_piece, offset, key_block, 0).reshape(
            key_block, heads, head_dim
        )
        piece_dctx = lax.dynamic_slice_in_dim(dctx_piece, offset, key_block, 0).reshape(
            key_block, heads, head_dim
        )
        piece_segs = lax.dynamic_slice_in_dim(key_seg_piece, offset, key_block, 0)
        piece_log = lax.dynamic_slice_in_dim(all_log_total, offset, key_block, 1)
        piece_delta = lax.dynamic_slice_in_dim(all_delta, offset, key_block, 1)

        def key_update(state):
            d_key, d_value = state
            probs, d_scores = grad_block(
                piece_query,
                piece_dctx,
                piece_log,
                piece_delta,
                piece_segs,
                key_local,
                value_local,
                segment_ids,
            )
            d_key = (
                d_key
                + jnp.einsum(
                    "hqk,qhd->khd", d_scores, piece_query, preferred_element_type=jnp.float32
                )
                * scale_factor
            )
            d_value = d_value + jnp.einsum(
                "hqk,qhd->khd", probs, piece_dctx, preferred_element_type=jnp.float32
            )
            return (d_key, d_value)

        touches = jnp.logical_and(piece_segs[0] <= seg_high, piece_segs[-1] >= seg_low)
        return lax.cond(touches, key_update, keep_state, state)

    d_key_heads, d_value_heads = lax.fori_loop(
        0, count // key_block, key_step, (zero_heads, zero_heads)
    )
    d_keys = d_key_heads.reshape(tok_rows, width)
    d_values = d_value_heads.reshape(tok_rows, width)
    d_query = d_query.reshape(tok_rows, width)
    grad_b_qv = jnp.stack([jnp.sum(d_query, axis=0), jnp.sum(d_values, axis=0)], axis=0)
    d_qkv = jnp.concatenate([d_query, d_keys, d_values], axis=1).astype(jnp.bfloat16)
    grad_w_qkv = jnp.einsum("td,te->de", hidden, d_qkv, preferred_element_type=jnp.float32)
    d_hidden = d_resid1 + jnp.einsum(
        "te,de->td", d_qkv, wq_full, preferred_element_type=jnp.float32
    )
    local_grads = (
        grad_w_qkv,
        grad_b_qv,
        grad_w_out,
        grad_b_out,
        grad_gain1,
        grad_shift1,
        grad_w_in,
        grad_b_in,
        grad_w_back,
        grad_b_back,
        grad_gain2,
        grad_shift2,
    )
    shard_grads = (
        lax.psum_scatter(
            local_grads[0].astype(jnp.bfloat16), "shard", scatter_dimension=0, tiled=True
        ).astype(jnp.float32),
        lax.psum_scatter(
            local_grads[1].astype(jnp.bfloat16), "shard", scatter_dimension=1, tiled=True
        ).astype(jnp.float32),
        lax.psum_scatter(
            local_grads[2].astype(jnp.bfloat16), "shard", scatter_dimension=0, tiled=True
        ).astype(jnp.float32),
        lax.psum_scatter(
            local_grads[3].astype(jnp.bfloat16), "shard", scatter_dimension=0, tiled=True
        ).astype(jnp.float32),
        lax.psum_scatter(
            local_grads[4].astype(jnp.bfloat16), "shard", scatter_dimension=0, tiled=True
        ).astype(jnp.float32),
        lax.psum_scatter(
            local_grads[5].astype(jnp.bfloat16), "shard", scatter_dimension=0, tiled=True
        ).astype(jnp.float32),
        lax.psum_scatter(
            local_grads[6].astype(jnp.bfloat16), "shard", scatter_dimension=0, tiled=True
        ).astype(jnp.float32),
        lax.psum_scatter(
            local_grads[7].astype(jnp.bfloat16), "shard", scatter_dimension=0, tiled=True
        ).astype(jnp.float32),
        lax.psum_scatter(
            local_grads[8].astype(jnp.bfloat16), "shard", scatter_dimension=0, tiled=True
        ).astype(jnp.float32),
        lax.psum_scatter(
            local_grads[9].astype(jnp.bfloat16), "shard", scatter_dimension=0, tiled=True
        ).astype(jnp.float32),
        lax.psum_scatter(
            local_grads[10].astype(jnp.bfloat16), "shard", scatter_dimension=0, tiled=True
        ).astype(jnp.float32),
        lax.psum_scatter(
            local_grads[11].astype(jnp.bfloat16), "shard", scatter_dimension=0, tiled=True
        ).astype(jnp.float32),
    )
    total_grads = (
        lax.psum(shard_grads[0].astype(jnp.bfloat16), "replica").astype(jnp.float32),
        lax.psum(shard_grads[1].astype(jnp.bfloat16), "replica").astype(jnp.float32),
        lax.psum(shard_grads[2].astype(jnp.bfloat16), "replica").astype(jnp.float32),
        lax.psum(shard_grads[3].astype(jnp.bfloat16), "replica").astype(jnp.float32),
        lax.psum(shard_grads[4].astype(jnp.bfloat16), "replica").astype(jnp.float32),
        lax.psum(shard_grads[5].astype(jnp.bfloat16), "replica").astype(jnp.float32),
        lax.psum(shard_grads[6].astype(jnp.bfloat16), "replica").astype(jnp.float32),
        lax.psum(shard_grads[7].astype(jnp.bfloat16), "replica").astype(jnp.float32),
        lax.psum(shard_grads[8].astype(jnp.bfloat16), "replica").astype(jnp.float32),
        lax.psum(shard_grads[9].astype(jnp.bfloat16), "replica").astype(jnp.float32),
        lax.psum(shard_grads[10].astype(jnp.bfloat16), "replica").astype(jnp.float32),
        lax.psum(shard_grads[11].astype(jnp.bfloat16), "replica").astype(jnp.float32),
    )
    return (output, d_hidden) + tuple(total_grads)


PLANE = 8
LINE = 4
CHIPS = 4
MESH = pl.DeviceIdType.MESH
VMEM = pltpu.VMEM
ANY = pl.ANY
f32 = jnp.float32
bf16 = jnp.bfloat16


class Wires:
    def __init__(self, send, recv):
        self.send, self.recv, self.used = send, recv, 0
        me = lax.axis_index("shard")
        self.me = me
        self.core = me % 2
        self.chip = me // 2
        self.mate = me + 1 - 2 * self.core
        self.xn = me + 2 - 4 * (self.chip % 2)
        self.yn = me + 4 - 8 * (me // 4)
        self.dn = self.xn + 4 - 8 * (me // 4)
        self.cx = self.xn // 2
        self.cy = self.yn // 2
        self.cd = self.dn // 2

    def copy(self, src, dst, where):
        slot = self.used
        self.used += 1
        return pltpu.make_async_remote_copy(
            src_ref=src,
            dst_ref=dst,
            send_sem=self.send.at[slot],
            recv_sem=self.recv.at[slot],
            device_id=where if isinstance(where, dict) else {"shard": where},
            device_id_type=MESH,
        )

    def start(self, src, dst, where):
        made = self.copy(src, dst, where)
        made.start()
        return made


def plane_others(me):
    return [{"shard": (me + step) % PLANE} for step in range(1, PLANE)]


def dma_sems(count):
    return [pltpu.SemaphoreType.DMA((count,)), pltpu.SemaphoreType.DMA((count,))]


class Gather:
    def __init__(self, wires, block, out, local_sem):
        w = self.w = wires
        self.out = out
        self.half = block.shape[0] // 2
        mine = self.at(w.me)
        self.own = pltpu.make_async_copy(block, mine, local_sem)
        self.own.start()
        self.to_x = w.start(block, mine, w.xn)
        self.to_y = w.start(block, mine, w.yn)
        self.to_mate = w.start(block, mine, w.mate)

    def at(self, who, *rows):
        if rows:
            return self.out.at[who // 2, who % 2, rows[0]]
        return self.out.at[who // 2, who % 2]

    def relay(self):
        w, at, half = self.w, self.at, self.half
        low, high = pl.ds(0, half), pl.ds(half, half)
        self.to_x.wait_recv()
        self.x_on = w.start(at(w.xn, low), at(w.xn, low), w.yn)
        self.x_mate = w.start(at(w.xn), at(w.xn), w.mate)
        self.to_y.wait_recv()
        self.y_on = w.start(at(w.yn, high), at(w.yn, high), w.xn)
        self.y_mate = w.start(at(w.yn), at(w.yn), w.mate)

    def finish(self):
        w, at, half = self.w, self.at, self.half
        low, high = pl.ds(0, half), pl.ds(half, half)
        self.x_on.wait_recv()
        self.d_low = w.start(at(w.dn, low), at(w.dn, low), w.mate)
        self.y_on.wait_recv()
        self.d_high = w.start(at(w.dn, high), at(w.dn, high), w.mate)

    def done(self):
        for made in (self.to_mate, self.x_mate, self.y_mate, self.d_low, self.d_high):
            made.wait_recv()
        for made in (
            self.to_x,
            self.to_y,
            self.to_mate,
            self.x_on,
            self.x_mate,
            self.y_on,
            self.y_mate,
            self.d_low,
            self.d_high,
        ):
            made.wait_send()
        self.own.wait()


SPAN = 512
AHEAD = 3
BAND = 32


def dot(left, right, left_dim, right_dim):
    return lax.dot_general(
        left, right, (((left_dim,), (right_dim,)), ((), ())), preferred_element_type=f32
    )


def turn(block):
    return block.astype(f32).T


def allowed_pairs(segk, segq):
    return jnp.concatenate([segk] * (segq.shape[1] // 128), axis=1) == segq


def upper(block):
    return jnp.concatenate([block, jnp.zeros_like(block)], axis=0)


def lower(block):
    return jnp.concatenate([jnp.zeros_like(block), block], axis=0)


def attend(query, kv_ref, vt_ref, segk_ref, segq, hd):
    heads, keys = kv_ref.shape[:2]
    rows = query.shape[1]
    wide = [upper(query[head * hd : (head + 1) * hd]) for head in range(heads)]

    def step(index, state):
        at = pl.ds(pl.multiple_of(index * SPAN, SPAN), SPAN)
        allowed = allowed_pairs(segk_ref[at, :], segq)
        scores = [
            jnp.where(allowed, dot(kv_ref[head, at, :], wide[head], 1, 0), masked_value)
            for head in range(heads)
        ]
        made = []
        for head in range(heads):
            top, total, acc = state[head]
            new = jnp.maximum(top, jnp.max(scores[head], axis=0, keepdims=True))
            weights = jnp.exp(scores[head] - new)
            factor = jnp.exp(top - new)
            made.append(
                (
                    new,
                    total * factor + jnp.sum(weights, axis=0, keepdims=True),
                    acc * factor + dot(vt_ref[head * hd : (head + 1) * hd, at], weights.astype(bf16), 1, 0),
                )
            )
        return tuple(made)

    zero = tuple(
        (
            jnp.full((1, rows), 0.5 * masked_value, f32),
            jnp.zeros((1, rows), f32),
            jnp.zeros((hd, rows), f32),
        )
        for _ in range(heads)
    )
    state = lax.fori_loop(0, keys // SPAN, step, zero)
    return (
        jnp.concatenate([acc / total for _, total, acc in state], axis=0),
        jnp.concatenate([top + jnp.log(total) for top, total, _ in state], axis=0),
    )


def attend_back(qt, dt, log, delta, kv_ref, kt_ref, segk_ref, segq, dkv_ref, start, stop, hd):
    heads = kv_ref.shape[0]
    rows = qt.shape[1]
    part = [slice(head * hd, (head + 1) * hd) for head in range(heads)]
    wide_q = [upper(qt[one]) for one in part]
    wide_d = [lower(dt[one]) for one in part]

    def step(index, state):
        at = pl.ds(pl.multiple_of(index * SPAN, SPAN), SPAN)
        allowed = allowed_pairs(segk_ref[at, :], segq)
        low = []
        for head in range(heads):
            both = kv_ref[head, at, :]
            scores = dot(both, wide_q[head], 1, 0)
            d_prob = dot(both, wide_d[head], 1, 0)
            probs = jnp.where(allowed, jnp.exp(scores - log[head : head + 1]), 0.0)
            low.append((probs.astype(bf16), (probs * (d_prob - delta[head])).astype(bf16)))
        made = [
            state[head] + dot(kt_ref[part[head], at], low[head][1], 1, 0) for head in range(heads)
        ]
        dkv_ref[at, :] += jnp.concatenate(
            [dot(low[head][1], qt[part[head]], 1, 1) for head in range(heads)]
            + [dot(low[head][0], dt[part[head]], 1, 1) for head in range(heads)],
            axis=1,
        )
        return tuple(made)

    zero = tuple(jnp.zeros((hd, rows), f32) for _ in range(heads))
    return jnp.concatenate(lax.fori_loop(start, stop, step, zero), axis=0)


def add_into(dst, other, out=None):
    out = dst if out is None else out
    lead = dst.shape[0] if len(dst.shape) == 3 else 0
    rows = dst.shape[-2]

    def go(index, carry):
        if lead:
            at = (index // (rows // 16), pl.ds(pl.multiple_of((index % (rows // 16)) * 16, 16), 16))
        else:
            at = (pl.ds(pl.multiple_of(index * 16, 16), 16),)
        out[at] = (dst[at].astype(f32) + other[at].astype(f32)).astype(out.dtype)
        return carry

    lax.fori_loop(0, max(lead, 1) * (rows // 16), go, 0)


class Reduce:
    def __init__(self, wires, full, pair, land, pick):
        self.w, self.full, self.pair, self.land = wires, full, pair, land
        self.half = pair.shape[1] // 2
        self.pick = pick
        if full is not None:
            self.meet = wires.copy(pick(full, 1 - wires.core), pair, wires.mate)

    def first(self):
        w, pair, land = self.w, self.pair, self.land
        low, high = pl.ds(0, self.half), pl.ds(self.half, self.half)
        if self.full is not None:
            self.meet.wait_recv()
            add_into(pair, self.pick(self.full, w.core))
        self.x0 = w.start(pair.at[w.cd, low], land.at[1], w.xn)
        self.y0 = w.start(pair.at[w.cd, high], land.at[3], w.yn)
        self.x1 = w.start(pair.at[w.cx, low], land.at[0], w.xn)
        self.y1 = w.start(pair.at[w.cy, high], land.at[2], w.yn)

    def second(self):
        w, pair, land = self.w, self.pair, self.land
        low, high = pl.ds(0, self.half), pl.ds(self.half, self.half)
        self.x0.wait_recv()
        add_into(pair.at[w.cy, low], land.at[1])
        self.y2 = w.start(pair.at[w.cy, low], land.at[4], w.yn)
        self.y0.wait_recv()
        add_into(pair.at[w.cx, high], land.at[3])
        self.x2 = w.start(pair.at[w.cx, high], land.at[5], w.xn)
        self.x1.wait_recv()
        add_into(pair.at[w.chip, low], land.at[0])
        self.y1.wait_recv()
        add_into(pair.at[w.chip, high], land.at[2])

    def third(self, out):
        w, pair, land = self.w, self.pair, self.land
        low, high = pl.ds(0, self.half), pl.ds(self.half, self.half)
        self.y2.wait_recv()
        add_into(pair.at[w.chip, low], land.at[4], out.at[low])
        self.x2.wait_recv()
        add_into(pair.at[w.chip, high], land.at[5], out.at[high])

    def done(self):
        made = [self.x0, self.x1, self.y0, self.y1, self.x2, self.y2]
        if self.full is not None:
            made.append(self.meet)
        for one in made:
            one.wait_send()


class Line:
    def __init__(self, wires, z, block, land, out):
        self.w, self.z, self.block, self.land, self.out = wires, z, block, land, out
        self.edge = (z == 0) | (z == LINE - 1)
        self.inner = {"replica": 1 + z // 2}
        self.outer = {"replica": 3 * (z // 2)}
        self.across = {"replica": 2 - z // 2}
        self.up = wires.copy(block, land.at[0], self.inner)
        self.over = wires.copy(block, land.at[1], {"replica": 3 - z})
        self.back = wires.copy(out, out, self.outer)

    def first(self):
        @pl.when(self.edge)
        def _():
            self.up.start()

    def second(self):
        @pl.when(jnp.logical_not(self.edge))
        def _():
            self.up.wait_recv()
            add_into(self.block, self.land.at[0])
            self.over.start()

    def third(self):
        @pl.when(jnp.logical_not(self.edge))
        def _():
            self.over.wait_recv()
            add_into(self.block, self.land.at[1], self.out)
            self.back.start()

    def done(self):
        @pl.when(self.edge)
        def _():
            self.up.wait_send()
            self.back.wait_recv()

        @pl.when(jnp.logical_not(self.edge))
        def _():
            self.over.wait_send()
            self.back.wait_send()


def each(rows, block, step, init):
    def go(index, carry):
        return step(pl.ds(pl.multiple_of(index * block, block), block), carry)

    return lax.fori_loop(0, rows // block, go, init)


def fold_rows(block):
    return jnp.sum(block.reshape(block.shape[0] // 8, 8, block.shape[1]), axis=0)


def settle(block):
    return jnp.sum(block, axis=0, keepdims=True)


def vector(small, row, part):
    return jnp.concatenate(
        [small[source, row : row + 1, :part].astype(f32) for source in range(PLANE)], axis=1
    )


def put_vector(stack, row, value, part):
    for source in range(PLANE):
        stack[source, row : row + 1, :part] = value[:, source * part : (source + 1) * part]


def moments(block):
    mean_value = jnp.mean(block, axis=-1, keepdims=True)
    centered = block - mean_value
    scale = lax.rsqrt(jnp.mean(centered * centered, axis=-1, keepdims=True) + norm_epsilon)
    return centered * scale, scale


def norm_back(grad, gain, unit, scale):
    scaled = grad * gain
    return (
        scaled
        - jnp.mean(scaled, axis=-1, keepdims=True)
        - unit * jnp.mean(scaled * unit, axis=-1, keepdims=True)
    ) * scale


def layer_kernel(
    hid,
    wq,
    small,
    wo,
    wi,
    wb,
    cot,
    out_o,
    dq_o,
    db_o,
    di_o,
    do_o,
    dh_o,
    small_o,
    wo_s,
    wi_s,
    wb_s,
    names_s,
    wq_s,
    wq_a,
    hid_s,
    hidt,
    qt,
    kv_s,
    kt,
    vt,
    segk,
    segq,
    ctx32,
    log,
    ctx_s,
    ctxt,
    acc_s,
    unit_s,
    scale_s,
    low_s,
    lowt_s,
    act_s,
    slope_s,
    wide_s,
    grad_s,
    resid_s,
    dctx_s,
    dkv_a,
    dqkv_s,
    gq_s,
    tiny_s,
    q_pair,
    q_all,
    pair,
    land,
    dh_land,
    part_s,
    s_land,
    s_sum,
    zq_land,
    z_land,
    zs_land,
    send,
    recv,
    loc,
    *,
    hd,
):
    w = Wires(send, recv)
    z = lax.axis_index("replica")
    me, core = w.me, w.core
    tok, width = hid.shape
    wide = width // CHIPS
    heads = wide // hd
    ff = wi.shape[1]
    part = width // PLANE
    fold = ff // width
    rows_in = ff // PLANE // 128
    seg_row = 8 + rows_in

    barrier = pltpu.get_barrier_semaphore()
    for other in plane_others(me):
        pl.semaphore_signal(barrier, inc=1, device_id=other, device_id_type=MESH)
    edge = (z == 0) | (z == LINE - 1)

    @pl.when(edge)
    def _():
        pl.semaphore_signal(barrier, inc=1, device_id={"replica": 1 + z // 2}, device_id_type=MESH)

    @pl.when(jnp.logical_not(edge))
    def _():
        pl.semaphore_signal(barrier, inc=1, device_id={"replica": 3 * (z // 2)}, device_id_type=MESH)
        pl.semaphore_signal(barrier, inc=1, device_id={"replica": 3 - z}, device_id_type=MESH)

    for chip in range(CHIPS):
        for place, section in enumerate((1, 2, 0)):
            start = section * width + chip * wide
            wq_s[chip, :, place * wide : (place + 1) * wide] = wq[:, start : start + wide]

    @pl.when(edge)
    def _():
        pl.semaphore_wait(barrier, PLANE)

    @pl.when(jnp.logical_not(edge))
    def _():
        pl.semaphore_wait(barrier, PLANE + 1)

    names_s[me] = small[...]
    first = Gather(w, hid, hid_s, loc.at[0])
    wq_a[me] = wq_s[w.chip]
    q_mate = w.start(wq_s.at[w.chip], wq_a.at[me], w.mate)
    q_d = w.start(wq_s.at[w.cd], wq_a.at[me], w.dn)
    q_x = w.start(wq_s.at[w.cx], wq_a.at[me], w.xn)
    q_y = w.start(wq_s.at[w.cy], wq_a.at[me], w.yn)
    smalls = [w.start(small, names_s.at[me], (me + step) % PLANE) for step in range(1, PLANE)]
    first.relay()
    q_on = []
    for came, source in ((q_x, w.xn), (q_y, w.yn), (q_d, w.dn)):
        came.wait_recv()
        q_on.append(w.start(wq_a.at[source], wq_a.at[source], w.mate))
    rest = [
        Gather(w, block, out, loc.at[1 + slot])
        for slot, (block, out) in enumerate(((wo, wo_s), (wi, wi_s), (wb, wb_s)))
    ]
    for made in smalls:
        made.wait_recv()
    for source in range(PLANE):
        ids = names_s[source].astype(f32)[seg_row : seg_row + tok // 128]
        segq[source] = jnp.concatenate([ids[one : one + 1] for one in range(tok // 128)], axis=1)
        for one in range(tok // 128):
            at = source * tok + one * 128
            segk[at : at + 128, :] = jnp.broadcast_to(ids[one : one + 1], (128, 128)).T
    first.finish()
    for made in [q_mate] + q_on:
        made.wait_recv()
    first.done()

    names = [names_s[2 * w.chip + side].astype(f32).T for side in range(2)]
    bias_q = jnp.concatenate([one[:part, 0:1] for one in names], axis=0)
    bias_v = jnp.concatenate([one[:part, 1:2] for one in names], axis=0)

    def project(index, carry):
        for mine in (True, False):
            side = core if mine else 1 - core
            block = hid_s[index, side]
            weight = wq_a[...].reshape(width, 3 * wide)
            rows = pl.ds(pl.multiple_of((2 * index + side) * tok, tok), tok)
            kv = dot(block, weight if mine else weight[:, : 2 * wide], 1, 0)
            kvt = kv.T
            low_v = (kvt[wide : 2 * wide] + bias_v).astype(bf16)
            kt[:, rows] = kvt[:wide].astype(bf16)
            vt[:, rows] = low_v
            back = turn(low_v)
            for head in range(heads):
                cols = slice(head * hd, (head + 1) * hd)
                kv_s[head, rows, :] = jnp.concatenate([kv[:, cols], back[:, cols]], axis=1).astype(bf16)
            if mine:
                query = kvt[2 * wide :] + bias_q
                qt[index] = (query.astype(bf16).astype(f32) * scale_factor).astype(bf16)
                hidt[index] = turn(block).astype(bf16)
        return carry

    lax.fori_loop(0, CHIPS, project, 0)
    rest[0].relay()

    def one_block(turn_no, carry):
        index = (
            (turn_no == 0) * w.cd + (turn_no == 1) * w.cx + (turn_no == 2) * w.cy + (turn_no == 3) * w.chip
        )
        context, logs = attend(qt[index], kv_s, vt, segk, segq[2 * index + core], hd)
        ctx32[index] = context
        ctx_s[index] = context.astype(bf16)
        log[index] = logs
        return carry

    lax.fori_loop(0, 2, one_block, 0)
    c_d = w.start(ctx_s.at[w.cd], ctxt.at[w.chip], w.dn)
    c_x = w.start(ctx_s.at[w.cx], ctxt.at[w.chip], w.xn)
    rest[1].relay()
    rest[0].finish()
    lax.fori_loop(2, 4, one_block, 0)
    c_y = w.start(ctx_s.at[w.cy], ctxt.at[w.chip], w.yn)
    ctxt[w.chip] = ctx_s[w.chip]
    rest[1].finish()
    rest[2].relay()
    rest[0].done()
    for made in (c_d, c_x, c_y):
        made.wait()

    wo_v = wo_s[...].reshape(width, width)
    bo, g1, s1, bb, g2, s2 = (vector(names_s, row, part) for row in range(2, 8))
    tiny_s[...] = jnp.zeros_like(tiny_s)
    acc_s[...] = dot(turn(ctxt[...].reshape(width, tok)).astype(bf16), wo_v, 1, 0)

    def open_one(at, carry):
        unit, scale = moments(hid[at, :].astype(f32) + acc_s[at, :] + bo)
        unit_s[at, :] = unit
        scale_s[at, :] = jnp.broadcast_to(scale, (BAND, 128))
        normed = unit * g1 + s1
        low_s[at, :] = normed.astype(bf16)
        acc_s[at, :] = normed + bb
        return carry

    each(tok, BAND, open_one, 0)
    lowt_s[...] = turn(low_s[...]).astype(bf16)
    rest[1].done()

    def up(chunk, carry):
        cols = pl.ds(pl.multiple_of(chunk * width, width), width)
        bias = jnp.concatenate(
            [
                names_s[2 * chunk + side, 8 + row : 9 + row, :].astype(f32)
                for side in range(2)
                for row in range(rows_in)
            ],
            axis=1,
        )
        wide_s[...] = dot(low_s[...], wi_s[:, :, :, cols].reshape(width, width), 1, 0)

        def gelu(at, carry):
            pre = wide_s[at, :] + bias
            phi = 0.5 * (1.0 + lax.erf(pre * math.sqrt(0.5)))
            act_s[chunk, at, :] = (pre * phi).astype(bf16)
            slope_s[chunk, at, :] = phi + pre * (
                jnp.exp(-0.5 * pre * pre) * (1.0 / math.sqrt(2.0 * math.pi))
            )
            return carry

        each(tok, BAND, gelu, 0)
        return carry

    lax.fori_loop(0, fold, up, 0)
    rest[2].finish()
    rest[2].done()

    def join_back(chunk, carry):
        acc_s[...] += dot(act_s[chunk], wb_s[chunk].reshape(width, width), 1, 0)
        return carry

    lax.fori_loop(0, fold, join_back, 0)

    zero = jnp.zeros((8, width), f32)

    def close(at, sums):
        unit, scale = moments(acc_s[at, :])
        out_o[at, :] = (unit * g2 + s2).astype(bf16)
        grad = cot[at, :]
        d_resid = norm_back(grad, g2, unit, scale)
        acc_s[at, :] = d_resid
        grad_s[at, :] = d_resid.astype(bf16)
        return (sums[0] + fold_rows(d_resid), sums[1] + fold_rows(grad * unit), sums[2] + fold_rows(grad))

    sums = each(tok, BAND, close, (zero, zero, zero))
    for row, value in zip((5, 6, 7), sums):
        put_vector(tiny_s, row, settle(value), part)

    def down(chunk, carry):
        grad = grad_s[...]
        wide_s[...] = dot(grad, wb_s[chunk].reshape(width, width), 1, 1)
        wb_s[chunk] = (
            dot(turn(act_s[chunk]).astype(bf16), grad, 1, 0).astype(bf16).reshape(2, ff // PLANE, width)
        )

        def through(at, sums):
            d_pre = wide_s[at, :] * slope_s[chunk, at, :]
            act_s[chunk, at, :] = d_pre.astype(bf16)
            return sums + fold_rows(d_pre)

        total = settle(each(tok, BAND, through, zero))
        for side in range(2):
            for row in range(rows_in):
                start = (side * rows_in + row) * 128
                tiny_s[2 * chunk + side, 8 + row : 9 + row, :] = total[:, start : start + 128]
        return carry

    lax.fori_loop(0, fold, down, 0)

    picks = []
    for slot in range(wb.shape[0] // part):
        at = pl.ds(slot * part, part)
        picks.append((wb_s, lambda ref, core, at=at: ref.at[:, core, at], db_o.at[at]))
    for slot in range(fold):
        at = pl.ds(slot * width, width)
        picks.append((wi_s, lambda ref, core, at=at: ref.at[:, core, :, at], di_o.at[:, at]))
    picks.append((wo_s, lambda ref, core: ref.at[:, core], do_o))
    count = len(picks)
    chunks = [
        Reduce(w, full, pair.at[slot], land.at[slot], pick)
        for slot, (full, pick, _) in enumerate(picks)
    ]
    lines = [
        Line(w, z, part_s.at[slot], z_land.at[slot], out) for slot, (_, _, out) in enumerate(picks)
    ]
    for one in chunks[:AHEAD]:
        one.meet.start()
    ticks = 0

    def tick():
        nonlocal ticks
        now = ticks
        ticks += 1
        if now + AHEAD < count:
            chunks[now + AHEAD].meet.start()
        if now < count:
            chunks[now].first()
        if 0 <= now - 1 < count:
            chunks[now - 1].second()
        if 0 <= now - 2 < count:
            chunks[now - 2].third(part_s.at[now - 2])
            lines[now - 2].first()
        if 0 <= now - 3 < count:
            lines[now - 3].second()
        if 0 <= now - 4 < count:
            lines[now - 4].third()

    for chunk in range(fold):
        cols = slice(chunk * width, (chunk + 1) * width)
        d_low = act_s[chunk]
        acc_s[...] += dot(d_low, wi_s[:, :, :, cols].reshape(width, width), 1, 1)
        wi_s[:, :, :, cols] = dot(lowt_s[...], d_low, 1, 0).astype(bf16).reshape(CHIPS, 2, part, width)
        tick()

    def finish(at, sums):
        unit = unit_s[at, :]
        grad = acc_s[at, :]
        d_resid = norm_back(grad, g1, unit, scale_s[at, 0:1])
        resid_s[at, :] = d_resid
        grad_s[at, :] = d_resid.astype(bf16)
        return (sums[0] + fold_rows(d_resid), sums[1] + fold_rows(grad * unit), sums[2] + fold_rows(grad))

    sums = each(tok, BAND, finish, (zero, zero, zero))
    grad = grad_s[...]
    ctx_s[...] = dot(wo_s[...].reshape(width, width), grad, 1, 1).astype(bf16).reshape(CHIPS, wide, tok)
    dctx_made = [
        w.start(ctx_s.at[chip], dctx_s.at[w.chip], who)
        for chip, who in ((w.cx, w.xn), (w.cy, w.yn), (w.cd, w.dn))
    ]
    dctx_s[w.chip] = ctx_s[w.chip]
    wo_s[...] = dot(ctxt[...].reshape(width, tok), grad, 1, 0).astype(bf16).reshape(CHIPS, 2, part, width)
    for row, value in zip((2, 3, 4), sums):
        put_vector(tiny_s, row, settle(value), part)
    tick()

    dq_s = slope_s.at[:, 0:wide, 0:tok]
    dkv_a[...] = jnp.zeros_like(dkv_a)
    steps = PLANE * tok // SPAN
    for turn_no, index in enumerate((w.chip, w.cx, w.cy, w.cd)):
        if turn_no:
            dctx_made[turn_no - 1].wait_recv()
        dt = dctx_s[index]
        product = dt.astype(f32) * ctx32[index]
        delta = [
            jnp.sum(product[head * hd : (head + 1) * hd], axis=0, keepdims=True) for head in range(heads)
        ]
        dq_s[index] = attend_back(
            qt[index], dt, log[index], delta, kv_s, kt, segk, segq[2 * index + core], dkv_a, 0, steps, hd
        )
        tick()

    dkv_s = hid_s.at[:, 0, :, 0 : 2 * wide]
    dkv_land = hid_s.at[:, 1, :, 0 : 2 * wide]

    def away(index, carry):
        at = pl.ds(pl.multiple_of((2 * index + 1 - core) * tok, tok), tok)
        dkv_s[index] = dkv_a[at, :].astype(bf16)
        return carry

    lax.fori_loop(0, CHIPS, away, 0)
    meet = w.start(dkv_s, dkv_land, w.mate)
    tick()
    meet.wait_recv()

    def join(index, sums):
        at = pl.ds(pl.multiple_of((2 * index + core) * tok, tok), tok)
        dkv = dkv_a[at, :] + dkv_land[index].astype(f32)
        dqkv = jnp.concatenate([dkv, (dq_s[index] * scale_factor).T], axis=1)
        dqkv_s[index] = dqkv.astype(bf16)
        return sums + jnp.sum(dqkv, axis=0, keepdims=True)

    sums = lax.fori_loop(0, CHIPS, join, jnp.zeros((1, 3 * wide), f32))
    for half in range(2):
        at = slice(half * width // 2, (half + 1) * width // 2)
        total = sum(dot(hidt[index, at, :], dqkv_s[index], 1, 0) for index in range(CHIPS))
        gq_s[2 * half : 2 * half + 2] = total.astype(bf16).reshape(2, 2, part, 3 * wide)
    q_meet = w.start(gq_s.at[:, 1 - core], q_pair, w.mate)
    for side in range(2):
        slot = 2 * w.chip + side
        tiny_s[slot, 0:1, :part] = sums[:, 2 * wide + side * part : 2 * wide + (side + 1) * part]
        tiny_s[slot, 1:2, :part] = sums[:, wide + side * part : wide + (side + 1) * part]
    tinies = [
        w.start(tiny_s.at[(me + step) % PLANE], s_land.at[me], (me + step) % PLANE)
        for step in range(1, PLANE)
    ]
    s_land[me] = tiny_s[me]
    dh_s = act_s
    hidden = Reduce(w, None, dh_s, dh_land, None)

    q_meet.wait_recv()
    add_into(q_pair, gq_s.at[:, core])
    q_made = [
        w.start(q_pair.at[chip], q_all.at[w.chip], who)
        for chip, who in ((w.cx, w.xn), (w.cy, w.yn), (w.cd, w.dn))
    ]
    q_all[w.chip] = q_pair[w.chip]
    q_lines = [
        Line(w, z, q_all.at[chip], zq_land.at[chip], dq_o.at[chip]) for chip in (w.chip, w.cx, w.cy, w.cd)
    ]
    q_lines[0].first()

    def input_grad(index, carry):
        dh_s[index] = dot(dqkv_s[index], wq_a[...].reshape(width, 3 * wide), 1, 1).astype(bf16)
        return carry

    lax.fori_loop(0, CHIPS, input_grad, 0)
    hidden.first()
    tick()
    for one in tinies:
        one.wait_recv()
    s_sum[...] = jnp.sum(s_land[...], axis=0)
    s_line = Line(w, z, s_sum, zs_land, small_o)
    s_line.first()
    for slot in (1, 2, 3):
        q_made[slot - 1].wait_recv()
        q_lines[slot].first()
        q_lines[slot - 1].second()
        if slot > 1:
            q_lines[slot - 2].third()
    tick()
    s_line.second()
    q_lines[3].second()
    q_lines[2].third()
    hidden.second()
    while ticks < count + 4:
        tick()
    s_line.third()
    q_lines[3].third()
    hidden.third(dh_o)
    for one in [q_mate, q_x, q_y, q_d] + q_on + smalls + tinies + q_made + [q_meet, meet] + dctx_made:
        one.wait_send()
    for one in chunks + [hidden]:
        one.done()
    for one in lines + q_lines + [s_line]:
        one.done()
    dh_o[...] = (resid_s[...] + dh_o[...].astype(f32)).astype(dh_o.dtype)


def layer_all(hid, wq, small, wo, wi, wb, cot, hd):
    tok, width = hid.shape
    wide = width // CHIPS
    part = wq.shape[0]
    ff = wi.shape[1]
    fold = ff // width
    seq = PLANE * tok
    rows, cols = wo.shape
    count = wb.shape[0] // rows + fold + 1
    q_block = (CHIPS, part, 3 * wide)
    shape = jax.ShapeDtypeStruct
    outs = [
        shape((tok, width), bf16),
        shape(q_block, bf16),
        shape(wb.shape, bf16),
        shape(wi.shape, bf16),
        shape(wo.shape, bf16),
        shape((tok, width), f32),
        shape((16, 128), f32),
    ]
    pairs = (CHIPS, 2)
    heads_block = (CHIPS, wide, tok)
    scratch = [
        VMEM(pairs + wo.shape, bf16),
        VMEM(pairs + wi.shape, bf16),
        VMEM(pairs + wb.shape, bf16),
        VMEM((PLANE, 16, 128), bf16),
        VMEM(q_block, bf16),
        VMEM((PLANE, part, 3 * wide), bf16),
        VMEM(pairs + (tok, width), bf16),
        VMEM((CHIPS, width, tok), bf16),
        VMEM(heads_block, bf16),
        VMEM((wide // hd, seq, 2 * hd), bf16),
        VMEM((wide, seq), bf16),
        VMEM((wide, seq), bf16),
        VMEM((seq, 128), f32),
        VMEM((PLANE, 1, tok), f32),
        VMEM(heads_block, f32),
        VMEM((CHIPS, wide // hd, tok), f32),
        VMEM(heads_block, bf16),
        VMEM(heads_block, bf16),
        VMEM((tok, width), f32),
        VMEM((tok, width), f32),
        VMEM((tok, 128), f32),
        VMEM((tok, width), bf16),
        VMEM((width, tok), bf16),
        VMEM((fold, tok, width), bf16),
        VMEM((fold, tok, width), f32),
        VMEM((tok, width), f32),
        VMEM((tok, width), bf16),
        VMEM((tok, width), f32),
        VMEM(heads_block, bf16),
        VMEM((seq, 2 * wide), f32),
        VMEM((CHIPS, tok, 3 * wide), bf16),
        VMEM(pairs + (part, 3 * wide), bf16),
        VMEM((PLANE, 16, 128), f32),
        VMEM(q_block, bf16),
        VMEM(q_block, bf16),
        VMEM((count, CHIPS, rows, cols), bf16),
        VMEM((count, 6, rows // 2, cols), bf16),
        VMEM((6, tok // 2, width), bf16),
        VMEM((count, rows, cols), bf16),
        VMEM((PLANE, 16, 128), f32),
        VMEM((16, 128), f32),
        VMEM((CHIPS, 2) + q_block[1:], bf16),
        VMEM((count, 2, rows, cols), bf16),
        VMEM((2, 16, 128), f32),
    ]
    return pl.pallas_call(
        functools.partial(layer_kernel, hd=hd),
        out_shape=outs,
        in_specs=[pl.BlockSpec(memory_space=VMEM)] * 7,
        out_specs=[pl.BlockSpec(memory_space=VMEM)] * 7,
        scratch_shapes=scratch + dma_sems(count * 10 + 100) + [pltpu.SemaphoreType.DMA((4,))],
        compiler_params=pltpu.CompilerParams(
            collective_id=1, has_side_effects=True, vmem_limit_bytes=67043328
        ),
        name="layer_all",
    )(hid, wq, small, wo, wi, wb, cot)


def finish_kernel(dq, db, di, do, dh, out, q_o, b_o, i_o, o_o, h_o, out_o):
    wide = dq.shape[2] // 3
    width = dh.shape[1]
    for chip in range(CHIPS):
        for place, section in enumerate((1, 2, 0)):
            start = section * width + chip * wide
            q_o[:, start : start + wide] = dq[chip, :, place * wide : (place + 1) * wide].astype(f32)
    b_o[...] = db[...].astype(f32)
    i_o[...] = di[...].astype(f32)
    o_o[...] = do[...].astype(f32)
    h_o[...] = dh[...]
    out_o[...] = out[...]


def finish_all(dq, db, di, do, dh, out):
    part, wide = dq.shape[1:]
    shape = jax.ShapeDtypeStruct
    outs = [shape((part, CHIPS * wide), f32)] + [shape(one.shape, f32) for one in (db, di, do, dh)]
    outs.append(shape(out.shape, out.dtype))
    return pl.pallas_call(
        finish_kernel,
        out_shape=outs,
        in_specs=[pl.BlockSpec(memory_space=VMEM)] * 6,
        out_specs=[pl.BlockSpec(memory_space=VMEM)] * 6,
        compiler_params=pltpu.CompilerParams(vmem_limit_bytes=32 << 20),
        name="finish_all",
    )(dq, db, di, do, dh, out)


def fast_body(
    hidden,
    segment_ids,
    w_qkv,
    b_qv,
    w_out,
    b_out,
    gain1,
    shift1,
    w_in,
    b_in,
    w_back,
    b_back,
    gain2,
    shift2,
    cotangent,
):
    tok, width = hidden.shape
    hd = width // HEADS
    part = w_qkv.shape[0]
    ff = w_in.shape[1]
    lines = b_in.shape[0] // 128
    narrow = jnp.concatenate(
        [b_qv] + [one[None] for one in (b_out, gain1, shift1, b_back, gain2, shift2)], axis=0
    )
    small = jnp.concatenate(
        [
            jnp.pad(narrow, ((0, 0), (0, 128 - part))),
            b_in.reshape(lines, 128),
            segment_ids.astype(bf16).reshape(tok // 128, 128),
            jnp.zeros((8 - lines - tok // 128, 128), bf16),
        ],
        axis=0,
    )
    output, dq, db, di, do, dh, tiny = layer_all(
        hidden, w_qkv, small, w_out, w_in, w_back, cotangent, hd
    )
    g_qkv, g_back, g_in, g_out, d_hidden, output = finish_all(dq, db, di, do, dh, output)
    return (
        output,
        d_hidden,
        g_qkv,
        tiny[0:2, :part],
        g_out,
        tiny[2, :part],
        tiny[3, :part],
        tiny[4, :part],
        g_in,
        tiny[8 : 8 + lines].reshape(ff // PLANE),
        g_back,
        tiny[5, :part],
        tiny[6, :part],
        tiny[7, :part],
    )


def solution(mesh):
    in_specs = (
        P(("replica", "shard"), None),
        P(("replica", "shard")),
        P("shard", None),
        P(None, "shard"),
        P("shard", None),
        P("shard"),
        P("shard"),
        P("shard"),
        P("shard", None),
        P("shard"),
        P("shard", None),
        P("shard"),
        P("shard"),
        P("shard"),
        P(("replica", "shard"), None),
    )
    out_specs = (
        P(("replica", "shard"), None),
        P(("replica", "shard"), None),
        P("shard", None),
        P(None, "shard"),
        P("shard", None),
        P("shard"),
        P("shard"),
        P("shard"),
        P("shard", None),
        P("shard"),
        P("shard", None),
        P("shard"),
        P("shard"),
        P("shard"),
    )
    paired = mesh.shape["shard"] == PLANE and mesh.shape["replica"] == LINE
    body = fast_body if paired else plain_body
    return jax.shard_map(body, mesh=mesh, in_specs=in_specs, out_specs=out_specs, check_vma=False)
```

```python
import functools
import math

import jax
import jax.numpy as jnp
from jax import lax
from jax.experimental import pallas as pl
from jax.experimental.pallas import tpu as pltpu
from jax.sharding import PartitionSpec as P

HEADS = 12


scale_factor = 0.125
norm_epsilon = 1e-05
masked_value = -1e30


def normalize(resid, gain, shift):
    mean_value = jnp.mean(resid, axis=-1, keepdims=True)
    centered = resid - mean_value
    variance = jnp.mean(centered * centered, axis=-1, keepdims=True)
    return centered * lax.rsqrt(variance + norm_epsilon) * gain + shift


def gelu_exact(values):
    return jax.nn.gelu(values, approximate=False)


def keep_state(state):
    return state


def block_size(count):
    return math.gcd(count, 512)


def masked_scores(query_heads, key_heads, query_segs, key_segs):
    scores = (
        jnp.einsum("qhd,khd->hqk", query_heads, key_heads, preferred_element_type=jnp.float32)
        * scale_factor
    )
    allowed = query_segs[:, None] == key_segs[None, :]
    return (scores, allowed[None])


def grad_block(
    query_heads, dctx_heads, log_total, delta, query_segs, key_heads, value_heads, key_segs
):
    scores, allowed = masked_scores(query_heads, key_heads, query_segs, key_segs)
    probs = jnp.where(allowed, jnp.exp(scores - log_total[:, :, None]), 0.0)
    d_prob = jnp.einsum("qhd,khd->hqk", dctx_heads, value_heads, preferred_element_type=jnp.float32)
    d_scores = (probs * (d_prob - delta[:, :, None])).astype(jnp.bfloat16)
    return (probs.astype(jnp.bfloat16), d_scores)


def plain_body(
    hidden,
    segment_ids,
    w_qkv,
    b_qv,
    w_out,
    b_out,
    gain1,
    shift1,
    w_in,
    b_in,
    w_back,
    b_back,
    gain2,
    shift2,
    cotangent,
):
    tok_rows, width = hidden.shape
    heads = HEADS
    head_dim = width // heads
    seg_low = segment_ids[0]
    seg_high = segment_ids[-1]
    wq_full, wo_full, bqv_full, bo_full, g1_full, s1_full = (
        lax.all_gather(w_qkv, "shard", axis=0, tiled=True),
        lax.all_gather(w_out, "shard", axis=0, tiled=True),
        lax.all_gather(b_qv, "shard", axis=1, tiled=True),
        lax.all_gather(b_out, "shard", axis=0, tiled=True),
        lax.all_gather(gain1, "shard", axis=0, tiled=True),
        lax.all_gather(shift1, "shard", axis=0, tiled=True),
    )
    qkv = jnp.dot(hidden, wq_full, preferred_element_type=jnp.float32)
    bqv_wide = bqv_full.astype(jnp.float32)
    query = (qkv[:, :width] + bqv_wide[0]).astype(jnp.bfloat16)
    keys = qkv[:, width : 2 * width].astype(jnp.bfloat16)
    values = (qkv[:, 2 * width :] + bqv_wide[1]).astype(jnp.bfloat16)
    query_heads = query.reshape(tok_rows, heads, head_dim)
    key_local = keys.reshape(tok_rows, heads, head_dim)
    value_local = values.reshape(tok_rows, heads, head_dim)
    start_state = (
        jnp.full((heads, tok_rows), masked_value, jnp.float32),
        jnp.zeros((heads, tok_rows), jnp.float32),
        jnp.zeros((tok_rows, heads, head_dim), jnp.float32),
    )
    key_piece = lax.all_gather(keys, "shard", axis=0, tiled=True)
    value_piece = lax.all_gather(values, "shard", axis=0, tiled=True)
    seg_piece = lax.all_gather(segment_ids, "shard", axis=0, tiled=True)
    count = key_piece.shape[0]
    block = block_size(count)

    def forward_step(index, state):
        offset = index * block
        key_heads = lax.dynamic_slice_in_dim(key_piece, offset, block, 0).reshape(
            block, heads, head_dim
        )
        value_heads = lax.dynamic_slice_in_dim(value_piece, offset, block, 0).reshape(
            block, heads, head_dim
        )
        key_segs = lax.dynamic_slice_in_dim(seg_piece, offset, block, 0)

        def forward_update(state):
            running_max, running_sum, accum = state
            scores, allowed = masked_scores(query_heads, key_heads, segment_ids, key_segs)
            new_max = jnp.maximum(
                running_max, jnp.max(jnp.where(allowed, scores, masked_value), axis=-1)
            )
            factor = jnp.exp(running_max - new_max)
            weights = jnp.where(allowed, jnp.exp(scores - new_max[:, :, None]), 0.0)
            running_sum = running_sum * factor + jnp.sum(weights, axis=-1)
            accum = accum * factor.T[:, :, None] + jnp.einsum(
                "hqk,khd->qhd",
                weights.astype(jnp.bfloat16),
                value_heads,
                preferred_element_type=jnp.float32,
            )
            return (new_max, running_sum, accum)

        touches = jnp.logical_and(key_segs[0] <= seg_high, key_segs[-1] >= seg_low)
        return lax.cond(touches, forward_update, keep_state, state)

    running_max, running_sum, accum = lax.fori_loop(0, count // block, forward_step, start_state)
    context32 = accum / running_sum.T[:, :, None]
    log_total = running_max + jnp.log(running_sum)
    context = context32.reshape(tok_rows, width).astype(jnp.bfloat16)
    resid1 = (
        hidden.astype(jnp.float32)
        + jnp.dot(context, wo_full, preferred_element_type=jnp.float32)
        + bo_full.astype(jnp.float32)
    )
    normed1, norm1_pull = jax.vjp(
        normalize, resid1, g1_full.astype(jnp.float32), s1_full.astype(jnp.float32)
    )
    wi_full, bi_full, wb_full, bb_full, g2_full, s2_full = (
        lax.all_gather(w_in, "shard", axis=0, tiled=True),
        lax.all_gather(b_in, "shard", axis=0, tiled=True),
        lax.all_gather(w_back, "shard", axis=0, tiled=True),
        lax.all_gather(b_back, "shard", axis=0, tiled=True),
        lax.all_gather(gain2, "shard", axis=0, tiled=True),
        lax.all_gather(shift2, "shard", axis=0, tiled=True),
    )
    normed1_low = normed1.astype(jnp.bfloat16)
    pre = jnp.dot(normed1_low, wi_full, preferred_element_type=jnp.float32) + bi_full.astype(
        jnp.float32
    )
    act, gelu_pull = jax.vjp(gelu_exact, pre)
    act_low = act.astype(jnp.bfloat16)
    resid2 = (
        normed1
        + jnp.dot(act_low, wb_full, preferred_element_type=jnp.float32)
        + bb_full.astype(jnp.float32)
    )
    out32, norm2_pull = jax.vjp(
        normalize, resid2, g2_full.astype(jnp.float32), s2_full.astype(jnp.float32)
    )
    output = out32.astype(jnp.bfloat16)
    d_resid2, grad_gain2, grad_shift2 = norm2_pull(cotangent)
    d_branch2 = d_resid2.astype(jnp.bfloat16)
    grad_b_back = jnp.sum(d_resid2, axis=0)
    grad_w_back = jnp.einsum("tf,td->fd", act_low, d_branch2, preferred_element_type=jnp.float32)
    d_act = jnp.einsum("td,fd->tf", d_branch2, wb_full, preferred_element_type=jnp.float32)
    (d_pre,) = gelu_pull(d_act)
    grad_b_in = jnp.sum(d_pre, axis=0)
    d_pre_low = d_pre.astype(jnp.bfloat16)
    grad_w_in = jnp.einsum("td,tf->df", normed1_low, d_pre_low, preferred_element_type=jnp.float32)
    d_normed1 = d_resid2 + jnp.einsum(
        "tf,df->td", d_pre_low, wi_full, preferred_element_type=jnp.float32
    )
    d_resid1, grad_gain1, grad_shift1 = norm1_pull(d_normed1)
    grad_b_out = jnp.sum(d_resid1, axis=0)
    d_branch1 = d_resid1.astype(jnp.bfloat16)
    grad_w_out = jnp.einsum("tc,td->cd", context, d_branch1, preferred_element_type=jnp.float32)
    d_context = jnp.einsum(
        "td,cd->tc", d_branch1, wo_full, preferred_element_type=jnp.float32
    ).astype(jnp.bfloat16)
    dctx_heads = d_context.reshape(tok_rows, heads, head_dim)
    delta = jnp.einsum("qhd,qhd->hq", dctx_heads.astype(jnp.float32), context32)
    zero_heads = jnp.zeros((tok_rows, heads, head_dim), jnp.float32)
    query_key_piece = lax.all_gather(keys, "shard", axis=0, tiled=True)
    query_value_piece = lax.all_gather(values, "shard", axis=0, tiled=True)
    query_seg_piece = lax.all_gather(segment_ids, "shard", axis=0, tiled=True)
    count = query_key_piece.shape[0]
    query_block = block_size(count)

    def query_step(index, summed):
        offset = index * query_block
        key_heads = lax.dynamic_slice_in_dim(query_key_piece, offset, query_block, 0).reshape(
            query_block, heads, head_dim
        )
        value_heads = lax.dynamic_slice_in_dim(query_value_piece, offset, query_block, 0).reshape(
            query_block, heads, head_dim
        )
        key_segs = lax.dynamic_slice_in_dim(query_seg_piece, offset, query_block, 0)

        def query_update(summed):
            probs, d_scores = grad_block(
                query_heads,
                dctx_heads,
                log_total,
                delta,
                segment_ids,
                key_heads,
                value_heads,
                key_segs,
            )
            return (
                summed
                + jnp.einsum(
                    "hqk,khd->qhd", d_scores, key_heads, preferred_element_type=jnp.float32
                )
                * scale_factor
            )

        touches = jnp.logical_and(key_segs[0] <= seg_high, key_segs[-1] >= seg_low)
        return lax.cond(touches, query_update, keep_state, summed)

    d_query = lax.fori_loop(0, count // query_block, query_step, zero_heads)
    all_log_total, all_delta = (
        lax.all_gather(log_total, "shard", axis=1, tiled=True),
        lax.all_gather(delta, "shard", axis=1, tiled=True),
    )
    query_piece = lax.all_gather(query, "shard", axis=0, tiled=True)
    dctx_piece = lax.all_gather(d_context, "shard", axis=0, tiled=True)
    key_seg_piece = lax.all_gather(segment_ids, "shard", axis=0, tiled=True)
    count = query_piece.shape[0]
    key_block = block_size(count)

    def key_step(index, state):
        offset = index * key_block
        piece_query = lax.dynamic_slice_in_dim(query_piece, offset, key_block, 0).reshape(
            key_block, heads, head_dim
        )
        piece_dctx = lax.dynamic_slice_in_dim(dctx_piece, offset, key_block, 0).reshape(
            key_block, heads, head_dim
        )
        piece_segs = lax.dynamic_slice_in_dim(key_seg_piece, offset, key_block, 0)
        piece_log = lax.dynamic_slice_in_dim(all_log_total, offset, key_block, 1)
        piece_delta = lax.dynamic_slice_in_dim(all_delta, offset, key_block, 1)

        def key_update(state):
            d_key, d_value = state
            probs, d_scores = grad_block(
                piece_query,
                piece_dctx,
                piece_log,
                piece_delta,
                piece_segs,
                key_local,
                value_local,
                segment_ids,
            )
            d_key = (
                d_key
                + jnp.einsum(
                    "hqk,qhd->khd", d_scores, piece_query, preferred_element_type=jnp.float32
                )
                * scale_factor
            )
            d_value = d_value + jnp.einsum(
                "hqk,qhd->khd", probs, piece_dctx, preferred_element_type=jnp.float32
            )
            return (d_key, d_value)

        touches = jnp.logical_and(piece_segs[0] <= seg_high, piece_segs[-1] >= seg_low)
        return lax.cond(touches, key_update, keep_state, state)

    d_key_heads, d_value_heads = lax.fori_loop(
        0, count // key_block, key_step, (zero_heads, zero_heads)
    )
    d_keys = d_key_heads.reshape(tok_rows, width)
    d_values = d_value_heads.reshape(tok_rows, width)
    d_query = d_query.reshape(tok_rows, width)
    grad_b_qv = jnp.stack([jnp.sum(d_query, axis=0), jnp.sum(d_values, axis=0)], axis=0)
    d_qkv = jnp.concatenate([d_query, d_keys, d_values], axis=1).astype(jnp.bfloat16)
    grad_w_qkv = jnp.einsum("td,te->de", hidden, d_qkv, preferred_element_type=jnp.float32)
    d_hidden = d_resid1 + jnp.einsum(
        "te,de->td", d_qkv, wq_full, preferred_element_type=jnp.float32
    )
    local_grads = (
        grad_w_qkv,
        grad_b_qv,
        grad_w_out,
        grad_b_out,
        grad_gain1,
        grad_shift1,
        grad_w_in,
        grad_b_in,
        grad_w_back,
        grad_b_back,
        grad_gain2,
        grad_shift2,
    )
    shard_grads = (
        lax.psum_scatter(
            local_grads[0].astype(jnp.bfloat16), "shard", scatter_dimension=0, tiled=True
        ).astype(jnp.float32),
        lax.psum_scatter(
            local_grads[1].astype(jnp.bfloat16), "shard", scatter_dimension=1, tiled=True
        ).astype(jnp.float32),
        lax.psum_scatter(
            local_grads[2].astype(jnp.bfloat16), "shard", scatter_dimension=0, tiled=True
        ).astype(jnp.float32),
        lax.psum_scatter(
            local_grads[3].astype(jnp.bfloat16), "shard", scatter_dimension=0, tiled=True
        ).astype(jnp.float32),
        lax.psum_scatter(
            local_grads[4].astype(jnp.bfloat16), "shard", scatter_dimension=0, tiled=True
        ).astype(jnp.float32),
        lax.psum_scatter(
            local_grads[5].astype(jnp.bfloat16), "shard", scatter_dimension=0, tiled=True
        ).astype(jnp.float32),
        lax.psum_scatter(
            local_grads[6].astype(jnp.bfloat16), "shard", scatter_dimension=0, tiled=True
        ).astype(jnp.float32),
        lax.psum_scatter(
            local_grads[7].astype(jnp.bfloat16), "shard", scatter_dimension=0, tiled=True
        ).astype(jnp.float32),
        lax.psum_scatter(
            local_grads[8].astype(jnp.bfloat16), "shard", scatter_dimension=0, tiled=True
        ).astype(jnp.float32),
        lax.psum_scatter(
            local_grads[9].astype(jnp.bfloat16), "shard", scatter_dimension=0, tiled=True
        ).astype(jnp.float32),
        lax.psum_scatter(
            local_grads[10].astype(jnp.bfloat16), "shard", scatter_dimension=0, tiled=True
        ).astype(jnp.float32),
        lax.psum_scatter(
            local_grads[11].astype(jnp.bfloat16), "shard", scatter_dimension=0, tiled=True
        ).astype(jnp.float32),
    )
    total_grads = (
        lax.psum(shard_grads[0].astype(jnp.bfloat16), "replica").astype(jnp.float32),
        lax.psum(shard_grads[1].astype(jnp.bfloat16), "replica").astype(jnp.float32),
        lax.psum(shard_grads[2].astype(jnp.bfloat16), "replica").astype(jnp.float32),
        lax.psum(shard_grads[3].astype(jnp.bfloat16), "replica").astype(jnp.float32),
        lax.psum(shard_grads[4].astype(jnp.bfloat16), "replica").astype(jnp.float32),
        lax.psum(shard_grads[5].astype(jnp.bfloat16), "replica").astype(jnp.float32),
        lax.psum(shard_grads[6].astype(jnp.bfloat16), "replica").astype(jnp.float32),
        lax.psum(shard_grads[7].astype(jnp.bfloat16), "replica").astype(jnp.float32),
        lax.psum(shard_grads[8].astype(jnp.bfloat16), "replica").astype(jnp.float32),
        lax.psum(shard_grads[9].astype(jnp.bfloat16), "replica").astype(jnp.float32),
        lax.psum(shard_grads[10].astype(jnp.bfloat16), "replica").astype(jnp.float32),
        lax.psum(shard_grads[11].astype(jnp.bfloat16), "replica").astype(jnp.float32),
    )
    return (output, d_hidden) + tuple(total_grads)


PLANE = 8
LINE = 4
CHIPS = 4
MESH = pl.DeviceIdType.MESH
VMEM = pltpu.VMEM
ANY = pl.ANY
f32 = jnp.float32
bf16 = jnp.bfloat16


class Wires:
    def __init__(self, send, recv):
        self.send, self.recv, self.used = send, recv, 0
        me = lax.axis_index("shard")
        self.me = me
        self.core = me % 2
        self.chip = me // 2
        self.mate = me + 1 - 2 * self.core
        self.xn = me + 2 - 4 * (self.chip % 2)
        self.yn = me + 4 - 8 * (me // 4)
        self.dn = self.xn + 4 - 8 * (me // 4)
        self.cx = self.xn // 2
        self.cy = self.yn // 2
        self.cd = self.dn // 2

    def copy(self, src, dst, where):
        slot = self.used
        self.used += 1
        return pltpu.make_async_remote_copy(
            src_ref=src,
            dst_ref=dst,
            send_sem=self.send.at[slot],
            recv_sem=self.recv.at[slot],
            device_id=where if isinstance(where, dict) else {"shard": where},
            device_id_type=MESH,
        )

    def start(self, src, dst, where):
        made = self.copy(src, dst, where)
        made.start()
        return made


def plane_others(me):
    return [{"shard": (me + step) % PLANE} for step in range(1, PLANE)]


def dma_sems(count):
    return [pltpu.SemaphoreType.DMA((count,)), pltpu.SemaphoreType.DMA((count,))]


class Gather:
    def __init__(self, wires, out, block=None, far=None):
        self.w, self.out, self.far = wires, out, far
        self.half = out.shape[2] // 2
        self.block = self.at(wires.me) if block is None else block
        self.made = []

    def at(self, who, *rows):
        if rows:
            return self.out.at[who // 2, who % 2, rows[0]]
        return self.out.at[who // 2, who % 2]

    def start(self, where, who, *rows):
        one = self.w.start(self.at(who, *rows), self.at(who, *rows), where)
        self.made.append(one)
        return one

    def pass_on(self, who):
        one = self.start(self.far, who)
        return one

    def begin(self):
        w, mine = self.w, self.at(self.w.me)
        self.to_x = w.start(self.block, mine, w.xn)
        self.to_y = w.start(self.block, mine, w.yn)
        self.to_mate = w.start(self.block, mine, w.mate)
        self.made += [self.to_x, self.to_y, self.to_mate]

    def relay(self):
        w, half = self.w, self.half
        self.to_x.wait_recv()
        self.x_on = self.start(w.yn, w.xn, pl.ds(0, half))
        if self.far is not None:
            self.x_far = self.pass_on(w.xn)
        self.x_mate = self.start(w.mate, w.xn)
        self.to_y.wait_recv()
        self.y_on = self.start(w.xn, w.yn, pl.ds(half, half))
        if self.far is not None:
            self.y_far = self.pass_on(w.yn)
        self.y_mate = self.start(w.mate, w.yn)

    def finish(self):
        w, half = self.w, self.half
        self.x_on.wait_recv()
        self.d_low = self.start(w.mate, w.dn, pl.ds(0, half))
        self.y_on.wait_recv()
        self.d_high = self.start(w.mate, w.dn, pl.ds(half, half))
        if self.far is not None:
            self.d_far = self.pass_on(w.dn)

    def done(self):
        for made in (self.to_mate, self.x_mate, self.y_mate, self.d_low, self.d_high):
            made.wait_recv()
        for made in self.made:
            made.wait_send()


class Passed:
    def __init__(self, wires, out, source):
        self.w, self.source = wires, source
        self.near = Gather(wires, out)
        self.relays = []

    def begin(self):
        w = self.w
        self.to_mate = self.near.start(w.mate, w.me)

    def relay(self):
        self.source.x_far.wait_recv()
        self.relays.append(self.near.start(self.w.mate, self.w.xn))
        self.source.y_far.wait_recv()
        self.relays.append(self.near.start(self.w.mate, self.w.yn))

    def finish(self):
        self.source.d_far.wait_recv()
        self.relays.append(self.near.start(self.w.mate, self.w.dn))

    def done(self):
        for made in [self.to_mate] + self.relays:
            made.wait_recv()
        for made in self.near.made:
            made.wait_send()


SPAN = 512
AHEAD = 3
LATE = 4
PAIRED = ((0, 2), (1, 3), (5, 6))
COMMON = (4, 7, 8)
BAND = 32


def dot(left, right, left_dim, right_dim):
    return lax.dot_general(
        left, right, (((left_dim,), (right_dim,)), ((), ())), preferred_element_type=f32
    )


def turn(block):
    return block.astype(f32).T


def allowed_pairs(segk, segq):
    return jnp.concatenate([segk] * (segq.shape[1] // 128), axis=1) == segq


def upper(block):
    return jnp.concatenate([block, jnp.zeros_like(block)], axis=0)


def lower(block):
    return jnp.concatenate([jnp.zeros_like(block), block], axis=0)


def attend(query, kv_ref, vt_ref, segk_ref, segq, hd):
    heads, keys = kv_ref.shape[:2]
    rows = query.shape[1]
    wide = [upper(query[head * hd : (head + 1) * hd]) for head in range(heads)]

    def step(index, state):
        at = pl.ds(pl.multiple_of(index * SPAN, SPAN), SPAN)
        allowed = allowed_pairs(segk_ref[at, :], segq)
        scores = [
            jnp.where(allowed, dot(kv_ref[head, at, :], wide[head], 1, 0), masked_value)
            for head in range(heads)
        ]
        made = []
        for head in range(heads):
            top, total, acc = state[head]
            new = jnp.maximum(top, jnp.max(scores[head], axis=0, keepdims=True))
            weights = jnp.exp(scores[head] - new)
            factor = jnp.exp(top - new)
            made.append(
                (
                    new,
                    total * factor + jnp.sum(weights, axis=0, keepdims=True),
                    acc * factor + dot(vt_ref[head * hd : (head + 1) * hd, at], weights.astype(bf16), 1, 0),
                )
            )
        return tuple(made)

    zero = tuple(
        (
            jnp.full((1, rows), 0.5 * masked_value, f32),
            jnp.zeros((1, rows), f32),
            jnp.zeros((hd, rows), f32),
        )
        for _ in range(heads)
    )
    state = lax.fori_loop(0, keys // SPAN, step, zero)
    return (
        jnp.concatenate([acc / total for _, total, acc in state], axis=0),
        jnp.concatenate([top + jnp.log(total) for top, total, _ in state], axis=0),
    )


def attend_back(qt, dt, log, delta, kv_ref, kt_ref, segk_ref, segq, dkv_ref, start, stop, hd):
    heads = kv_ref.shape[0]
    rows = qt.shape[1]
    part = [slice(head * hd, (head + 1) * hd) for head in range(heads)]
    wide_q = [upper(qt[one]) for one in part]
    wide_d = [lower(dt[one]) for one in part]

    def step(index, state):
        at = pl.ds(pl.multiple_of(index * SPAN, SPAN), SPAN)
        allowed = allowed_pairs(segk_ref[at, :], segq)
        low = []
        for head in range(heads):
            both = kv_ref[head, at, :]
            scores = dot(both, wide_q[head], 1, 0)
            d_prob = dot(both, wide_d[head], 1, 0)
            probs = jnp.where(allowed, jnp.exp(scores - log[head : head + 1]), 0.0)
            low.append((probs.astype(bf16), (probs * (d_prob - delta[head])).astype(bf16)))
        made = [
            state[head] + dot(kt_ref[part[head], at], low[head][1], 1, 0) for head in range(heads)
        ]
        dkv_ref[at, :] += jnp.concatenate(
            [dot(low[head][1], qt[part[head]], 1, 1) for head in range(heads)]
            + [dot(low[head][0], dt[part[head]], 1, 1) for head in range(heads)],
            axis=1,
        )
        return tuple(made)

    zero = tuple(jnp.zeros((hd, rows), f32) for _ in range(heads))
    return jnp.concatenate(lax.fori_loop(start, stop, step, zero), axis=0)


def add_into(dst, other, out=None):
    out = dst if out is None else out
    lead = dst.shape[0] if len(dst.shape) == 3 else 0
    rows = dst.shape[-2]
    band = 48 if rows % 48 == 0 else 32 if rows % 32 == 0 else 16
    steps = rows // band

    def go(index, carry):
        if lead:
            at = (index // steps, pl.ds(pl.multiple_of((index % steps) * band, band), band))
        else:
            at = (pl.ds(pl.multiple_of(index * band, band), band),)
        out[at] = (dst[at] + other[at]).astype(out.dtype)
        return carry

    lax.fori_loop(0, max(lead, 1) * steps, go, 0)


class Reduce:
    def __init__(self, wires, full, pair, land):
        self.w, self.full, self.pair, self.land = wires, full, pair, land
        self.half = pair.shape[1] // 2
        if full is not None:
            self.meet = wires.copy(full.at[:, 1 - wires.core], pair, wires.mate)

    def first(self):
        w, pair, land = self.w, self.pair, self.land
        low, high = pl.ds(0, self.half), pl.ds(self.half, self.half)
        if self.full is not None:
            self.meet.wait_recv()
            add_into(pair, self.full.at[:, w.core])
        self.x0 = w.start(pair.at[w.cd, low], land.at[1], w.xn)
        self.y0 = w.start(pair.at[w.cd, high], land.at[3], w.yn)
        self.x1 = w.start(pair.at[w.cx, low], land.at[0], w.xn)
        self.y1 = w.start(pair.at[w.cy, high], land.at[2], w.yn)

    def second(self):
        w, pair, land = self.w, self.pair, self.land
        low, high = pl.ds(0, self.half), pl.ds(self.half, self.half)
        self.x0.wait_recv()
        add_into(pair.at[w.cy, low], land.at[1])
        self.y2 = w.start(pair.at[w.cy, low], land.at[4], w.yn)
        self.y0.wait_recv()
        add_into(pair.at[w.cx, high], land.at[3])
        self.x2 = w.start(pair.at[w.cx, high], land.at[5], w.xn)
        self.x1.wait_recv()
        add_into(pair.at[w.chip, low], land.at[0])
        self.y1.wait_recv()
        add_into(pair.at[w.chip, high], land.at[2])

    def third(self, out):
        w, pair, land = self.w, self.pair, self.land
        low, high = pl.ds(0, self.half), pl.ds(self.half, self.half)
        self.y2.wait_recv()
        add_into(pair.at[w.chip, low], land.at[4], out.at[low])
        self.x2.wait_recv()
        add_into(pair.at[w.chip, high], land.at[5], out.at[high])

    def done(self):
        made = [self.x0, self.x1, self.y0, self.y1, self.x2, self.y2]
        if self.full is not None:
            made.append(self.meet)
        for one in made:
            one.wait_send()


class Line:
    def __init__(self, wires, z, block, land, out):
        self.w, self.z, self.block, self.land, self.out = wires, z, block, land, out
        self.edge = (z == 0) | (z == LINE - 1)
        self.inner = {"replica": 1 + z // 2}
        self.outer = {"replica": 3 * (z // 2)}
        self.across = {"replica": 2 - z // 2}
        self.up = wires.copy(block, land.at[0], self.inner)
        self.over = wires.copy(block, land.at[1], {"replica": 3 - z})
        self.back = wires.copy(out, out, self.outer)

    def first(self):
        @pl.when(self.edge)
        def _():
            self.up.start()

    def second(self):
        @pl.when(jnp.logical_not(self.edge))
        def _():
            self.up.wait_recv()
            add_into(self.block, self.land.at[0])
            self.over.start()

    def third(self):
        @pl.when(jnp.logical_not(self.edge))
        def _():
            self.over.wait_recv()
            add_into(self.block, self.land.at[1], self.out)
            self.back.start()

    def done(self):
        @pl.when(self.edge)
        def _():
            self.up.wait_send()
            self.back.wait_recv()

        @pl.when(jnp.logical_not(self.edge))
        def _():
            self.over.wait_send()
            self.back.wait_send()


def each(rows, block, step, init):
    def go(index, carry):
        return step(pl.ds(pl.multiple_of(index * block, block), block), carry)

    return lax.fori_loop(0, rows // block, go, init)


def fold_rows(block):
    return jnp.sum(block.reshape(block.shape[0] // 8, 8, block.shape[1]), axis=0)


def settle(block):
    return jnp.sum(block, axis=0, keepdims=True)


def vector(small, row, part):
    return jnp.concatenate(
        [small[source, row : row + 1, :part].astype(f32) for source in range(PLANE)], axis=1
    )


def put_vector(stack, row, value, part):
    for source in range(PLANE):
        stack[source, row : row + 1, :part] = value[:, source * part : (source + 1) * part]


def moments(block):
    mean_value = jnp.mean(block, axis=-1, keepdims=True)
    centered = block - mean_value
    scale = lax.rsqrt(jnp.mean(centered * centered, axis=-1, keepdims=True) + norm_epsilon)
    return centered * scale, scale


def norm_back(grad, gain, unit, scale):
    scaled = grad * gain
    return (
        scaled
        - jnp.mean(scaled, axis=-1, keepdims=True)
        - unit * jnp.mean(scaled * unit, axis=-1, keepdims=True)
    ) * scale


def layer_kernel(
    hid,
    wq,
    small,
    wo,
    wi,
    wb,
    cot,
    out_o,
    dq_o,
    db_o,
    di_o,
    do_o,
    dh_o,
    small_o,
    weights,
    names_s,
    wq_s,
    wq_a,
    hid_s,
    hidt,
    qt,
    kv_s,
    kt,
    vt,
    segk,
    segq,
    ctx32,
    log,
    ctx_s,
    ctxt,
    acc_s,
    unit_s,
    scale_s,
    low_s,
    lowt_s,
    act_s,
    slope_s,
    wide_s,
    grad_s,
    resid_s,
    dctx_s,
    dkv_a,
    dqkv_s,
    gq_s,
    tiny_s,
    q_pair,
    q_all,
    pair,
    land,
    dh_land,
    part_s,
    s_land,
    s_sum,
    zq_land,
    z_land,
    zs_land,
    send,
    recv,
    loc,
    *,
    hd,
):
    w = Wires(send, recv)
    z = lax.axis_index("replica")
    me, core = w.me, w.core
    tok, width = hid.shape
    wide = width // CHIPS
    heads = wide // hd
    ff = wi.shape[1]
    part = width // PLANE
    fold = ff // width
    rows_in = ff // PLANE // 128
    seg_row = 8 + rows_in

    loads = [pltpu.make_async_copy(wo, weights.at[0, w.chip, core], loc.at[0])]
    for slot in range(fold):
        loads.append(
            pltpu.make_async_copy(
                wi.at[:, pl.ds(slot * width, width)], weights.at[1 + slot, w.chip, core], loc.at[1 + slot]
            )
        )
    for slot in range(fold):
        loads.append(
            pltpu.make_async_copy(
                wb.at[pl.ds(slot * part, part)],
                weights.at[1 + fold + slot, w.chip, core],
                loc.at[1 + fold + slot],
            )
        )
    for one in loads:
        one.start()

    barrier = pltpu.get_barrier_semaphore()
    for other in plane_others(me):
        pl.semaphore_signal(barrier, inc=1, device_id=other, device_id_type=MESH)
    edge = (z == 0) | (z == LINE - 1)

    @pl.when(edge)
    def _():
        pl.semaphore_signal(barrier, inc=1, device_id={"replica": 1 + z // 2}, device_id_type=MESH)

    @pl.when(jnp.logical_not(edge))
    def _():
        pl.semaphore_signal(barrier, inc=1, device_id={"replica": 3 * (z // 2)}, device_id_type=MESH)
        pl.semaphore_signal(barrier, inc=1, device_id={"replica": 3 - z}, device_id_type=MESH)

    odd = z % 2
    far = {"replica": z + 1 - 2 * odd}
    for chip in range(CHIPS):
        for place, section in enumerate((1, 2, 0)):
            start = section * width + chip * wide
            wq_s[chip, :, place * wide : (place + 1) * wide] = wq[:, start : start + wide]

    @pl.when(edge)
    def _():
        pl.semaphore_wait(barrier, PLANE)

    @pl.when(jnp.logical_not(edge))
    def _():
        pl.semaphore_wait(barrier, PLANE + 1)

    names_s[me] = small[...]
    hid_s[w.chip, core] = hid[...]
    first = Gather(w, hid_s, hid)
    first.begin()
    wq_a[me] = wq_s[w.chip]
    q_mate = w.start(wq_s.at[w.chip], wq_a.at[me], w.mate)
    q_d = w.start(wq_s.at[w.cd], wq_a.at[me], w.dn)
    q_x = w.start(wq_s.at[w.cx], wq_a.at[me], w.xn)
    q_y = w.start(wq_s.at[w.cy], wq_a.at[me], w.yn)
    smalls = [w.start(small, names_s.at[me], (me + step) % PLANE) for step in range(1, PLANE)]
    first.relay()
    q_on = []
    for came, source in ((q_x, w.xn), (q_y, w.yn), (q_d, w.dn)):
        came.wait_recv()
        q_on.append(w.start(wq_a.at[source], wq_a.at[source], w.mate))
    for one in loads:
        one.wait()
    own_ids = [even + odd * (uneven - even) for even, uneven in PAIRED]
    far_ids = [uneven + odd * (even - uneven) for even, uneven in PAIRED]
    mine = [Gather(w, weights.at[one], far=far) for one in own_ids]
    theirs = [Passed(w, weights.at[one], source) for one, source in zip(far_ids, mine)]
    both = [Gather(w, weights.at[one]) for one in COMMON]
    for one in mine + theirs:
        one.begin()
    for made in smalls:
        made.wait_recv()
    for source in range(PLANE):
        ids = names_s[source].astype(f32)[seg_row : seg_row + tok // 128]
        segq[source] = jnp.concatenate([ids[one : one + 1] for one in range(tok // 128)], axis=1)
        for one in range(tok // 128):
            at = source * tok + one * 128
            segk[at : at + 128, :] = jnp.broadcast_to(ids[one : one + 1], (128, 128)).T
    first.finish()
    for made in [q_mate] + q_on:
        made.wait_recv()
    first.done()

    names = [names_s[2 * w.chip + side].astype(f32).T for side in range(2)]
    bias_q = jnp.concatenate([one[:part, 0:1] for one in names], axis=0)
    bias_v = jnp.concatenate([one[:part, 1:2] for one in names], axis=0)

    def project(index, carry):
        for mine in (True, False):
            side = core if mine else 1 - core
            block = hid_s[index, side]
            weight = wq_a[...].reshape(width, 3 * wide)
            rows = pl.ds(pl.multiple_of((2 * index + side) * tok, tok), tok)
            kv = dot(block, weight if mine else weight[:, : 2 * wide], 1, 0)
            kvt = kv.T
            low_v = (kvt[wide : 2 * wide] + bias_v).astype(bf16)
            kt[:, rows] = kvt[:wide].astype(bf16)
            vt[:, rows] = low_v
            back = turn(low_v)
            for head in range(heads):
                cols = slice(head * hd, (head + 1) * hd)
                kv_s[head, rows, :] = jnp.concatenate([kv[:, cols], back[:, cols]], axis=1).astype(bf16)
            if mine:
                query = kvt[2 * wide :] + bias_q
                qt[index] = (query.astype(bf16).astype(f32) * scale_factor).astype(bf16)
                hidt[index] = turn(block).astype(bf16)
        return carry

    lax.fori_loop(0, CHIPS, project, 0)
    mine[0].relay()
    ctx_made = []
    for turn_no, (index, who) in enumerate(
        ((w.cd, w.dn), (w.cx, w.xn), (w.cy, w.yn), (w.chip, None))
    ):
        context, logs = attend(qt[index], kv_s, vt, segk, segq[2 * index + core], hd)
        ctx32[index] = context
        log[index] = logs
        if who is None:
            ctxt[w.chip] = context.astype(bf16)
        else:
            ctx_s[index] = context.astype(bf16)
            ctx_made.append(w.start(ctx_s.at[index], ctxt.at[w.chip], who))
        if turn_no == 0:
            mine[1].relay()
            mine[0].finish()
            mine[2].relay()
            for one in both:
                one.begin()
        if turn_no == 1:
            mine[1].finish()
            theirs[0].relay()
            mine[2].finish()
        if turn_no == 2:
            theirs[0].finish()
            both[0].relay()
    both[1].relay()
    theirs[1].relay()
    both[0].finish()
    both[2].relay()
    theirs[1].finish()
    for made in ctx_made:
        made.wait()
    theirs[0].done()
    mine[0].done()

    wo_v = weights[0].reshape(width, width)
    bo, g1, s1, bb, g2, s2 = (vector(names_s, row, part) for row in range(2, 8))
    tiny_s[...] = jnp.zeros_like(tiny_s)
    acc_s[...] = dot(turn(ctxt[...].reshape(width, tok)).astype(bf16), wo_v, 1, 0)

    def open_one(at, carry):
        unit, scale = moments(hid[at, :].astype(f32) + acc_s[at, :] + bo)
        unit_s[at, :] = unit
        scale_s[at, :] = jnp.broadcast_to(scale, (BAND, 128))
        normed = unit * g1 + s1
        low_s[at, :] = normed.astype(bf16)
        acc_s[at, :] = normed + bb
        return carry

    each(tok, BAND, open_one, 0)
    lowt_s[...] = turn(low_s[...]).astype(bf16)
    both[1].finish()
    theirs[1].done()
    mine[1].done()
    both[0].done()

    def up(chunk, carry):
        bias = jnp.concatenate(
            [
                names_s[2 * chunk + side, 8 + row : 9 + row, :].astype(f32)
                for side in range(2)
                for row in range(rows_in)
            ],
            axis=1,
        )
        wide_s[...] = dot(low_s[...], weights[1 + chunk].reshape(width, width), 1, 0)

        def gelu(at, carry):
            pre = wide_s[at, :] + bias
            phi = 0.5 * (1.0 + lax.erf(pre * math.sqrt(0.5)))
            act_s[chunk, at, :] = (pre * phi).astype(bf16)
            slope_s[chunk, at, :] = phi + pre * (
                jnp.exp(-0.5 * pre * pre) * (1.0 / math.sqrt(2.0 * math.pi))
            )
            return carry

        each(tok, BAND, gelu, 0)
        return carry

    lax.fori_loop(0, fold, up, 0)
    both[2].finish()
    theirs[2].relay()
    theirs[2].finish()
    for one in (mine[2], theirs[2], both[1], both[2]):
        one.done()

    def back_rows(chunk):
        return jnp.concatenate(
            [weights[1 + fold + row, chunk, side] for side in range(2) for row in range(fold)], axis=0
        )

    def join_back(chunk, carry):
        acc_s[...] += dot(act_s[chunk], back_rows(chunk), 1, 0)
        return carry

    lax.fori_loop(0, fold, join_back, 0)

    zero = jnp.zeros((8, width), f32)

    def close(at, sums):
        unit, scale = moments(acc_s[at, :])
        out_o[at, :] = (unit * g2 + s2).astype(bf16)
        grad = cot[at, :]
        d_resid = norm_back(grad, g2, unit, scale)
        acc_s[at, :] = d_resid
        grad_s[at, :] = d_resid.astype(bf16)
        return (sums[0] + fold_rows(d_resid), sums[1] + fold_rows(grad * unit), sums[2] + fold_rows(grad))

    sums = each(tok, BAND, close, (zero, zero, zero))
    for row, value in zip((5, 6, 7), sums):
        put_vector(tiny_s, row, settle(value), part)

    def down(chunk, carry):
        grad = grad_s[...]
        wide_s[...] = dot(grad, back_rows(chunk), 1, 1)
        made = dot(turn(act_s[chunk]).astype(bf16), grad, 1, 0).astype(bf16)
        for side in range(2):
            for row in range(fold):
                start = (side * fold + row) * part
                weights[1 + fold + row, chunk, side] = made[start : start + part]

        def through(at, sums):
            d_pre = wide_s[at, :] * slope_s[chunk, at, :]
            act_s[chunk, at, :] = d_pre.astype(bf16)
            return sums + fold_rows(d_pre)

        total = settle(each(tok, BAND, through, zero))
        for side in range(2):
            for row in range(rows_in):
                start = (side * rows_in + row) * 128
                tiny_s[2 * chunk + side, 8 + row : 9 + row, :] = total[:, start : start + 128]
        return carry

    lax.fori_loop(0, fold, down, 0)

    picks = [(1 + fold + slot, db_o.at[pl.ds(slot * part, part)]) for slot in range(fold)]
    picks += [(1 + slot, di_o.at[:, pl.ds(slot * width, width)]) for slot in range(fold)]
    picks.append((0, do_o))
    count = len(picks)
    chunks = [
        Reduce(w, weights.at[which], pair.at[slot], land.at[slot]) for slot, (which, _) in enumerate(picks)
    ]
    lines = [
        Line(w, z, part_s.at[slot], z_land.at[slot], out) for slot, (_, out) in enumerate(picks)
    ]
    for one in chunks[:AHEAD]:
        one.meet.start()
    ticks = 0

    def tick():
        nonlocal ticks
        now = ticks
        ticks += 1
        if now + AHEAD < count:
            chunks[now + AHEAD].meet.start()
        if now < count:
            chunks[now].first()
        if 0 <= now - 1 < count:
            chunks[now - 1].second()
        if 0 <= now - 2 < count:
            chunks[now - 2].third(part_s.at[now - 2])
            lines[now - 2].first()
        if 0 <= now - LATE < count:
            lines[now - LATE].second()
        if 0 <= now - 2 * LATE + 2 < count:
            lines[now - 2 * LATE + 2].third()

    for chunk in range(fold):
        d_low = act_s[chunk]
        acc_s[...] += dot(d_low, weights[1 + chunk].reshape(width, width), 1, 1)
        weights[1 + chunk] = dot(lowt_s[...], d_low, 1, 0).astype(bf16).reshape(CHIPS, 2, part, width)
        tick()

    def finish(at, sums):
        unit = unit_s[at, :]
        grad = acc_s[at, :]
        d_resid = norm_back(grad, g1, unit, scale_s[at, 0:1])
        resid_s[at, :] = d_resid
        grad_s[at, :] = d_resid.astype(bf16)
        return (sums[0] + fold_rows(d_resid), sums[1] + fold_rows(grad * unit), sums[2] + fold_rows(grad))

    sums = each(tok, BAND, finish, (zero, zero, zero))
    grad = grad_s[...]
    ctx_s[...] = dot(weights[0].reshape(width, width), grad, 1, 1).astype(bf16).reshape(CHIPS, wide, tok)
    dctx_made = [
        w.start(ctx_s.at[chip], dctx_s.at[w.chip], who)
        for chip, who in ((w.cx, w.xn), (w.cy, w.yn), (w.cd, w.dn))
    ]
    dctx_s[w.chip] = ctx_s[w.chip]
    weights[0] = dot(ctxt[...].reshape(width, tok), grad, 1, 0).astype(bf16).reshape(CHIPS, 2, part, width)
    for row, value in zip((2, 3, 4), sums):
        put_vector(tiny_s, row, settle(value), part)
    tick()

    dq_s = slope_s.at[:, 0:wide, 0:tok]
    dkv_a[...] = jnp.zeros_like(dkv_a)
    steps = PLANE * tok // SPAN
    for turn_no, index in enumerate((w.chip, w.cx, w.cy, w.cd)):
        if turn_no:
            dctx_made[turn_no - 1].wait_recv()
        dt = dctx_s[index]
        product = dt.astype(f32) * ctx32[index]
        delta = [
            jnp.sum(product[head * hd : (head + 1) * hd], axis=0, keepdims=True) for head in range(heads)
        ]
        dq_s[index] = attend_back(
            qt[index], dt, log[index], delta, kv_s, kt, segk, segq[2 * index + core], dkv_a, 0, steps, hd
        )
        tick()

    dkv_s = hid_s.at[:, 0, :, 0 : 2 * wide]
    dkv_land = hid_s.at[:, 1, :, 0 : 2 * wide]

    def away(index, carry):
        at = pl.ds(pl.multiple_of((2 * index + 1 - core) * tok, tok), tok)
        dkv_s[index] = dkv_a[at, :].astype(bf16)
        return carry

    lax.fori_loop(0, CHIPS, away, 0)
    meet = w.start(dkv_s, dkv_land, w.mate)
    tick()
    meet.wait_recv()

    def join(index, sums):
        at = pl.ds(pl.multiple_of((2 * index + core) * tok, tok), tok)
        dkv = dkv_a[at, :] + dkv_land[index].astype(f32)
        dqkv = jnp.concatenate([dkv, (dq_s[index] * scale_factor).T], axis=1)
        dqkv_s[index] = dqkv.astype(bf16)
        return sums + jnp.sum(dqkv, axis=0, keepdims=True)

    sums = lax.fori_loop(0, CHIPS, join, jnp.zeros((1, 3 * wide), f32))
    for half in range(2):
        at = slice(half * width // 2, (half + 1) * width // 2)
        total = sum(dot(hidt[index, at, :], dqkv_s[index], 1, 0) for index in range(CHIPS))
        gq_s[2 * half : 2 * half + 2] = total.astype(bf16).reshape(2, 2, part, 3 * wide)
    q_meet = w.start(gq_s.at[:, 1 - core], q_pair, w.mate)
    for side in range(2):
        slot = 2 * w.chip + side
        tiny_s[slot, 0:1, :part] = sums[:, 2 * wide + side * part : 2 * wide + (side + 1) * part]
        tiny_s[slot, 1:2, :part] = sums[:, wide + side * part : wide + (side + 1) * part]
    tinies = [
        w.start(tiny_s.at[(me + step) % PLANE], s_land.at[me], (me + step) % PLANE)
        for step in range(1, PLANE)
    ]
    s_land[me] = tiny_s[me]
    dh_s = act_s
    hidden = Reduce(w, None, dh_s, dh_land)

    q_meet.wait_recv()
    add_into(q_pair, gq_s.at[:, core])
    q_made = [
        w.start(q_pair.at[chip], q_all.at[w.chip], who)
        for chip, who in ((w.cx, w.xn), (w.cy, w.yn), (w.cd, w.dn))
    ]
    q_all[w.chip] = q_pair[w.chip]
    q_lines = [
        Line(w, z, q_all.at[chip], zq_land.at[chip], dq_o.at[chip]) for chip in (w.chip, w.cx, w.cy, w.cd)
    ]
    q_lines[0].first()

    def input_grad(index, carry):
        dh_s[index] = dot(dqkv_s[index], wq_a[...].reshape(width, 3 * wide), 1, 1).astype(bf16)
        return carry

    lax.fori_loop(0, CHIPS, input_grad, 0)
    hidden.first()
    tick()
    for one in tinies:
        one.wait_recv()
    s_sum[...] = jnp.sum(s_land[...], axis=0)
    s_line = Line(w, z, s_sum, zs_land, small_o)
    s_line.first()
    for slot in (1, 2, 3):
        q_made[slot - 1].wait_recv()
        q_lines[slot].first()
        q_lines[slot - 1].second()
        if slot > 1:
            q_lines[slot - 2].third()
    tick()
    s_line.second()
    q_lines[3].second()
    q_lines[2].third()
    hidden.second()
    while ticks < count + 2 * LATE - 2:
        tick()
    s_line.third()
    q_lines[3].third()
    hidden.third(dh_o)
    for one in [q_mate, q_x, q_y, q_d] + q_on + smalls + tinies + q_made + [q_meet, meet] + dctx_made:
        one.wait_send()
    for one in chunks + [hidden]:
        one.done()
    for one in lines + q_lines + [s_line]:
        one.done()
    dh_o[...] = (resid_s[...] + dh_o[...].astype(f32)).astype(dh_o.dtype)


def layer_all(hid, wq, small, wo, wi, wb, cot, hd):
    tok, width = hid.shape
    wide = width // CHIPS
    part = wq.shape[0]
    ff = wi.shape[1]
    fold = ff // width
    seq = PLANE * tok
    rows, cols = wo.shape
    count = wb.shape[0] // rows + fold + 1
    q_block = (CHIPS, part, 3 * wide)
    shape = jax.ShapeDtypeStruct
    outs = [
        shape((tok, width), bf16),
        shape(q_block, bf16),
        shape(wb.shape, bf16),
        shape(wi.shape, bf16),
        shape(wo.shape, bf16),
        shape((tok, width), f32),
        shape((16, 128), f32),
    ]
    pairs = (CHIPS, 2)
    heads_block = (CHIPS, wide, tok)
    scratch = [
        VMEM((count,) + pairs + wo.shape, bf16),
        VMEM((PLANE, 16, 128), bf16),
        VMEM(q_block, bf16),
        VMEM((PLANE, part, 3 * wide), bf16),
        VMEM(pairs + (tok, width), bf16),
        VMEM((CHIPS, width, tok), bf16),
        VMEM(heads_block, bf16),
        VMEM((wide // hd, seq, 2 * hd), bf16),
        VMEM((wide, seq), bf16),
        VMEM((wide, seq), bf16),
        VMEM((seq, 128), f32),
        VMEM((PLANE, 1, tok), f32),
        VMEM(heads_block, f32),
        VMEM((CHIPS, wide // hd, tok), f32),
        VMEM(heads_block, bf16),
        VMEM(heads_block, bf16),
        VMEM((tok, width), f32),
        VMEM((tok, width), f32),
        VMEM((tok, 128), f32),
        VMEM((tok, width), bf16),
        VMEM((width, tok), bf16),
        VMEM((fold, tok, width), bf16),
        VMEM((fold, tok, width), f32),
        VMEM((tok, width), f32),
        VMEM((tok, width), bf16),
        VMEM((tok, width), f32),
        VMEM(heads_block, bf16),
        VMEM((seq, 2 * wide), f32),
        VMEM((CHIPS, tok, 3 * wide), bf16),
        VMEM(pairs + (part, 3 * wide), bf16),
        VMEM((PLANE, 16, 128), f32),
        VMEM(q_block, bf16),
        VMEM(q_block, bf16),
        VMEM((count, CHIPS, rows, cols), bf16),
        VMEM((count, 6, rows // 2, cols), bf16),
        VMEM((6, tok // 2, width), bf16),
        VMEM((count, rows, cols), bf16),
        VMEM((PLANE, 16, 128), f32),
        VMEM((16, 128), f32),
        VMEM((CHIPS, 2) + q_block[1:], bf16),
        VMEM((count, 2, rows, cols), bf16),
        VMEM((2, 16, 128), f32),
    ]
    return pl.pallas_call(
        functools.partial(layer_kernel, hd=hd),
        out_shape=outs,
        in_specs=[pl.BlockSpec(memory_space=space) for space in (VMEM, VMEM, VMEM, ANY, ANY, ANY, VMEM)],
        out_specs=[pl.BlockSpec(memory_space=VMEM)] * 7,
        scratch_shapes=scratch + dma_sems(count * 10 + 170) + [pltpu.SemaphoreType.DMA((count,))],
        compiler_params=pltpu.CompilerParams(
            collective_id=1, has_side_effects=True, vmem_limit_bytes=67043328
        ),
        name="layer_all",
    )(hid, wq, small, wo, wi, wb, cot)


def finish_kernel(*refs):
    ins, rest = refs[:7], refs[7:]
    dq_o, db_o, di_o, do_o, dh_o, out_o, qv_o, bi_o = rest[:8]
    vectors, copies, sems = rest[8:14], rest[14:21], rest[21]
    made = [
        pltpu.make_async_copy(one, copy, sems.at[slot]) for slot, (one, copy) in enumerate(zip(ins, copies))
    ]
    for one in made:
        one.start()
    dq, db, di, do, dh, out, tiny = copies
    wide = dq.shape[2] // 3
    width = dh.shape[1]
    part = do.shape[0]
    made[0].wait()
    for chip in range(CHIPS):
        for place, section in enumerate((1, 2, 0)):
            start = section * width + chip * wide
            dq_o[:, start : start + wide] = dq[chip, :, place * wide : (place + 1) * wide].astype(f32)
    for one in made[1:]:
        one.wait()
    db_o[...] = db[...].astype(f32)
    di_o[...] = di[...].astype(f32)
    do_o[...] = do[...].astype(f32)
    dh_o[...] = dh[...]
    out_o[...] = out[...]
    qv_o[...] = tiny[0:2, :part]
    for row, one in enumerate(vectors):
        one[...] = tiny[2 + row : 3 + row, :part]
    lines = bi_o.shape[1] // 128
    bi_o[...] = jnp.concatenate([tiny[8 + row : 9 + row, :] for row in range(lines)], axis=1)


def finish_all(dq, db, di, do, dh, out, tiny):
    part, wide = dq.shape[1:]
    shape = jax.ShapeDtypeStruct
    ins = (dq, db, di, do, dh, out, tiny)
    outs = [shape((part, CHIPS * wide), f32)] + [shape(one.shape, f32) for one in (db, di, do, dh)]
    outs += [shape(out.shape, out.dtype), shape((2, part), f32), shape((1, db.shape[0]), f32)]
    outs += [shape((1, part), f32)] * 6
    return pl.pallas_call(
        finish_kernel,
        out_shape=outs,
        in_specs=[pl.BlockSpec(memory_space=ANY)] * 7,
        out_specs=[pl.BlockSpec(memory_space=VMEM)] * 14,
        scratch_shapes=[VMEM(one.shape, one.dtype) for one in ins] + [pltpu.SemaphoreType.DMA((7,))],
        compiler_params=pltpu.CompilerParams(vmem_limit_bytes=60 << 20),
        name="finish_all",
    )(*ins)


def fast_body(
    hidden,
    segment_ids,
    w_qkv,
    b_qv,
    w_out,
    b_out,
    gain1,
    shift1,
    w_in,
    b_in,
    w_back,
    b_back,
    gain2,
    shift2,
    cotangent,
):
    tok, width = hidden.shape
    hd = width // HEADS
    part = w_qkv.shape[0]
    ff = w_in.shape[1]
    lines = b_in.shape[0] // 128
    narrow = jnp.concatenate(
        [b_qv] + [one[None] for one in (b_out, gain1, shift1, b_back, gain2, shift2)], axis=0
    )
    small = jnp.concatenate(
        [
            jnp.pad(narrow, ((0, 0), (0, 128 - part))),
            b_in.reshape(lines, 128),
            segment_ids.astype(bf16).reshape(tok // 128, 128),
            jnp.zeros((8 - lines - tok // 128, 128), bf16),
        ],
        axis=0,
    )
    output, dq, db, di, do, dh, tiny = layer_all(
        hidden, w_qkv, small, w_out, w_in, w_back, cotangent, hd
    )
    g_qkv, g_back, g_in, g_out, d_hidden, output, g_qv, g_bin, *vectors = finish_all(
        dq, db, di, do, dh, output, tiny
    )
    g_bout, g_gain1, g_shift1, g_bback, g_gain2, g_shift2 = (one.reshape(part) for one in vectors)
    return (
        output,
        d_hidden,
        g_qkv,
        g_qv,
        g_out,
        g_bout,
        g_gain1,
        g_shift1,
        g_in,
        g_bin.reshape(ff // PLANE),
        g_back,
        g_bback,
        g_gain2,
        g_shift2,
    )


def solution(mesh):
    in_specs = (
        P(("replica", "shard"), None),
        P(("replica", "shard")),
        P("shard", None),
        P(None, "shard"),
        P("shard", None),
        P("shard"),
        P("shard"),
        P("shard"),
        P("shard", None),
        P("shard"),
        P("shard", None),
        P("shard"),
        P("shard"),
        P("shard"),
        P(("replica", "shard"), None),
    )
    out_specs = (
        P(("replica", "shard"), None),
        P(("replica", "shard"), None),
        P("shard", None),
        P(None, "shard"),
        P("shard", None),
        P("shard"),
        P("shard"),
        P("shard"),
        P("shard", None),
        P("shard"),
        P("shard", None),
        P("shard"),
        P("shard"),
        P("shard"),
    )
    paired = mesh.shape["shard"] == PLANE and mesh.shape["replica"] == LINE
    body = fast_body if paired else plain_body
    return jax.shard_map(body, mesh=mesh, in_specs=in_specs, out_specs=out_specs, check_vma=False)
```

```python
import functools
import math

import jax
import jax.numpy as jnp
from jax import lax
from jax.experimental import pallas as pl
from jax.experimental.pallas import tpu as pltpu
from jax.sharding import PartitionSpec as P

HEADS = 12


scale_factor = 0.125
norm_epsilon = 1e-05
masked_value = -1e30


def normalize(resid, gain, shift):
    mean_value = jnp.mean(resid, axis=-1, keepdims=True)
    centered = resid - mean_value
    variance = jnp.mean(centered * centered, axis=-1, keepdims=True)
    return centered * lax.rsqrt(variance + norm_epsilon) * gain + shift


def gelu_exact(values):
    return jax.nn.gelu(values, approximate=False)


def keep_state(state):
    return state


def block_size(count):
    return math.gcd(count, 512)


def masked_scores(query_heads, key_heads, query_segs, key_segs):
    scores = (
        jnp.einsum("qhd,khd->hqk", query_heads, key_heads, preferred_element_type=jnp.float32)
        * scale_factor
    )
    allowed = query_segs[:, None] == key_segs[None, :]
    return (scores, allowed[None])


def grad_block(
    query_heads, dctx_heads, log_total, delta, query_segs, key_heads, value_heads, key_segs
):
    scores, allowed = masked_scores(query_heads, key_heads, query_segs, key_segs)
    probs = jnp.where(allowed, jnp.exp(scores - log_total[:, :, None]), 0.0)
    d_prob = jnp.einsum("qhd,khd->hqk", dctx_heads, value_heads, preferred_element_type=jnp.float32)
    d_scores = (probs * (d_prob - delta[:, :, None])).astype(jnp.bfloat16)
    return (probs.astype(jnp.bfloat16), d_scores)


def plain_body(
    hidden,
    segment_ids,
    w_qkv,
    b_qv,
    w_out,
    b_out,
    gain1,
    shift1,
    w_in,
    b_in,
    w_back,
    b_back,
    gain2,
    shift2,
    cotangent,
):
    tok_rows, width = hidden.shape
    heads = HEADS
    head_dim = width // heads
    seg_low = segment_ids[0]
    seg_high = segment_ids[-1]
    wq_full, wo_full, bqv_full, bo_full, g1_full, s1_full = (
        lax.all_gather(w_qkv, "shard", axis=0, tiled=True),
        lax.all_gather(w_out, "shard", axis=0, tiled=True),
        lax.all_gather(b_qv, "shard", axis=1, tiled=True),
        lax.all_gather(b_out, "shard", axis=0, tiled=True),
        lax.all_gather(gain1, "shard", axis=0, tiled=True),
        lax.all_gather(shift1, "shard", axis=0, tiled=True),
    )
    qkv = jnp.dot(hidden, wq_full, preferred_element_type=jnp.float32)
    bqv_wide = bqv_full.astype(jnp.float32)
    query = (qkv[:, :width] + bqv_wide[0]).astype(jnp.bfloat16)
    keys = qkv[:, width : 2 * width].astype(jnp.bfloat16)
    values = (qkv[:, 2 * width :] + bqv_wide[1]).astype(jnp.bfloat16)
    query_heads = query.reshape(tok_rows, heads, head_dim)
    key_local = keys.reshape(tok_rows, heads, head_dim)
    value_local = values.reshape(tok_rows, heads, head_dim)
    start_state = (
        jnp.full((heads, tok_rows), masked_value, jnp.float32),
        jnp.zeros((heads, tok_rows), jnp.float32),
        jnp.zeros((tok_rows, heads, head_dim), jnp.float32),
    )
    key_piece = lax.all_gather(keys, "shard", axis=0, tiled=True)
    value_piece = lax.all_gather(values, "shard", axis=0, tiled=True)
    seg_piece = lax.all_gather(segment_ids, "shard", axis=0, tiled=True)
    count = key_piece.shape[0]
    block = block_size(count)

    def forward_step(index, state):
        offset = index * block
        key_heads = lax.dynamic_slice_in_dim(key_piece, offset, block, 0).reshape(
            block, heads, head_dim
        )
        value_heads = lax.dynamic_slice_in_dim(value_piece, offset, block, 0).reshape(
            block, heads, head_dim
        )
        key_segs = lax.dynamic_slice_in_dim(seg_piece, offset, block, 0)

        def forward_update(state):
            running_max, running_sum, accum = state
            scores, allowed = masked_scores(query_heads, key_heads, segment_ids, key_segs)
            new_max = jnp.maximum(
                running_max, jnp.max(jnp.where(allowed, scores, masked_value), axis=-1)
            )
            factor = jnp.exp(running_max - new_max)
            weights = jnp.where(allowed, jnp.exp(scores - new_max[:, :, None]), 0.0)
            running_sum = running_sum * factor + jnp.sum(weights, axis=-1)
            accum = accum * factor.T[:, :, None] + jnp.einsum(
                "hqk,khd->qhd",
                weights.astype(jnp.bfloat16),
                value_heads,
                preferred_element_type=jnp.float32,
            )
            return (new_max, running_sum, accum)

        touches = jnp.logical_and(key_segs[0] <= seg_high, key_segs[-1] >= seg_low)
        return lax.cond(touches, forward_update, keep_state, state)

    running_max, running_sum, accum = lax.fori_loop(0, count // block, forward_step, start_state)
    context32 = accum / running_sum.T[:, :, None]
    log_total = running_max + jnp.log(running_sum)
    context = context32.reshape(tok_rows, width).astype(jnp.bfloat16)
    resid1 = (
        hidden.astype(jnp.float32)
        + jnp.dot(context, wo_full, preferred_element_type=jnp.float32)
        + bo_full.astype(jnp.float32)
    )
    normed1, norm1_pull = jax.vjp(
        normalize, resid1, g1_full.astype(jnp.float32), s1_full.astype(jnp.float32)
    )
    wi_full, bi_full, wb_full, bb_full, g2_full, s2_full = (
        lax.all_gather(w_in, "shard", axis=0, tiled=True),
        lax.all_gather(b_in, "shard", axis=0, tiled=True),
        lax.all_gather(w_back, "shard", axis=0, tiled=True),
        lax.all_gather(b_back, "shard", axis=0, tiled=True),
        lax.all_gather(gain2, "shard", axis=0, tiled=True),
        lax.all_gather(shift2, "shard", axis=0, tiled=True),
    )
    normed1_low = normed1.astype(jnp.bfloat16)
    pre = jnp.dot(normed1_low, wi_full, preferred_element_type=jnp.float32) + bi_full.astype(
        jnp.float32
    )
    act, gelu_pull = jax.vjp(gelu_exact, pre)
    act_low = act.astype(jnp.bfloat16)
    resid2 = (
        normed1
        + jnp.dot(act_low, wb_full, preferred_element_type=jnp.float32)
        + bb_full.astype(jnp.float32)
    )
    out32, norm2_pull = jax.vjp(
        normalize, resid2, g2_full.astype(jnp.float32), s2_full.astype(jnp.float32)
    )
    output = out32.astype(jnp.bfloat16)
    d_resid2, grad_gain2, grad_shift2 = norm2_pull(cotangent)
    d_branch2 = d_resid2.astype(jnp.bfloat16)
    grad_b_back = jnp.sum(d_resid2, axis=0)
    grad_w_back = jnp.einsum("tf,td->fd", act_low, d_branch2, preferred_element_type=jnp.float32)
    d_act = jnp.einsum("td,fd->tf", d_branch2, wb_full, preferred_element_type=jnp.float32)
    (d_pre,) = gelu_pull(d_act)
    grad_b_in = jnp.sum(d_pre, axis=0)
    d_pre_low = d_pre.astype(jnp.bfloat16)
    grad_w_in = jnp.einsum("td,tf->df", normed1_low, d_pre_low, preferred_element_type=jnp.float32)
    d_normed1 = d_resid2 + jnp.einsum(
        "tf,df->td", d_pre_low, wi_full, preferred_element_type=jnp.float32
    )
    d_resid1, grad_gain1, grad_shift1 = norm1_pull(d_normed1)
    grad_b_out = jnp.sum(d_resid1, axis=0)
    d_branch1 = d_resid1.astype(jnp.bfloat16)
    grad_w_out = jnp.einsum("tc,td->cd", context, d_branch1, preferred_element_type=jnp.float32)
    d_context = jnp.einsum(
        "td,cd->tc", d_branch1, wo_full, preferred_element_type=jnp.float32
    ).astype(jnp.bfloat16)
    dctx_heads = d_context.reshape(tok_rows, heads, head_dim)
    delta = jnp.einsum("qhd,qhd->hq", dctx_heads.astype(jnp.float32), context32)
    zero_heads = jnp.zeros((tok_rows, heads, head_dim), jnp.float32)
    query_key_piece = lax.all_gather(keys, "shard", axis=0, tiled=True)
    query_value_piece = lax.all_gather(values, "shard", axis=0, tiled=True)
    query_seg_piece = lax.all_gather(segment_ids, "shard", axis=0, tiled=True)
    count = query_key_piece.shape[0]
    query_block = block_size(count)

    def query_step(index, summed):
        offset = index * query_block
        key_heads = lax.dynamic_slice_in_dim(query_key_piece, offset, query_block, 0).reshape(
            query_block, heads, head_dim
        )
        value_heads = lax.dynamic_slice_in_dim(query_value_piece, offset, query_block, 0).reshape(
            query_block, heads, head_dim
        )
        key_segs = lax.dynamic_slice_in_dim(query_seg_piece, offset, query_block, 0)

        def query_update(summed):
            probs, d_scores = grad_block(
                query_heads,
                dctx_heads,
                log_total,
                delta,
                segment_ids,
                key_heads,
                value_heads,
                key_segs,
            )
            return (
                summed
                + jnp.einsum(
                    "hqk,khd->qhd", d_scores, key_heads, preferred_element_type=jnp.float32
                )
                * scale_factor
            )

        touches = jnp.logical_and(key_segs[0] <= seg_high, key_segs[-1] >= seg_low)
        return lax.cond(touches, query_update, keep_state, summed)

    d_query = lax.fori_loop(0, count // query_block, query_step, zero_heads)
    all_log_total, all_delta = (
        lax.all_gather(log_total, "shard", axis=1, tiled=True),
        lax.all_gather(delta, "shard", axis=1, tiled=True),
    )
    query_piece = lax.all_gather(query, "shard", axis=0, tiled=True)
    dctx_piece = lax.all_gather(d_context, "shard", axis=0, tiled=True)
    key_seg_piece = lax.all_gather(segment_ids, "shard", axis=0, tiled=True)
    count = query_piece.shape[0]
    key_block = block_size(count)

    def key_step(index, state):
        offset = index * key_block
        piece_query = lax.dynamic_slice_in_dim(query_piece, offset, key_block, 0).reshape(
            key_block, heads, head_dim
        )
        piece_dctx = lax.dynamic_slice_in_dim(dctx_piece, offset, key_block, 0).reshape(
            key_block, heads, head_dim
        )
        piece_segs = lax.dynamic_slice_in_dim(key_seg_piece, offset, key_block, 0)
        piece_log = lax.dynamic_slice_in_dim(all_log_total, offset, key_block, 1)
        piece_delta = lax.dynamic_slice_in_dim(all_delta, offset, key_block, 1)

        def key_update(state):
            d_key, d_value = state
            probs, d_scores = grad_block(
                piece_query,
                piece_dctx,
                piece_log,
                piece_delta,
                piece_segs,
                key_local,
                value_local,
                segment_ids,
            )
            d_key = (
                d_key
                + jnp.einsum(
                    "hqk,qhd->khd", d_scores, piece_query, preferred_element_type=jnp.float32
                )
                * scale_factor
            )
            d_value = d_value + jnp.einsum(
                "hqk,qhd->khd", probs, piece_dctx, preferred_element_type=jnp.float32
            )
            return (d_key, d_value)

        touches = jnp.logical_and(piece_segs[0] <= seg_high, piece_segs[-1] >= seg_low)
        return lax.cond(touches, key_update, keep_state, state)

    d_key_heads, d_value_heads = lax.fori_loop(
        0, count // key_block, key_step, (zero_heads, zero_heads)
    )
    d_keys = d_key_heads.reshape(tok_rows, width)
    d_values = d_value_heads.reshape(tok_rows, width)
    d_query = d_query.reshape(tok_rows, width)
    grad_b_qv = jnp.stack([jnp.sum(d_query, axis=0), jnp.sum(d_values, axis=0)], axis=0)
    d_qkv = jnp.concatenate([d_query, d_keys, d_values], axis=1).astype(jnp.bfloat16)
    grad_w_qkv = jnp.einsum("td,te->de", hidden, d_qkv, preferred_element_type=jnp.float32)
    d_hidden = d_resid1 + jnp.einsum(
        "te,de->td", d_qkv, wq_full, preferred_element_type=jnp.float32
    )
    local_grads = (
        grad_w_qkv,
        grad_b_qv,
        grad_w_out,
        grad_b_out,
        grad_gain1,
        grad_shift1,
        grad_w_in,
        grad_b_in,
        grad_w_back,
        grad_b_back,
        grad_gain2,
        grad_shift2,
    )
    shard_grads = (
        lax.psum_scatter(
            local_grads[0].astype(jnp.bfloat16), "shard", scatter_dimension=0, tiled=True
        ).astype(jnp.float32),
        lax.psum_scatter(
            local_grads[1].astype(jnp.bfloat16), "shard", scatter_dimension=1, tiled=True
        ).astype(jnp.float32),
        lax.psum_scatter(
            local_grads[2].astype(jnp.bfloat16), "shard", scatter_dimension=0, tiled=True
        ).astype(jnp.float32),
        lax.psum_scatter(
            local_grads[3].astype(jnp.bfloat16), "shard", scatter_dimension=0, tiled=True
        ).astype(jnp.float32),
        lax.psum_scatter(
            local_grads[4].astype(jnp.bfloat16), "shard", scatter_dimension=0, tiled=True
        ).astype(jnp.float32),
        lax.psum_scatter(
            local_grads[5].astype(jnp.bfloat16), "shard", scatter_dimension=0, tiled=True
        ).astype(jnp.float32),
        lax.psum_scatter(
            local_grads[6].astype(jnp.bfloat16), "shard", scatter_dimension=0, tiled=True
        ).astype(jnp.float32),
        lax.psum_scatter(
            local_grads[7].astype(jnp.bfloat16), "shard", scatter_dimension=0, tiled=True
        ).astype(jnp.float32),
        lax.psum_scatter(
            local_grads[8].astype(jnp.bfloat16), "shard", scatter_dimension=0, tiled=True
        ).astype(jnp.float32),
        lax.psum_scatter(
            local_grads[9].astype(jnp.bfloat16), "shard", scatter_dimension=0, tiled=True
        ).astype(jnp.float32),
        lax.psum_scatter(
            local_grads[10].astype(jnp.bfloat16), "shard", scatter_dimension=0, tiled=True
        ).astype(jnp.float32),
        lax.psum_scatter(
            local_grads[11].astype(jnp.bfloat16), "shard", scatter_dimension=0, tiled=True
        ).astype(jnp.float32),
    )
    total_grads = (
        lax.psum(shard_grads[0].astype(jnp.bfloat16), "replica").astype(jnp.float32),
        lax.psum(shard_grads[1].astype(jnp.bfloat16), "replica").astype(jnp.float32),
        lax.psum(shard_grads[2].astype(jnp.bfloat16), "replica").astype(jnp.float32),
        lax.psum(shard_grads[3].astype(jnp.bfloat16), "replica").astype(jnp.float32),
        lax.psum(shard_grads[4].astype(jnp.bfloat16), "replica").astype(jnp.float32),
        lax.psum(shard_grads[5].astype(jnp.bfloat16), "replica").astype(jnp.float32),
        lax.psum(shard_grads[6].astype(jnp.bfloat16), "replica").astype(jnp.float32),
        lax.psum(shard_grads[7].astype(jnp.bfloat16), "replica").astype(jnp.float32),
        lax.psum(shard_grads[8].astype(jnp.bfloat16), "replica").astype(jnp.float32),
        lax.psum(shard_grads[9].astype(jnp.bfloat16), "replica").astype(jnp.float32),
        lax.psum(shard_grads[10].astype(jnp.bfloat16), "replica").astype(jnp.float32),
        lax.psum(shard_grads[11].astype(jnp.bfloat16), "replica").astype(jnp.float32),
    )
    return (output, d_hidden) + tuple(total_grads)


PLANE = 8
LINE = 4
CHIPS = 4
MESH = pl.DeviceIdType.MESH
VMEM = pltpu.VMEM
ANY = pl.ANY
f32 = jnp.float32
bf16 = jnp.bfloat16


class Wires:
    def __init__(self, send, recv):
        self.send, self.recv, self.used = send, recv, 0
        me = lax.axis_index("shard")
        self.me = me
        self.core = me % 2
        self.chip = me // 2
        self.mate = me + 1 - 2 * self.core
        self.xn = me + 2 - 4 * (self.chip % 2)
        self.yn = me + 4 - 8 * (me // 4)
        self.dn = self.xn + 4 - 8 * (me // 4)
        self.cx = self.xn // 2
        self.cy = self.yn // 2
        self.cd = self.dn // 2

    def copy(self, src, dst, where):
        slot = self.used
        self.used += 1
        return pltpu.make_async_remote_copy(
            src_ref=src,
            dst_ref=dst,
            send_sem=self.send.at[slot],
            recv_sem=self.recv.at[slot],
            device_id=where if isinstance(where, dict) else {"shard": where},
            device_id_type=MESH,
        )

    def start(self, src, dst, where):
        made = self.copy(src, dst, where)
        made.start()
        return made


def plane_others(me):
    return [{"shard": (me + step) % PLANE} for step in range(1, PLANE)]


def dma_sems(count):
    return [pltpu.SemaphoreType.DMA((count,)), pltpu.SemaphoreType.DMA((count,))]


class Gather:
    def __init__(self, wires, out, block=None, far=None):
        self.w, self.out, self.far = wires, out, far
        self.half = out.shape[2] // 2
        self.block = self.at(wires.me) if block is None else block
        self.made = []
        self.came = set()

    def at(self, who, *rows):
        if rows:
            return self.out.at[who // 2, who % 2, rows[0]]
        return self.out.at[who // 2, who % 2]

    def start(self, where, who, *rows):
        one = self.w.start(self.at(who, *rows), self.at(who, *rows), where)
        self.made.append(one)
        return one

    def pass_on(self, who):
        one = self.start(self.far, who)
        return one

    def begin(self):
        w, mine = self.w, self.at(self.w.me)
        self.to_x = w.start(self.block, mine, w.xn)
        self.to_y = w.start(self.block, mine, w.yn)
        self.to_mate = w.start(self.block, mine, w.mate)
        self.made += [self.to_x, self.to_y, self.to_mate]

    def relay(self):
        w, half = self.w, self.half
        self.to_x.wait_recv()
        self.x_on = self.start(w.yn, w.xn, pl.ds(0, half))
        if self.far is not None:
            self.x_far = self.pass_on(w.xn)
        self.x_mate = self.start(w.mate, w.xn)
        self.to_y.wait_recv()
        self.y_on = self.start(w.xn, w.yn, pl.ds(half, half))
        if self.far is not None:
            self.y_far = self.pass_on(w.yn)
        self.y_mate = self.start(w.mate, w.yn)

    def finish(self):
        w, half = self.w, self.half
        self.x_on.wait_recv()
        self.d_low = self.start(w.mate, w.dn, pl.ds(0, half))
        self.y_on.wait_recv()
        self.d_high = self.start(w.mate, w.dn, pl.ds(half, half))
        if self.far is not None:
            self.d_far = self.pass_on(w.dn)

    def took(self, *names):
        for name in names:
            if name not in self.came:
                self.came.add(name)
                getattr(self, name).wait_recv()

    def done(self):
        self.took("to_mate", "x_mate", "y_mate", "d_low", "d_high")
        for made in self.made:
            made.wait_send()


class Passed:
    def __init__(self, wires, out, source):
        self.w, self.source = wires, source
        self.near = Gather(wires, out)
        self.relays = []

    def begin(self):
        w = self.w
        self.to_mate = self.near.start(w.mate, w.me)

    def relay(self):
        self.source.x_far.wait_recv()
        self.relays.append(self.near.start(self.w.mate, self.w.xn))
        self.source.y_far.wait_recv()
        self.relays.append(self.near.start(self.w.mate, self.w.yn))

    def finish(self):
        self.source.d_far.wait_recv()
        self.relays.append(self.near.start(self.w.mate, self.w.dn))

    def done(self):
        for made in [self.to_mate] + self.relays:
            made.wait_recv()
        for made in self.near.made:
            made.wait_send()


SPAN = 512
PLAN_DOWN = ((), ("F0",), ("F1",), ("S0", "F2"))
PLAN_OPEN = ("S1", "T0")
PLAN_IN = (("M4",), ("M5", "F3"), ("M6", "S2", "T1"), ("M7",), ("M8", "Y0"))
PLAN_BACK = (
    ("F4", "S3", "T2", "Y1", "Z0"),
    ("F5", "S4", "T3", "Y2", "Z1"),
    ("F6", "S5", "T4", "Y3", "Z2"),
    ("F7", "S6", "T5", "Y4", "Z3"),
)
PLAN_MEET = ("F8", "S7", "T6", "Y5", "Z4")
PLAN_GRAD = ("S8", "T7", "Y6", "Z5")
PLAN_SENT = ("Z6",)
PLAN_END = (("T8", "Y7"), ("Z7",), ("Y8",), ("Z8",))
PAIRED = ((0, 2), (1, 3))
COMMON = (4, 5, 6, 7, 8)
BAND = 32


def dot(left, right, left_dim, right_dim):
    return lax.dot_general(
        left, right, (((left_dim,), (right_dim,)), ((), ())), preferred_element_type=f32
    )


def turn(block):
    return block.astype(f32).T


def allowed_pairs(segk, segq):
    return jnp.concatenate([segk] * (segq.shape[1] // 128), axis=1) == segq


def upper(block):
    return jnp.concatenate([block, jnp.zeros_like(block)], axis=0)


def lower(block):
    return jnp.concatenate([jnp.zeros_like(block), block], axis=0)


def attend(query, kv_ref, vt_ref, segk_ref, segq, hd):
    heads, keys = kv_ref.shape[:2]
    rows = query.shape[1]
    wide = [upper(query[head * hd : (head + 1) * hd]) for head in range(heads)]

    def step(index, state):
        at = pl.ds(pl.multiple_of(index * SPAN, SPAN), SPAN)
        allowed = allowed_pairs(segk_ref[at, :], segq)
        scores = [
            jnp.where(allowed, dot(kv_ref[head, at, :], wide[head], 1, 0), masked_value)
            for head in range(heads)
        ]
        made = []
        for head in range(heads):
            top, total, acc = state[head]
            new = jnp.maximum(top, jnp.max(scores[head], axis=0, keepdims=True))
            weights = jnp.exp(scores[head] - new)
            factor = jnp.exp(top - new)
            made.append(
                (
                    new,
                    total * factor + jnp.sum(weights, axis=0, keepdims=True),
                    acc * factor + dot(vt_ref[head * hd : (head + 1) * hd, at], weights.astype(bf16), 1, 0),
                )
            )
        return tuple(made)

    zero = tuple(
        (
            jnp.full((1, rows), 0.5 * masked_value, f32),
            jnp.zeros((1, rows), f32),
            jnp.zeros((hd, rows), f32),
        )
        for _ in range(heads)
    )
    state = lax.fori_loop(0, keys // SPAN, step, zero)
    return (
        jnp.concatenate([acc / total for _, total, acc in state], axis=0),
        jnp.concatenate([top + jnp.log(total) for top, total, _ in state], axis=0),
    )


def attend_back(qt, dt, log, delta, kv_ref, kt_ref, segk_ref, segq, dkv_ref, start, stop, hd):
    heads = kv_ref.shape[0]
    rows = qt.shape[1]
    part = [slice(head * hd, (head + 1) * hd) for head in range(heads)]
    wide_q = [upper(qt[one]) for one in part]
    wide_d = [lower(dt[one]) for one in part]

    def step(index, state):
        at = pl.ds(pl.multiple_of(index * SPAN, SPAN), SPAN)
        allowed = allowed_pairs(segk_ref[at, :], segq)
        low = []
        for head in range(heads):
            both = kv_ref[head, at, :]
            scores = dot(both, wide_q[head], 1, 0)
            d_prob = dot(both, wide_d[head], 1, 0)
            probs = jnp.where(allowed, jnp.exp(scores - log[head : head + 1]), 0.0)
            low.append((probs.astype(bf16), (probs * (d_prob - delta[head])).astype(bf16)))
        made = [
            state[head] + dot(kt_ref[part[head], at], low[head][1], 1, 0) for head in range(heads)
        ]
        dkv_ref[at, :] += jnp.concatenate(
            [dot(low[head][1], qt[part[head]], 1, 1) for head in range(heads)]
            + [dot(low[head][0], dt[part[head]], 1, 1) for head in range(heads)],
            axis=1,
        )
        return tuple(made)

    zero = tuple(jnp.zeros((hd, rows), f32) for _ in range(heads))
    return jnp.concatenate(lax.fori_loop(start, stop, step, zero), axis=0)


def add_into(dst, other, out=None):
    out = dst if out is None else out
    lead = dst.shape[0] if len(dst.shape) == 3 else 0
    rows = dst.shape[-2]
    band = 48 if rows % 48 == 0 else 32 if rows % 32 == 0 else 16
    steps = rows // band

    def go(index, carry):
        if lead:
            at = (index // steps, pl.ds(pl.multiple_of((index % steps) * band, band), band))
        else:
            at = (pl.ds(pl.multiple_of(index * band, band), band),)
        out[at] = (dst[at] + other[at]).astype(out.dtype)
        return carry

    lax.fori_loop(0, max(lead, 1) * steps, go, 0)


class Reduce:
    def __init__(self, wires, full, pair, land):
        self.w, self.full, self.pair, self.land = wires, full, pair, land
        self.half = pair.shape[1] // 2
        if full is not None:
            self.meet = wires.copy(full.at[:, 1 - wires.core], pair, wires.mate)

    def first(self):
        w, pair, land = self.w, self.pair, self.land
        low, high = pl.ds(0, self.half), pl.ds(self.half, self.half)
        if self.full is not None:
            self.meet.wait_recv()
            add_into(pair, self.full.at[:, w.core])
        self.x0 = w.start(pair.at[w.cd, low], land.at[1], w.xn)
        self.y0 = w.start(pair.at[w.cd, high], land.at[3], w.yn)
        self.x1 = w.start(pair.at[w.cx, low], land.at[0], w.xn)
        self.y1 = w.start(pair.at[w.cy, high], land.at[2], w.yn)

    def second(self):
        w, pair, land = self.w, self.pair, self.land
        low, high = pl.ds(0, self.half), pl.ds(self.half, self.half)
        self.x0.wait_recv()
        add_into(pair.at[w.cy, low], land.at[1])
        self.y2 = w.start(pair.at[w.cy, low], land.at[4], w.yn)
        self.y0.wait_recv()
        add_into(pair.at[w.cx, high], land.at[3])
        self.x2 = w.start(pair.at[w.cx, high], land.at[5], w.xn)
        self.x1.wait_recv()
        add_into(pair.at[w.chip, low], land.at[0])
        self.y1.wait_recv()
        add_into(pair.at[w.chip, high], land.at[2])

    def third(self, out):
        w, pair, land = self.w, self.pair, self.land
        low, high = pl.ds(0, self.half), pl.ds(self.half, self.half)
        self.y2.wait_recv()
        add_into(pair.at[w.chip, low], land.at[4], out.at[low])
        self.x2.wait_recv()
        add_into(pair.at[w.chip, high], land.at[5], out.at[high])

    def done(self):
        made = [self.x0, self.x1, self.y0, self.y1, self.x2, self.y2]
        if self.full is not None:
            made.append(self.meet)
        for one in made:
            one.wait_send()


class Line:
    def __init__(self, wires, z, block, land, out):
        self.w, self.z, self.block, self.land, self.out = wires, z, block, land, out
        self.edge = (z == 0) | (z == LINE - 1)
        self.inner = {"replica": 1 + z // 2}
        self.outer = {"replica": 3 * (z // 2)}
        self.across = {"replica": 2 - z // 2}
        self.up = wires.copy(block, land.at[0], self.inner)
        self.over = wires.copy(block, land.at[1], {"replica": 3 - z})
        self.back = wires.copy(out, out, self.outer)

    def first(self):
        @pl.when(self.edge)
        def _():
            self.up.start()

    def second(self):
        @pl.when(jnp.logical_not(self.edge))
        def _():
            self.up.wait_recv()
            add_into(self.block, self.land.at[0])
            self.over.start()

    def third(self):
        @pl.when(jnp.logical_not(self.edge))
        def _():
            self.over.wait_recv()
            add_into(self.block, self.land.at[1], self.out)
            self.back.start()

    def done(self):
        @pl.when(self.edge)
        def _():
            self.up.wait_send()
            self.back.wait_recv()

        @pl.when(jnp.logical_not(self.edge))
        def _():
            self.over.wait_send()
            self.back.wait_send()


def each(rows, block, step, init):
    def go(index, carry):
        return step(pl.ds(pl.multiple_of(index * block, block), block), carry)

    return lax.fori_loop(0, rows // block, go, init)


def fold_rows(block):
    return jnp.sum(block.reshape(block.shape[0] // 8, 8, block.shape[1]), axis=0)


def settle(block):
    return jnp.sum(block, axis=0, keepdims=True)


def vector(small, row, part):
    return jnp.concatenate(
        [small[source, row : row + 1, :part].astype(f32) for source in range(PLANE)], axis=1
    )


def put_vector(stack, row, value, part):
    for source in range(PLANE):
        stack[source, row : row + 1, :part] = value[:, source * part : (source + 1) * part]


def moments(block):
    mean_value = jnp.mean(block, axis=-1, keepdims=True)
    centered = block - mean_value
    scale = lax.rsqrt(jnp.mean(centered * centered, axis=-1, keepdims=True) + norm_epsilon)
    return centered * scale, scale


def norm_back(grad, gain, unit, scale):
    scaled = grad * gain
    return (
        scaled
        - jnp.mean(scaled, axis=-1, keepdims=True)
        - unit * jnp.mean(scaled * unit, axis=-1, keepdims=True)
    ) * scale


def layer_kernel(
    hid,
    wq,
    small,
    wo,
    wi,
    wb,
    cot,
    out_o,
    dq_o,
    db_o,
    di_o,
    do_o,
    dh_o,
    small_o,
    weights,
    names_s,
    wq_s,
    wq_a,
    hid_s,
    hidt,
    qt,
    kv_s,
    kt,
    vt,
    segk,
    segq,
    ctx32,
    log,
    ctx_s,
    ctxt,
    acc_s,
    bias_s,
    unit_s,
    scale_s,
    low_s,
    lowt_s,
    act_s,
    slope_s,
    wide_s,
    grad_s,
    resid_s,
    dctx_s,
    dkv_a,
    dqkv_s,
    gq_s,
    tiny_s,
    q_pair,
    q_all,
    pair,
    land,
    dh_land,
    part_s,
    s_land,
    s_sum,
    zq_land,
    z_land,
    zs_land,
    send,
    recv,
    loc,
    *,
    hd,
):
    w = Wires(send, recv)
    z = lax.axis_index("replica")
    me, core = w.me, w.core
    tok, width = hid.shape
    wide = width // CHIPS
    heads = wide // hd
    ff = wi.shape[1]
    part = width // PLANE
    fold = ff // width
    rows_in = ff // PLANE // 128
    seg_row = 8 + rows_in

    loads = [pltpu.make_async_copy(wo, weights.at[0, w.chip, core], loc.at[0])]
    for slot in range(fold):
        loads.append(
            pltpu.make_async_copy(
                wi.at[:, pl.ds(slot * width, width)], pair.at[0, slot], loc.at[1 + slot]
            )
        )
    for slot in range(fold):
        loads.append(
            pltpu.make_async_copy(
                wb.at[pl.ds(slot * part, part)],
                weights.at[1 + fold + slot, w.chip, core],
                loc.at[1 + fold + slot],
            )
        )
    for one in loads:
        one.start()

    barrier = pltpu.get_barrier_semaphore()
    for other in plane_others(me):
        pl.semaphore_signal(barrier, inc=1, device_id=other, device_id_type=MESH)
    edge = (z == 0) | (z == LINE - 1)

    @pl.when(edge)
    def _():
        pl.semaphore_signal(barrier, inc=1, device_id={"replica": 1 + z // 2}, device_id_type=MESH)

    @pl.when(jnp.logical_not(edge))
    def _():
        pl.semaphore_signal(barrier, inc=1, device_id={"replica": 3 * (z // 2)}, device_id_type=MESH)
        pl.semaphore_signal(barrier, inc=1, device_id={"replica": 3 - z}, device_id_type=MESH)

    odd = z % 2
    far = {"replica": z + 1 - 2 * odd}
    for chip in range(CHIPS):
        for place, section in enumerate((1, 2, 0)):
            start = section * width + chip * wide
            wq_s[chip, :, place * wide : (place + 1) * wide] = wq[:, start : start + wide]

    @pl.when(edge)
    def _():
        pl.semaphore_wait(barrier, PLANE)

    @pl.when(jnp.logical_not(edge))
    def _():
        pl.semaphore_wait(barrier, PLANE + 1)

    names_s[me] = small[...]
    smalls = [w.start(small, names_s.at[me], (me + step) % PLANE) for step in range(1, PLANE)]
    wq_a[me] = wq_s[w.chip]
    q_mate = w.start(wq_s.at[w.chip], wq_a.at[me], w.mate)
    q_d = w.start(wq_s.at[w.cd], wq_a.at[me], w.dn)
    q_x = w.start(wq_s.at[w.cx], wq_a.at[me], w.xn)
    q_y = w.start(wq_s.at[w.cy], wq_a.at[me], w.yn)
    hid_s[w.chip, core] = hid[...]
    first = Gather(w, hid_s, hid)
    first.begin()
    for one in loads:
        one.wait()
    per = PLANE // fold
    for chunk in range(fold):
        weights[1 + chunk, w.chip, core] = jnp.concatenate(
            [
                pair[0, shard // per, :, start : start + part]
                for shard in range(PLANE)
                for start in [(shard % per) * fold * part + chunk * part]
            ],
            axis=1,
        )
    own_ids = [even + odd * (uneven - even) for even, uneven in PAIRED]
    far_ids = [uneven + odd * (even - uneven) for even, uneven in PAIRED]
    mine = [Gather(w, weights.at[one], far=far) for one in own_ids]
    theirs = [Passed(w, weights.at[one], source) for one, source in zip(far_ids, mine)]
    both = [Gather(w, weights.at[one]) for one in COMMON]
    q_on = []
    for came, source in ((q_x, w.xn), (q_y, w.yn), (q_d, w.dn)):
        came.wait_recv()
        q_on.append(w.start(wq_a.at[source], wq_a.at[source], w.mate))
    for made in smalls:
        made.wait_recv()
    for source in range(PLANE):
        ids = names_s[source].astype(f32)[seg_row : seg_row + tok // 128]
        segq[source] = jnp.concatenate([ids[one : one + 1] for one in range(tok // 128)], axis=1)
        for one in range(tok // 128):
            at = source * tok + one * 128
            segk[at : at + 128, :] = jnp.broadcast_to(ids[one : one + 1], (128, 128)).T
    names = [names_s[2 * w.chip + side].astype(f32).T for side in range(2)]
    bias_q = jnp.concatenate([one[:part, 0:1] for one in names], axis=0)
    bias_v = jnp.concatenate([one[:part, 1:2] for one in names], axis=0)
    spread = [
        jnp.concatenate(
            [names_s[source, 8 + row : 9 + row, :].astype(f32) for row in range(rows_in)], axis=1
        )
        for source in range(PLANE)
    ]
    for chunk in range(fold):
        bias_s[chunk] = jnp.concatenate(
            [one[:, chunk * part : (chunk + 1) * part] for one in spread], axis=1
        )
    for made in [q_mate] + q_on:
        made.wait_recv()

    def project(turn_no, carry):
        index = pick_turn(turn_no)
        for own in (True, False):
            side = core if own else 1 - core
            block = hid_s[index, side]
            weight = wq_a[...].reshape(width, 3 * wide)
            rows = pl.ds(pl.multiple_of((2 * index + side) * tok, tok), tok)
            kv = dot(block, weight if own else weight[:, : 2 * wide], 1, 0)
            kvt = kv.T
            low_v = (kvt[wide : 2 * wide] + bias_v).astype(bf16)
            kt[:, rows] = kvt[:wide].astype(bf16)
            vt[:, rows] = low_v
            back = turn(low_v)
            for head in range(heads):
                cols = slice(head * hd, (head + 1) * hd)
                kv_s[head, rows, :] = jnp.concatenate([kv[:, cols], back[:, cols]], axis=1).astype(bf16)
            if own:
                query = kvt[2 * wide :] + bias_q
                qt[index] = (query.astype(bf16).astype(f32) * scale_factor).astype(bf16)
                hidt[index] = turn(block).astype(bf16)
        return carry

    def pick_turn(turn_no):
        return (
            (turn_no == 0) * w.chip + (turn_no == 1) * w.cx + (turn_no == 2) * w.cy + (turn_no == 3) * w.cd
        )

    first.took("to_mate")
    lax.fori_loop(0, 1, project, 0)
    first.relay()
    for one in mine + theirs:
        one.begin()
    both[0].begin()
    first.took("x_mate", "y_mate")
    lax.fori_loop(1, 3, project, 0)
    first.finish()
    mine[0].relay()
    first.took("d_low", "d_high")
    lax.fori_loop(3, 4, project, 0)
    first.done()
    both[1].begin()
    mine[1].relay()
    ctx_made = []
    for turn_no, (index, who) in enumerate(
        ((w.cd, w.dn), (w.cx, w.xn), (w.cy, w.yn), (w.chip, None))
    ):
        context, logs = attend(qt[index], kv_s, vt, segk, segq[2 * index + core], hd)
        ctx32[index] = context
        log[index] = logs
        if who is None:
            ctxt[w.chip] = context.astype(bf16)
        else:
            ctx_s[index] = context.astype(bf16)
            ctx_made.append(w.start(ctx_s.at[index], ctxt.at[w.chip], who))
        if turn_no == 0:
            both[2].begin()
        if turn_no == 1:
            both[0].relay()
            both[3].begin()
            mine[0].finish()
        if turn_no == 2:
            both[1].relay()
            both[4].begin()
            mine[1].finish()
            theirs[0].relay()
        if turn_no == 3:
            both[2].relay()
            theirs[0].finish()
            both[0].finish()
            theirs[1].relay()
            both[3].relay()
    for made in ctx_made:
        made.wait()
    theirs[0].done()
    mine[0].done()

    wo_v = weights[0].reshape(width, width)
    bo, g1, s1, bb, g2, s2 = (vector(names_s, row, part) for row in range(2, 8))
    tiny_s[...] = jnp.zeros_like(tiny_s)
    acc_s[...] = dot(turn(ctxt[...].reshape(width, tok)).astype(bf16), wo_v, 1, 0)

    def open_one(at, carry):
        unit, scale = moments(hid[at, :].astype(f32) + acc_s[at, :] + bo)
        unit_s[at, :] = unit
        scale_s[at, :] = jnp.broadcast_to(scale, (BAND, 128))
        normed = unit * g1 + s1
        low_s[at, :] = normed.astype(bf16)
        acc_s[at, :] = normed + bb
        return carry

    each(tok, BAND, open_one, 0)
    lowt_s[...] = turn(low_s[...]).astype(bf16)
    theirs[1].finish()
    both[1].finish()
    both[4].relay()
    both[2].finish()
    theirs[1].done()
    mine[1].done()
    both[0].done()

    def up(chunk, carry):
        bias = bias_s[chunk]
        wide_s[...] = dot(low_s[...], weights[1 + chunk].reshape(width, width), 1, 0)

        def gelu(at, carry):
            pre = wide_s[at, :] + bias
            phi = 0.5 * (1.0 + lax.erf(pre * math.sqrt(0.5)))
            act_s[chunk, at, :] = (pre * phi).astype(bf16)
            slope_s[chunk, at, :] = phi + pre * (
                jnp.exp(-0.5 * pre * pre) * (1.0 / math.sqrt(2.0 * math.pi))
            )
            return carry

        each(tok, BAND, gelu, 0)
        return carry

    lax.fori_loop(0, fold, up, 0)
    both[3].finish()
    both[4].finish()
    for one in both[1:]:
        one.done()

    def join_back(chunk, carry):
        acc_s[...] += dot(act_s[chunk], weights[1 + fold + chunk].reshape(width, width), 1, 0)
        return carry

    lax.fori_loop(0, fold, join_back, 0)

    zero = jnp.zeros((8, width), f32)

    def close(at, sums):
        unit, scale = moments(acc_s[at, :])
        out_o[at, :] = (unit * g2 + s2).astype(bf16)
        grad = cot[at, :]
        d_resid = norm_back(grad, g2, unit, scale)
        acc_s[at, :] = d_resid
        grad_s[at, :] = d_resid.astype(bf16)
        return (sums[0] + fold_rows(d_resid), sums[1] + fold_rows(grad * unit), sums[2] + fold_rows(grad))

    sums = each(tok, BAND, close, (zero, zero, zero))
    for row, value in zip((5, 6, 7), sums):
        put_vector(tiny_s, row, settle(value), part)

    picks = [(1 + fold + slot, db_o.at[pl.ds(slot * part, part)]) for slot in range(fold)]
    picks += [(1 + slot, di_o.at[:, pl.ds(slot * width, width)]) for slot in range(fold)]
    picks.append((0, do_o))
    count = len(picks)
    chunks = [
        Reduce(w, weights.at[which], pair.at[slot], land.at[slot]) for slot, (which, _) in enumerate(picks)
    ]
    lines = [
        Line(w, z, part_s.at[slot], z_land.at[slot], out) for slot, (_, out) in enumerate(picks)
    ]
    left = [op + str(slot) for slot in range(count) for op in "MFSTYZ"]

    def go(plan):
        for name in plan:
            left.remove(name)
            slot = int(name[1:])
            chunk, line = chunks[slot], lines[slot]
            if name[0] == "M":
                chunk.meet.start()
            elif name[0] == "F":
                chunk.first()
            elif name[0] == "S":
                chunk.second()
            elif name[0] == "T":
                chunk.third(part_s.at[slot])
                line.first()
            elif name[0] == "Y":
                line.second()
            else:
                line.third()

    for chunk in range(fold):
        grad = grad_s[...]
        wide_s[...] = dot(grad, weights[1 + fold + chunk].reshape(width, width), 1, 1)
        weights[1 + fold + chunk] = (
            dot(turn(act_s[chunk]).astype(bf16), grad, 1, 0).astype(bf16).reshape(CHIPS, 2, part, width)
        )
        go(("M" + str(chunk),))

        def through(at, sums):
            d_pre = wide_s[at, :] * slope_s[chunk, at, :]
            act_s[chunk, at, :] = d_pre.astype(bf16)
            return sums + fold_rows(d_pre)

        put_vector(tiny_s, 8 + chunk, settle(each(tok, BAND, through, zero)), part)
        acc_s[...] += dot(act_s[chunk], weights[1 + chunk].reshape(width, width), 1, 1)
        go(PLAN_DOWN[chunk])

    def finish(at, sums):
        unit = unit_s[at, :]
        grad = acc_s[at, :]
        d_resid = norm_back(grad, g1, unit, scale_s[at, 0:1])
        resid_s[at, :] = d_resid
        grad_s[at, :] = d_resid.astype(bf16)
        return (sums[0] + fold_rows(d_resid), sums[1] + fold_rows(grad * unit), sums[2] + fold_rows(grad))

    sums = each(tok, BAND, finish, (zero, zero, zero))
    grad = grad_s[...]
    ctx_s[...] = dot(weights[0].reshape(width, width), grad, 1, 1).astype(bf16).reshape(CHIPS, wide, tok)
    dctx_made = [
        w.start(ctx_s.at[chip], dctx_s.at[w.chip], who)
        for chip, who in ((w.cx, w.xn), (w.cy, w.yn), (w.cd, w.dn))
    ]
    dctx_s[w.chip] = ctx_s[w.chip]
    go(PLAN_OPEN)
    for chunk in range(fold):
        weights[1 + chunk] = dot(lowt_s[...], act_s[chunk], 1, 0).astype(bf16).reshape(CHIPS, 2, part, width)
        go(PLAN_IN[chunk])
    weights[0] = dot(ctxt[...].reshape(width, tok), grad, 1, 0).astype(bf16).reshape(CHIPS, 2, part, width)
    for row, value in zip((2, 3, 4), sums):
        put_vector(tiny_s, row, settle(value), part)
    go(PLAN_IN[fold])

    dq_s = slope_s.at[:, 0:wide, 0:tok]
    dkv_a[...] = jnp.zeros_like(dkv_a)
    steps = PLANE * tok // SPAN
    for turn_no, index in enumerate((w.chip, w.cx, w.cy, w.cd)):
        if turn_no:
            dctx_made[turn_no - 1].wait_recv()
        dt = dctx_s[index]
        product = dt.astype(f32) * ctx32[index]
        delta = [
            jnp.sum(product[head * hd : (head + 1) * hd], axis=0, keepdims=True) for head in range(heads)
        ]
        dq_s[index] = attend_back(
            qt[index], dt, log[index], delta, kv_s, kt, segk, segq[2 * index + core], dkv_a, 0, steps, hd
        )
        go(PLAN_BACK[turn_no])

    dkv_s = hid_s.at[:, 0, :, 0 : 2 * wide]
    dkv_land = hid_s.at[:, 1, :, 0 : 2 * wide]

    def away(index, carry):
        at = pl.ds(pl.multiple_of((2 * index + 1 - core) * tok, tok), tok)
        dkv_s[index] = dkv_a[at, :].astype(bf16)
        return carry

    lax.fori_loop(0, CHIPS, away, 0)
    meet = w.start(dkv_s, dkv_land, w.mate)
    go(PLAN_MEET)
    meet.wait_recv()

    def join(index, sums):
        at = pl.ds(pl.multiple_of((2 * index + core) * tok, tok), tok)
        dkv = dkv_a[at, :] + dkv_land[index].astype(f32)
        dqkv = jnp.concatenate([dkv, (dq_s[index] * scale_factor).T], axis=1)
        dqkv_s[index] = dqkv.astype(bf16)
        return sums + jnp.sum(dqkv, axis=0, keepdims=True)

    sums = lax.fori_loop(0, CHIPS, join, jnp.zeros((1, 3 * wide), f32))
    for half in range(2):
        at = slice(half * width // 2, (half + 1) * width // 2)
        total = sum(dot(hidt[index, at, :], dqkv_s[index], 1, 0) for index in range(CHIPS))
        gq_s[2 * half : 2 * half + 2] = total.astype(bf16).reshape(2, 2, part, 3 * wide)
    q_meet = w.start(gq_s.at[:, 1 - core], q_pair, w.mate)
    go(PLAN_GRAD)
    for side in range(2):
        slot = 2 * w.chip + side
        tiny_s[slot, 0:1, :part] = sums[:, 2 * wide + side * part : 2 * wide + (side + 1) * part]
        tiny_s[slot, 1:2, :part] = sums[:, wide + side * part : wide + (side + 1) * part]
    tinies = [
        w.start(tiny_s.at[(me + step) % PLANE], s_land.at[me], (me + step) % PLANE)
        for step in range(1, PLANE)
    ]
    s_land[me] = tiny_s[me]
    dh_s = act_s
    hidden = Reduce(w, None, dh_s, dh_land)

    q_meet.wait_recv()
    add_into(q_pair, gq_s.at[:, core])
    q_made = [
        w.start(q_pair.at[chip], q_all.at[w.chip], who)
        for chip, who in ((w.cx, w.xn), (w.cy, w.yn), (w.cd, w.dn))
    ]
    q_all[w.chip] = q_pair[w.chip]
    halves = [pl.ds(0, part // 2), pl.ds(part // 2, part // 2)]
    q_lines = [
        Line(w, z, q_all.at[chip, rows], zq_land.at[chip, :, rows], dq_o.at[chip, rows])
        for chip in (w.chip, w.cx, w.cy, w.cd)
        for rows in halves
    ]
    q_lines[0].first()
    q_lines[1].first()
    go(PLAN_SENT)

    def input_grad(index, carry):
        dh_s[index] = dot(dqkv_s[index], wq_a[...].reshape(width, 3 * wide), 1, 1).astype(bf16)
        return carry

    lax.fori_loop(0, CHIPS, input_grad, 0)
    hidden.first()
    for one in tinies:
        one.wait_recv()
    s_sum[...] = jnp.sum(s_land[...], axis=0)
    s_line = Line(w, z, s_sum, zs_land, small_o)
    s_line.first()
    go(PLAN_END[0])
    for slot in (1, 2, 3):
        q_made[slot - 1].wait_recv()
        for half in range(2):
            q_lines[2 * slot + half].first()
        for half in range(2):
            q_lines[2 * slot - 2 + half].second()
        if slot > 1:
            for half in range(2):
                q_lines[2 * slot - 4 + half].third()
        go(PLAN_END[slot])
    s_line.second()
    q_lines[4].third()
    q_lines[6].second()
    q_lines[5].third()
    q_lines[7].second()
    hidden.second()
    go(tuple(left))
    s_line.third()
    q_lines[6].third()
    q_lines[7].third()
    hidden.third(dh_o)
    for one in [q_mate, q_x, q_y, q_d] + q_on + smalls + tinies + q_made + [q_meet, meet] + dctx_made:
        one.wait_send()
    for one in chunks + [hidden]:
        one.done()
    for one in lines + q_lines + [s_line]:
        one.done()
    dh_o[...] = (resid_s[...] + dh_o[...].astype(f32)).astype(dh_o.dtype)


def layer_all(hid, wq, small, wo, wi, wb, cot, hd):
    tok, width = hid.shape
    wide = width // CHIPS
    part = wq.shape[0]
    ff = wi.shape[1]
    fold = ff // width
    seq = PLANE * tok
    rows, cols = wo.shape
    count = wb.shape[0] // rows + fold + 1
    q_block = (CHIPS, part, 3 * wide)
    shape = jax.ShapeDtypeStruct
    outs = [
        shape((tok, width), bf16),
        shape(q_block, bf16),
        shape(wb.shape, bf16),
        shape(wi.shape, bf16),
        shape(wo.shape, bf16),
        shape((tok, width), f32),
        shape((16, 128), f32),
    ]
    pairs = (CHIPS, 2)
    heads_block = (CHIPS, wide, tok)
    scratch = [
        VMEM((count,) + pairs + wo.shape, bf16),
        VMEM((PLANE, 16, 128), bf16),
        VMEM(q_block, bf16),
        VMEM((PLANE, part, 3 * wide), bf16),
        VMEM(pairs + (tok, width), bf16),
        VMEM((CHIPS, width, tok), bf16),
        VMEM(heads_block, bf16),
        VMEM((wide // hd, seq, 2 * hd), bf16),
        VMEM((wide, seq), bf16),
        VMEM((wide, seq), bf16),
        VMEM((seq, 128), f32),
        VMEM((PLANE, 1, tok), f32),
        VMEM(heads_block, f32),
        VMEM((CHIPS, wide // hd, tok), f32),
        VMEM(heads_block, bf16),
        VMEM(heads_block, bf16),
        VMEM((tok, width), f32),
        VMEM((fold, 1, width), f32),
        VMEM((tok, width), f32),
        VMEM((tok, 128), f32),
        VMEM((tok, width), bf16),
        VMEM((width, tok), bf16),
        VMEM((fold, tok, width), bf16),
        VMEM((fold, tok, width), f32),
        VMEM((tok, width), f32),
        VMEM((tok, width), bf16),
        VMEM((tok, width), f32),
        VMEM(heads_block, bf16),
        VMEM((seq, 2 * wide), f32),
        VMEM((CHIPS, tok, 3 * wide), bf16),
        VMEM(pairs + (part, 3 * wide), bf16),
        VMEM((PLANE, 16, 128), f32),
        VMEM(q_block, bf16),
        VMEM(q_block, bf16),
        VMEM((count, CHIPS, rows, cols), bf16),
        VMEM((count, 6, rows // 2, cols), bf16),
        VMEM((6, tok // 2, width), bf16),
        VMEM((count, rows, cols), bf16),
        VMEM((PLANE, 16, 128), f32),
        VMEM((16, 128), f32),
        VMEM((CHIPS, 2) + q_block[1:], bf16),
        VMEM((count, 2, rows, cols), bf16),
        VMEM((2, 16, 128), f32),
    ]
    return pl.pallas_call(
        functools.partial(layer_kernel, hd=hd),
        out_shape=outs,
        in_specs=[pl.BlockSpec(memory_space=space) for space in (VMEM, VMEM, VMEM, ANY, ANY, ANY, VMEM)],
        out_specs=[pl.BlockSpec(memory_space=VMEM)] * 7,
        scratch_shapes=scratch + dma_sems(count * 10 + 190) + [pltpu.SemaphoreType.DMA((count,))],
        compiler_params=pltpu.CompilerParams(
            collective_id=1, has_side_effects=True, vmem_limit_bytes=67043328
        ),
        name="layer_all",
    )(hid, wq, small, wo, wi, wb, cot)


def finish_kernel(*refs):
    ins, rest = refs[:7], refs[7:]
    dq_o, db_o, di_o, do_o, dh_o, out_o, qv_o, bi_o = rest[:8]
    vectors, copies, sems = rest[8:14], rest[14:21], rest[21]
    made = [
        pltpu.make_async_copy(one, copy, sems.at[slot]) for slot, (one, copy) in enumerate(zip(ins, copies))
    ]
    for one in made:
        one.start()
    dq, db, di, do, dh, out, tiny = copies
    wide = dq.shape[2] // 3
    width = dh.shape[1]
    part = do.shape[0]
    made[0].wait()
    for chip in range(CHIPS):
        for place, section in enumerate((1, 2, 0)):
            start = section * width + chip * wide
            dq_o[:, start : start + wide] = dq[chip, :, place * wide : (place + 1) * wide].astype(f32)
    for one in made[1:]:
        one.wait()
    db_o[...] = db[...].astype(f32)
    fold = di.shape[1] // width
    for chunk in range(fold):
        for shard in range(PLANE):
            to, start = (shard * fold + chunk) * part, chunk * width + shard * part
            di_o[:, to : to + part] = di[:, start : start + part].astype(f32)
    do_o[...] = do[...].astype(f32)
    dh_o[...] = dh[...]
    out_o[...] = out[...]
    qv_o[...] = tiny[0:2, :part]
    for row, one in enumerate(vectors):
        one[...] = tiny[2 + row : 3 + row, :part]
    bi_o[...] = jnp.concatenate([tiny[8 + row : 9 + row, :part] for row in range(fold)], axis=1)


def finish_all(dq, db, di, do, dh, out, tiny):
    part, wide = dq.shape[1:]
    shape = jax.ShapeDtypeStruct
    ins = (dq, db, di, do, dh, out, tiny)
    outs = [shape((part, CHIPS * wide), f32)] + [shape(one.shape, f32) for one in (db, di, do, dh)]
    outs += [shape(out.shape, out.dtype), shape((2, part), f32), shape((1, db.shape[0]), f32)]
    outs += [shape((1, part), f32)] * 6
    return pl.pallas_call(
        finish_kernel,
        out_shape=outs,
        in_specs=[pl.BlockSpec(memory_space=ANY)] * 7,
        out_specs=[pl.BlockSpec(memory_space=VMEM)] * 14,
        scratch_shapes=[VMEM(one.shape, one.dtype) for one in ins] + [pltpu.SemaphoreType.DMA((7,))],
        compiler_params=pltpu.CompilerParams(vmem_limit_bytes=60 << 20),
        name="finish_all",
    )(*ins)


def fast_body(
    hidden,
    segment_ids,
    w_qkv,
    b_qv,
    w_out,
    b_out,
    gain1,
    shift1,
    w_in,
    b_in,
    w_back,
    b_back,
    gain2,
    shift2,
    cotangent,
):
    tok, width = hidden.shape
    hd = width // HEADS
    part = w_qkv.shape[0]
    ff = w_in.shape[1]
    lines = b_in.shape[0] // 128
    narrow = jnp.concatenate(
        [b_qv] + [one[None] for one in (b_out, gain1, shift1, b_back, gain2, shift2)], axis=0
    )
    small = jnp.concatenate(
        [
            jnp.pad(narrow, ((0, 0), (0, 128 - part))),
            b_in.reshape(lines, 128),
            segment_ids.astype(bf16).reshape(tok // 128, 128),
            jnp.zeros((8 - lines - tok // 128, 128), bf16),
        ],
        axis=0,
    )
    output, dq, db, di, do, dh, tiny = layer_all(
        hidden, w_qkv, small, w_out, w_in, w_back, cotangent, hd
    )
    g_qkv, g_back, g_in, g_out, d_hidden, output, g_qv, g_bin, *vectors = finish_all(
        dq, db, di, do, dh, output, tiny
    )
    g_bout, g_gain1, g_shift1, g_bback, g_gain2, g_shift2 = (one.reshape(part) for one in vectors)
    return (
        output,
        d_hidden,
        g_qkv,
        g_qv,
        g_out,
        g_bout,
        g_gain1,
        g_shift1,
        g_in,
        g_bin.reshape(ff // PLANE),
        g_back,
        g_bback,
        g_gain2,
        g_shift2,
    )


def solution(mesh):
    in_specs = (
        P(("replica", "shard"), None),
        P(("replica", "shard")),
        P("shard", None),
        P(None, "shard"),
        P("shard", None),
        P("shard"),
        P("shard"),
        P("shard"),
        P("shard", None),
        P("shard"),
        P("shard", None),
        P("shard"),
        P("shard"),
        P("shard"),
        P(("replica", "shard"), None),
    )
    out_specs = (
        P(("replica", "shard"), None),
        P(("replica", "shard"), None),
        P("shard", None),
        P(None, "shard"),
        P("shard", None),
        P("shard"),
        P("shard"),
        P("shard"),
        P("shard", None),
        P("shard"),
        P("shard", None),
        P("shard"),
        P("shard"),
        P("shard"),
    )
    paired = mesh.shape["shard"] == PLANE and mesh.shape["replica"] == LINE
    body = fast_body if paired else plain_body
    return jax.shard_map(body, mesh=mesh, in_specs=in_specs, out_specs=out_specs, check_vma=False)
```

```python
import functools
import math

import jax
import jax.numpy as jnp
from jax import lax
from jax.experimental import pallas as pl
from jax.experimental.pallas import tpu as pltpu
from jax.sharding import PartitionSpec as P

HEADS = 12


scale_factor = 0.125
norm_epsilon = 1e-05
masked_value = -1e30


def normalize(resid, gain, shift):
    mean_value = jnp.mean(resid, axis=-1, keepdims=True)
    centered = resid - mean_value
    variance = jnp.mean(centered * centered, axis=-1, keepdims=True)
    return centered * lax.rsqrt(variance + norm_epsilon) * gain + shift


def gelu_exact(values):
    return jax.nn.gelu(values, approximate=False)


def keep_state(state):
    return state


def block_size(count):
    return math.gcd(count, 512)


def masked_scores(query_heads, key_heads, query_segs, key_segs):
    scores = (
        jnp.einsum("qhd,khd->hqk", query_heads, key_heads, preferred_element_type=jnp.float32)
        * scale_factor
    )
    allowed = query_segs[:, None] == key_segs[None, :]
    return (scores, allowed[None])


def grad_block(
    query_heads, dctx_heads, log_total, delta, query_segs, key_heads, value_heads, key_segs
):
    scores, allowed = masked_scores(query_heads, key_heads, query_segs, key_segs)
    probs = jnp.where(allowed, jnp.exp(scores - log_total[:, :, None]), 0.0)
    d_prob = jnp.einsum("qhd,khd->hqk", dctx_heads, value_heads, preferred_element_type=jnp.float32)
    d_scores = (probs * (d_prob - delta[:, :, None])).astype(jnp.bfloat16)
    return (probs.astype(jnp.bfloat16), d_scores)


def plain_body(
    hidden,
    segment_ids,
    w_qkv,
    b_qv,
    w_out,
    b_out,
    gain1,
    shift1,
    w_in,
    b_in,
    w_back,
    b_back,
    gain2,
    shift2,
    cotangent,
):
    tok_rows, width = hidden.shape
    heads = HEADS
    head_dim = width // heads
    seg_low = segment_ids[0]
    seg_high = segment_ids[-1]
    wq_full, wo_full, bqv_full, bo_full, g1_full, s1_full = (
        lax.all_gather(w_qkv, "shard", axis=0, tiled=True),
        lax.all_gather(w_out, "shard", axis=0, tiled=True),
        lax.all_gather(b_qv, "shard", axis=1, tiled=True),
        lax.all_gather(b_out, "shard", axis=0, tiled=True),
        lax.all_gather(gain1, "shard", axis=0, tiled=True),
        lax.all_gather(shift1, "shard", axis=0, tiled=True),
    )
    qkv = jnp.dot(hidden, wq_full, preferred_element_type=jnp.float32)
    bqv_wide = bqv_full.astype(jnp.float32)
    query = (qkv[:, :width] + bqv_wide[0]).astype(jnp.bfloat16)
    keys = qkv[:, width : 2 * width].astype(jnp.bfloat16)
    values = (qkv[:, 2 * width :] + bqv_wide[1]).astype(jnp.bfloat16)
    query_heads = query.reshape(tok_rows, heads, head_dim)
    key_local = keys.reshape(tok_rows, heads, head_dim)
    value_local = values.reshape(tok_rows, heads, head_dim)
    start_state = (
        jnp.full((heads, tok_rows), masked_value, jnp.float32),
        jnp.zeros((heads, tok_rows), jnp.float32),
        jnp.zeros((tok_rows, heads, head_dim), jnp.float32),
    )
    key_piece = lax.all_gather(keys, "shard", axis=0, tiled=True)
    value_piece = lax.all_gather(values, "shard", axis=0, tiled=True)
    seg_piece = lax.all_gather(segment_ids, "shard", axis=0, tiled=True)
    count = key_piece.shape[0]
    block = block_size(count)

    def forward_step(index, state):
        offset = index * block
        key_heads = lax.dynamic_slice_in_dim(key_piece, offset, block, 0).reshape(
            block, heads, head_dim
        )
        value_heads = lax.dynamic_slice_in_dim(value_piece, offset, block, 0).reshape(
            block, heads, head_dim
        )
        key_segs = lax.dynamic_slice_in_dim(seg_piece, offset, block, 0)

        def forward_update(state):
            running_max, running_sum, accum = state
            scores, allowed = masked_scores(query_heads, key_heads, segment_ids, key_segs)
            new_max = jnp.maximum(
                running_max, jnp.max(jnp.where(allowed, scores, masked_value), axis=-1)
            )
            factor = jnp.exp(running_max - new_max)
            weights = jnp.where(allowed, jnp.exp(scores - new_max[:, :, None]), 0.0)
            running_sum = running_sum * factor + jnp.sum(weights, axis=-1)
            accum = accum * factor.T[:, :, None] + jnp.einsum(
                "hqk,khd->qhd",
                weights.astype(jnp.bfloat16),
                value_heads,
                preferred_element_type=jnp.float32,
            )
            return (new_max, running_sum, accum)

        touches = jnp.logical_and(key_segs[0] <= seg_high, key_segs[-1] >= seg_low)
        return lax.cond(touches, forward_update, keep_state, state)

    running_max, running_sum, accum = lax.fori_loop(0, count // block, forward_step, start_state)
    context32 = accum / running_sum.T[:, :, None]
    log_total = running_max + jnp.log(running_sum)
    context = context32.reshape(tok_rows, width).astype(jnp.bfloat16)
    resid1 = (
        hidden.astype(jnp.float32)
        + jnp.dot(context, wo_full, preferred_element_type=jnp.float32)
        + bo_full.astype(jnp.float32)
    )
    normed1, norm1_pull = jax.vjp(
        normalize, resid1, g1_full.astype(jnp.float32), s1_full.astype(jnp.float32)
    )
    wi_full, bi_full, wb_full, bb_full, g2_full, s2_full = (
        lax.all_gather(w_in, "shard", axis=0, tiled=True),
        lax.all_gather(b_in, "shard", axis=0, tiled=True),
        lax.all_gather(w_back, "shard", axis=0, tiled=True),
        lax.all_gather(b_back, "shard", axis=0, tiled=True),
        lax.all_gather(gain2, "shard", axis=0, tiled=True),
        lax.all_gather(shift2, "shard", axis=0, tiled=True),
    )
    normed1_low = normed1.astype(jnp.bfloat16)
    pre = jnp.dot(normed1_low, wi_full, preferred_element_type=jnp.float32) + bi_full.astype(
        jnp.float32
    )
    act, gelu_pull = jax.vjp(gelu_exact, pre)
    act_low = act.astype(jnp.bfloat16)
    resid2 = (
        normed1
        + jnp.dot(act_low, wb_full, preferred_element_type=jnp.float32)
        + bb_full.astype(jnp.float32)
    )
    out32, norm2_pull = jax.vjp(
        normalize, resid2, g2_full.astype(jnp.float32), s2_full.astype(jnp.float32)
    )
    output = out32.astype(jnp.bfloat16)
    d_resid2, grad_gain2, grad_shift2 = norm2_pull(cotangent)
    d_branch2 = d_resid2.astype(jnp.bfloat16)
    grad_b_back = jnp.sum(d_resid2, axis=0)
    grad_w_back = jnp.einsum("tf,td->fd", act_low, d_branch2, preferred_element_type=jnp.float32)
    d_act = jnp.einsum("td,fd->tf", d_branch2, wb_full, preferred_element_type=jnp.float32)
    (d_pre,) = gelu_pull(d_act)
    grad_b_in = jnp.sum(d_pre, axis=0)
    d_pre_low = d_pre.astype(jnp.bfloat16)
    grad_w_in = jnp.einsum("td,tf->df", normed1_low, d_pre_low, preferred_element_type=jnp.float32)
    d_normed1 = d_resid2 + jnp.einsum(
        "tf,df->td", d_pre_low, wi_full, preferred_element_type=jnp.float32
    )
    d_resid1, grad_gain1, grad_shift1 = norm1_pull(d_normed1)
    grad_b_out = jnp.sum(d_resid1, axis=0)
    d_branch1 = d_resid1.astype(jnp.bfloat16)
    grad_w_out = jnp.einsum("tc,td->cd", context, d_branch1, preferred_element_type=jnp.float32)
    d_context = jnp.einsum(
        "td,cd->tc", d_branch1, wo_full, preferred_element_type=jnp.float32
    ).astype(jnp.bfloat16)
    dctx_heads = d_context.reshape(tok_rows, heads, head_dim)
    delta = jnp.einsum("qhd,qhd->hq", dctx_heads.astype(jnp.float32), context32)
    zero_heads = jnp.zeros((tok_rows, heads, head_dim), jnp.float32)
    query_key_piece = lax.all_gather(keys, "shard", axis=0, tiled=True)
    query_value_piece = lax.all_gather(values, "shard", axis=0, tiled=True)
    query_seg_piece = lax.all_gather(segment_ids, "shard", axis=0, tiled=True)
    count = query_key_piece.shape[0]
    query_block = block_size(count)

    def query_step(index, summed):
        offset = index * query_block
        key_heads = lax.dynamic_slice_in_dim(query_key_piece, offset, query_block, 0).reshape(
            query_block, heads, head_dim
        )
        value_heads = lax.dynamic_slice_in_dim(query_value_piece, offset, query_block, 0).reshape(
            query_block, heads, head_dim
        )
        key_segs = lax.dynamic_slice_in_dim(query_seg_piece, offset, query_block, 0)

        def query_update(summed):
            probs, d_scores = grad_block(
                query_heads,
                dctx_heads,
                log_total,
                delta,
                segment_ids,
                key_heads,
                value_heads,
                key_segs,
            )
            return (
                summed
                + jnp.einsum(
                    "hqk,khd->qhd", d_scores, key_heads, preferred_element_type=jnp.float32
                )
                * scale_factor
            )

        touches = jnp.logical_and(key_segs[0] <= seg_high, key_segs[-1] >= seg_low)
        return lax.cond(touches, query_update, keep_state, summed)

    d_query = lax.fori_loop(0, count // query_block, query_step, zero_heads)
    all_log_total, all_delta = (
        lax.all_gather(log_total, "shard", axis=1, tiled=True),
        lax.all_gather(delta, "shard", axis=1, tiled=True),
    )
    query_piece = lax.all_gather(query, "shard", axis=0, tiled=True)
    dctx_piece = lax.all_gather(d_context, "shard", axis=0, tiled=True)
    key_seg_piece = lax.all_gather(segment_ids, "shard", axis=0, tiled=True)
    count = query_piece.shape[0]
    key_block = block_size(count)

    def key_step(index, state):
        offset = index * key_block
        piece_query = lax.dynamic_slice_in_dim(query_piece, offset, key_block, 0).reshape(
            key_block, heads, head_dim
        )
        piece_dctx = lax.dynamic_slice_in_dim(dctx_piece, offset, key_block, 0).reshape(
            key_block, heads, head_dim
        )
        piece_segs = lax.dynamic_slice_in_dim(key_seg_piece, offset, key_block, 0)
        piece_log = lax.dynamic_slice_in_dim(all_log_total, offset, key_block, 1)
        piece_delta = lax.dynamic_slice_in_dim(all_delta, offset, key_block, 1)

        def key_update(state):
            d_key, d_value = state
            probs, d_scores = grad_block(
                piece_query,
                piece_dctx,
                piece_log,
                piece_delta,
                piece_segs,
                key_local,
                value_local,
                segment_ids,
            )
            d_key = (
                d_key
                + jnp.einsum(
                    "hqk,qhd->khd", d_scores, piece_query, preferred_element_type=jnp.float32
                )
                * scale_factor
            )
            d_value = d_value + jnp.einsum(
                "hqk,qhd->khd", probs, piece_dctx, preferred_element_type=jnp.float32
            )
            return (d_key, d_value)

        touches = jnp.logical_and(piece_segs[0] <= seg_high, piece_segs[-1] >= seg_low)
        return lax.cond(touches, key_update, keep_state, state)

    d_key_heads, d_value_heads = lax.fori_loop(
        0, count // key_block, key_step, (zero_heads, zero_heads)
    )
    d_keys = d_key_heads.reshape(tok_rows, width)
    d_values = d_value_heads.reshape(tok_rows, width)
    d_query = d_query.reshape(tok_rows, width)
    grad_b_qv = jnp.stack([jnp.sum(d_query, axis=0), jnp.sum(d_values, axis=0)], axis=0)
    d_qkv = jnp.concatenate([d_query, d_keys, d_values], axis=1).astype(jnp.bfloat16)
    grad_w_qkv = jnp.einsum("td,te->de", hidden, d_qkv, preferred_element_type=jnp.float32)
    d_hidden = d_resid1 + jnp.einsum(
        "te,de->td", d_qkv, wq_full, preferred_element_type=jnp.float32
    )
    local_grads = (
        grad_w_qkv,
        grad_b_qv,
        grad_w_out,
        grad_b_out,
        grad_gain1,
        grad_shift1,
        grad_w_in,
        grad_b_in,
        grad_w_back,
        grad_b_back,
        grad_gain2,
        grad_shift2,
    )
    shard_grads = (
        lax.psum_scatter(
            local_grads[0].astype(jnp.bfloat16), "shard", scatter_dimension=0, tiled=True
        ).astype(jnp.float32),
        lax.psum_scatter(
            local_grads[1].astype(jnp.bfloat16), "shard", scatter_dimension=1, tiled=True
        ).astype(jnp.float32),
        lax.psum_scatter(
            local_grads[2].astype(jnp.bfloat16), "shard", scatter_dimension=0, tiled=True
        ).astype(jnp.float32),
        lax.psum_scatter(
            local_grads[3].astype(jnp.bfloat16), "shard", scatter_dimension=0, tiled=True
        ).astype(jnp.float32),
        lax.psum_scatter(
            local_grads[4].astype(jnp.bfloat16), "shard", scatter_dimension=0, tiled=True
        ).astype(jnp.float32),
        lax.psum_scatter(
            local_grads[5].astype(jnp.bfloat16), "shard", scatter_dimension=0, tiled=True
        ).astype(jnp.float32),
        lax.psum_scatter(
            local_grads[6].astype(jnp.bfloat16), "shard", scatter_dimension=0, tiled=True
        ).astype(jnp.float32),
        lax.psum_scatter(
            local_grads[7].astype(jnp.bfloat16), "shard", scatter_dimension=0, tiled=True
        ).astype(jnp.float32),
        lax.psum_scatter(
            local_grads[8].astype(jnp.bfloat16), "shard", scatter_dimension=0, tiled=True
        ).astype(jnp.float32),
        lax.psum_scatter(
            local_grads[9].astype(jnp.bfloat16), "shard", scatter_dimension=0, tiled=True
        ).astype(jnp.float32),
        lax.psum_scatter(
            local_grads[10].astype(jnp.bfloat16), "shard", scatter_dimension=0, tiled=True
        ).astype(jnp.float32),
        lax.psum_scatter(
            local_grads[11].astype(jnp.bfloat16), "shard", scatter_dimension=0, tiled=True
        ).astype(jnp.float32),
    )
    total_grads = (
        lax.psum(shard_grads[0].astype(jnp.bfloat16), "replica").astype(jnp.float32),
        lax.psum(shard_grads[1].astype(jnp.bfloat16), "replica").astype(jnp.float32),
        lax.psum(shard_grads[2].astype(jnp.bfloat16), "replica").astype(jnp.float32),
        lax.psum(shard_grads[3].astype(jnp.bfloat16), "replica").astype(jnp.float32),
        lax.psum(shard_grads[4].astype(jnp.bfloat16), "replica").astype(jnp.float32),
        lax.psum(shard_grads[5].astype(jnp.bfloat16), "replica").astype(jnp.float32),
        lax.psum(shard_grads[6].astype(jnp.bfloat16), "replica").astype(jnp.float32),
        lax.psum(shard_grads[7].astype(jnp.bfloat16), "replica").astype(jnp.float32),
        lax.psum(shard_grads[8].astype(jnp.bfloat16), "replica").astype(jnp.float32),
        lax.psum(shard_grads[9].astype(jnp.bfloat16), "replica").astype(jnp.float32),
        lax.psum(shard_grads[10].astype(jnp.bfloat16), "replica").astype(jnp.float32),
        lax.psum(shard_grads[11].astype(jnp.bfloat16), "replica").astype(jnp.float32),
    )
    return (output, d_hidden) + tuple(total_grads)


PLANE = 8
LINE = 4
CHIPS = 4
MESH = pl.DeviceIdType.MESH
VMEM = pltpu.VMEM
ANY = pl.ANY
f32 = jnp.float32
bf16 = jnp.bfloat16


class Wires:
    def __init__(self, send, recv):
        self.send, self.recv, self.used = send, recv, 0
        me = lax.axis_index("shard")
        self.me = me
        self.core = me % 2
        self.chip = me // 2
        self.mate = me + 1 - 2 * self.core
        self.xn = me + 2 - 4 * (self.chip % 2)
        self.yn = me + 4 - 8 * (me // 4)
        self.dn = self.xn + 4 - 8 * (me // 4)
        self.cx = self.xn // 2
        self.cy = self.yn // 2
        self.cd = self.dn // 2

    def copy(self, src, dst, where):
        slot = self.used
        self.used += 1
        return pltpu.make_async_remote_copy(
            src_ref=src,
            dst_ref=dst,
            send_sem=self.send.at[slot],
            recv_sem=self.recv.at[slot],
            device_id=where if isinstance(where, dict) else {"shard": where},
            device_id_type=MESH,
        )

    def start(self, src, dst, where):
        made = self.copy(src, dst, where)
        made.start()
        return made


def plane_others(me):
    return [{"shard": (me + step) % PLANE} for step in range(1, PLANE)]


def dma_sems(count):
    return [pltpu.SemaphoreType.DMA((count,)), pltpu.SemaphoreType.DMA((count,))]


class Gather:
    def __init__(self, wires, out, block=None, far=None):
        self.w, self.out, self.far = wires, out, far
        self.half = out.shape[2] // 2
        self.block = self.at(wires.me) if block is None else block
        self.made = []
        self.came = set()

    def at(self, who, *rows):
        if rows:
            return self.out.at[who // 2, who % 2, rows[0]]
        return self.out.at[who // 2, who % 2]

    def start(self, where, who, *rows):
        one = self.w.start(self.at(who, *rows), self.at(who, *rows), where)
        self.made.append(one)
        return one

    def pass_on(self, who):
        one = self.start(self.far, who)
        return one

    def begin(self):
        w, mine = self.w, self.at(self.w.me)
        self.to_x = w.start(self.block, mine, w.xn)
        self.to_y = w.start(self.block, mine, w.yn)
        self.to_mate = w.start(self.block, mine, w.mate)
        self.made += [self.to_x, self.to_y, self.to_mate]

    def relay(self):
        w, half = self.w, self.half
        self.to_x.wait_recv()
        self.x_on = self.start(w.yn, w.xn, pl.ds(0, half))
        if self.far is not None:
            self.x_far = self.pass_on(w.xn)
        self.x_mate = self.start(w.mate, w.xn)
        self.to_y.wait_recv()
        self.y_on = self.start(w.xn, w.yn, pl.ds(half, half))
        if self.far is not None:
            self.y_far = self.pass_on(w.yn)
        self.y_mate = self.start(w.mate, w.yn)

    def finish(self):
        w, half = self.w, self.half
        self.x_on.wait_recv()
        self.d_low = self.start(w.mate, w.dn, pl.ds(0, half))
        self.y_on.wait_recv()
        self.d_high = self.start(w.mate, w.dn, pl.ds(half, half))
        if self.far is not None:
            self.d_far = self.pass_on(w.dn)

    def took(self, *names):
        for name in names:
            if name not in self.came:
                self.came.add(name)
                getattr(self, name).wait_recv()

    def done(self):
        self.took("to_mate", "x_mate", "y_mate", "d_low", "d_high")
        for made in self.made:
            made.wait_send()


class Passed:
    def __init__(self, wires, out, source):
        self.w, self.source = wires, source
        self.near = Gather(wires, out)
        self.relays = []

    def begin(self):
        w = self.w
        self.to_mate = self.near.start(w.mate, w.me)

    def relay(self):
        self.source.x_far.wait_recv()
        self.relays.append(self.near.start(self.w.mate, self.w.xn))
        self.source.y_far.wait_recv()
        self.relays.append(self.near.start(self.w.mate, self.w.yn))

    def finish(self):
        self.source.d_far.wait_recv()
        self.relays.append(self.near.start(self.w.mate, self.w.dn))

    def done(self):
        for made in [self.to_mate] + self.relays:
            made.wait_recv()
        for made in self.near.made:
            made.wait_send()


SPAN = 512
PLAN_DOWN = ((), ("F0",), ("F1",), ("S0", "F2"))
PLAN_OPEN = ()
PLAN_IN = (("M4",), ("M5", "S1"), ("M6", "F3"), ("M7", "S2", "T0"), ("M8", "F4"))
PLAN_BACK = (
    ("S3", "F5", "T1", "Y0"),
    ("S4", "F6", "T2", "Y1", "Z0"),
    ("S5", "F7", "T3", "Y2", "Z1"),
    ("S6", "F8", "T4", "Y3", "Z2"),
)
PLAN_MEET = ("S7", "T5", "Y4", "Z3")
PLAN_GRAD = ("S8", "T6", "Y5", "Z4")
PLAN_SENT = ("T7", "Y6", "Z5")
PLAN_END = (("T8", "Y7", "Z6"), ("Z7",), ("Y8",), ("Z8",))
PAIRED = ((0, 2), (1, 3), (5, 6))
COMMON = (4, 7, 8)
BAND = 32


def dot(left, right, left_dim, right_dim):
    return lax.dot_general(
        left, right, (((left_dim,), (right_dim,)), ((), ())), preferred_element_type=f32
    )


def turn(block):
    return block.astype(f32).T


def allowed_pairs(segk, segq):
    return jnp.concatenate([segk] * (segq.shape[1] // 128), axis=1) == segq


def upper(block):
    return jnp.concatenate([block, jnp.zeros_like(block)], axis=0)


def lower(block):
    return jnp.concatenate([jnp.zeros_like(block), block], axis=0)


def attend(query, kv_ref, vt_ref, segk_ref, segq, hd):
    heads, keys = kv_ref.shape[:2]
    rows = query.shape[1]
    wide = [upper(query[head * hd : (head + 1) * hd]) for head in range(heads)]

    def step(index, state):
        at = pl.ds(pl.multiple_of(index * SPAN, SPAN), SPAN)
        allowed = allowed_pairs(segk_ref[at, :], segq)
        scores = [
            jnp.where(allowed, dot(kv_ref[head, at, :], wide[head], 1, 0), masked_value)
            for head in range(heads)
        ]
        made = []
        for head in range(heads):
            top, total, acc = state[head]
            new = jnp.maximum(top, jnp.max(scores[head], axis=0, keepdims=True))
            weights = jnp.exp(scores[head] - new)
            factor = jnp.exp(top - new)
            made.append(
                (
                    new,
                    total * factor + jnp.sum(weights, axis=0, keepdims=True),
                    acc * factor + dot(vt_ref[head * hd : (head + 1) * hd, at], weights.astype(bf16), 1, 0),
                )
            )
        return tuple(made)

    zero = tuple(
        (
            jnp.full((1, rows), 0.5 * masked_value, f32),
            jnp.zeros((1, rows), f32),
            jnp.zeros((hd, rows), f32),
        )
        for _ in range(heads)
    )
    state = lax.fori_loop(0, keys // SPAN, step, zero)
    return (
        jnp.concatenate([acc / total for _, total, acc in state], axis=0),
        jnp.concatenate([top + jnp.log(total) for top, total, _ in state], axis=0),
    )


def attend_back(qt, dt, log, delta, kv_ref, kt_ref, segk_ref, segq, dkv_ref, start, stop, hd):
    heads = kv_ref.shape[0]
    rows = qt.shape[1]
    part = [slice(head * hd, (head + 1) * hd) for head in range(heads)]
    wide_q = [upper(qt[one]) for one in part]
    wide_d = [lower(dt[one]) for one in part]

    def step(index, state):
        at = pl.ds(pl.multiple_of(index * SPAN, SPAN), SPAN)
        allowed = allowed_pairs(segk_ref[at, :], segq)
        low = []
        for head in range(heads):
            both = kv_ref[head, at, :]
            scores = dot(both, wide_q[head], 1, 0)
            d_prob = dot(both, wide_d[head], 1, 0)
            probs = jnp.where(allowed, jnp.exp(scores - log[head : head + 1]), 0.0)
            low.append((probs.astype(bf16), (probs * (d_prob - delta[head])).astype(bf16)))
        made = [
            state[head] + dot(kt_ref[part[head], at], low[head][1], 1, 0) for head in range(heads)
        ]
        dkv_ref[at, :] += jnp.concatenate(
            [dot(low[head][1], qt[part[head]], 1, 1) for head in range(heads)]
            + [dot(low[head][0], dt[part[head]], 1, 1) for head in range(heads)],
            axis=1,
        )
        return tuple(made)

    zero = tuple(jnp.zeros((hd, rows), f32) for _ in range(heads))
    return jnp.concatenate(lax.fori_loop(start, stop, step, zero), axis=0)


def add_into(dst, other, out=None):
    out = dst if out is None else out
    lead = dst.shape[0] if len(dst.shape) == 3 else 0
    rows = dst.shape[-2]
    band = 48 if rows % 48 == 0 else 32 if rows % 32 == 0 else 16
    steps = rows // band

    def go(index, carry):
        if lead:
            at = (index // steps, pl.ds(pl.multiple_of((index % steps) * band, band), band))
        else:
            at = (pl.ds(pl.multiple_of(index * band, band), band),)
        out[at] = (dst[at] + other[at]).astype(out.dtype)
        return carry

    lax.fori_loop(0, max(lead, 1) * steps, go, 0)


class Reduce:
    def __init__(self, wires, full, pair, land):
        self.w, self.full, self.pair, self.land = wires, full, pair, land
        self.half = pair.shape[1] // 2
        if full is not None:
            self.meet = wires.copy(full.at[:, 1 - wires.core], pair, wires.mate)

    def first(self):
        w, pair, land = self.w, self.pair, self.land
        low, high = pl.ds(0, self.half), pl.ds(self.half, self.half)
        if self.full is not None:
            self.meet.wait_recv()
            add_into(pair, self.full.at[:, w.core])
        self.x0 = w.start(pair.at[w.cd, low], land.at[1], w.xn)
        self.y0 = w.start(pair.at[w.cd, high], land.at[3], w.yn)
        self.x1 = w.start(pair.at[w.cx, low], land.at[0], w.xn)
        self.y1 = w.start(pair.at[w.cy, high], land.at[2], w.yn)

    def second(self):
        w, pair, land = self.w, self.pair, self.land
        low, high = pl.ds(0, self.half), pl.ds(self.half, self.half)
        self.x0.wait_recv()
        add_into(pair.at[w.cy, low], land.at[1])
        self.y2 = w.start(pair.at[w.cy, low], land.at[4], w.yn)
        self.y0.wait_recv()
        add_into(pair.at[w.cx, high], land.at[3])
        self.x2 = w.start(pair.at[w.cx, high], land.at[5], w.xn)
        self.x1.wait_recv()
        add_into(pair.at[w.chip, low], land.at[0])
        self.y1.wait_recv()
        add_into(pair.at[w.chip, high], land.at[2])

    def third(self, out):
        w, pair, land = self.w, self.pair, self.land
        low, high = pl.ds(0, self.half), pl.ds(self.half, self.half)
        self.y2.wait_recv()
        add_into(pair.at[w.chip, low], land.at[4], out.at[low])
        self.x2.wait_recv()
        add_into(pair.at[w.chip, high], land.at[5], out.at[high])

    def done(self):
        made = [self.x0, self.x1, self.y0, self.y1, self.x2, self.y2]
        if self.full is not None:
            made.append(self.meet)
        for one in made:
            one.wait_send()


class Line:
    def __init__(self, wires, z, block, land, out):
        self.w, self.z, self.block, self.land, self.out = wires, z, block, land, out
        self.edge = (z == 0) | (z == LINE - 1)
        self.inner = {"replica": 1 + z // 2}
        self.outer = {"replica": 3 * (z // 2)}
        self.across = {"replica": 2 - z // 2}
        self.up = wires.copy(block, land.at[0], self.inner)
        self.over = wires.copy(block, land.at[1], {"replica": 3 - z})
        self.back = wires.copy(out, out, self.outer)

    def first(self):
        @pl.when(self.edge)
        def _():
            self.up.start()

    def second(self):
        @pl.when(jnp.logical_not(self.edge))
        def _():
            self.up.wait_recv()
            add_into(self.block, self.land.at[0])
            self.over.start()

    def third(self):
        @pl.when(jnp.logical_not(self.edge))
        def _():
            self.over.wait_recv()
            add_into(self.block, self.land.at[1], self.out)
            self.back.start()

    def done(self):
        @pl.when(self.edge)
        def _():
            self.up.wait_send()
            self.back.wait_recv()

        @pl.when(jnp.logical_not(self.edge))
        def _():
            self.over.wait_send()
            self.back.wait_send()


def each(rows, block, step, init):
    def go(index, carry):
        return step(pl.ds(pl.multiple_of(index * block, block), block), carry)

    return lax.fori_loop(0, rows // block, go, init)


def fold_rows(block):
    return jnp.sum(block.reshape(block.shape[0] // 8, 8, block.shape[1]), axis=0)


def settle(block):
    return jnp.sum(block, axis=0, keepdims=True)


def vector(small, row, part):
    return jnp.concatenate(
        [small[source, row : row + 1, :part].astype(f32) for source in range(PLANE)], axis=1
    )


def put_vector(stack, row, value, part):
    for source in range(PLANE):
        stack[source, row : row + 1, :part] = value[:, source * part : (source + 1) * part]


def moments(block):
    mean_value = jnp.mean(block, axis=-1, keepdims=True)
    centered = block - mean_value
    scale = lax.rsqrt(jnp.mean(centered * centered, axis=-1, keepdims=True) + norm_epsilon)
    return centered * scale, scale


def norm_back(grad, gain, unit, scale):
    scaled = grad * gain
    return (
        scaled
        - jnp.mean(scaled, axis=-1, keepdims=True)
        - unit * jnp.mean(scaled * unit, axis=-1, keepdims=True)
    ) * scale


def layer_kernel(
    hid,
    wq,
    b_qv,
    vec2,
    vec3,
    vec4,
    vec5,
    vec6,
    vec7,
    b_in,
    ids_in,
    wo,
    wi,
    wb,
    cot,
    out_o,
    dq_o,
    db_o,
    di_o,
    do_o,
    dh_o,
    small_o,
    weights,
    names_s,
    wq_s,
    wq_a,
    hid_s,
    hidt,
    qt,
    kv_s,
    kt,
    vt,
    segk,
    segq,
    ctx32,
    log,
    ctx_s,
    ctxt,
    acc_s,
    bias_s,
    unit_s,
    scale_s,
    low_s,
    lowt_s,
    act_s,
    slope_s,
    wide_s,
    grad_s,
    resid_s,
    dctx_s,
    dkv_a,
    dqkv_s,
    gq_s,
    tiny_s,
    q_pair,
    q_all,
    pair,
    land,
    dh_land,
    part_s,
    s_land,
    s_sum,
    zq_land,
    z_land,
    zs_land,
    send,
    recv,
    loc,
    *,
    hd,
):
    w = Wires(send, recv)
    z = lax.axis_index("replica")
    me, core = w.me, w.core
    tok, width = hid.shape
    wide = width // CHIPS
    heads = wide // hd
    ff = wi.shape[1]
    part = width // PLANE
    fold = ff // width
    rows_in = ff // PLANE // 128
    seg_row = 8 + rows_in

    loads = [pltpu.make_async_copy(wo, weights.at[0, w.chip, core], loc.at[0])]
    for slot in range(fold):
        loads.append(
            pltpu.make_async_copy(
                wi.at[:, pl.ds(slot * width, width)], pair.at[0, slot], loc.at[1 + slot]
            )
        )
    for slot in range(fold):
        loads.append(
            pltpu.make_async_copy(
                wb.at[pl.ds(slot * part, part)],
                weights.at[1 + fold + slot, w.chip, core],
                loc.at[1 + fold + slot],
            )
        )
    for one in loads:
        one.start()

    barrier = pltpu.get_barrier_semaphore()
    for other in plane_others(me):
        pl.semaphore_signal(barrier, inc=1, device_id=other, device_id_type=MESH)
    edge = (z == 0) | (z == LINE - 1)

    @pl.when(edge)
    def _():
        pl.semaphore_signal(barrier, inc=1, device_id={"replica": 1 + z // 2}, device_id_type=MESH)

    @pl.when(jnp.logical_not(edge))
    def _():
        pl.semaphore_signal(barrier, inc=1, device_id={"replica": 3 * (z // 2)}, device_id_type=MESH)
        pl.semaphore_signal(barrier, inc=1, device_id={"replica": 3 - z}, device_id_type=MESH)

    odd = z % 2
    far = {"replica": z + 1 - 2 * odd}
    for chip in range(CHIPS):
        for place, section in enumerate((1, 2, 0)):
            start = section * width + chip * wide
            wq_s[chip, :, place * wide : (place + 1) * wide] = wq[:, start : start + wide]

    s_sum[...] = jnp.zeros_like(s_sum)
    s_sum[0:2, :part] = b_qv[...].astype(f32)
    for row, one in enumerate((vec2, vec3, vec4, vec5, vec6, vec7)):
        s_sum[2 + row : 3 + row, :part] = one[...].astype(f32).reshape(1, part)
    flat = b_in[...].astype(f32).reshape(1, rows_in * 128)
    for row in range(rows_in):
        s_sum[8 + row : 9 + row, :] = flat[:, row * 128 : (row + 1) * 128]
    flat = ids_in[...].astype(f32).reshape(1, tok)
    for row in range(tok // 128):
        s_sum[seg_row + row : seg_row + row + 1, :] = flat[:, row * 128 : (row + 1) * 128]
    names_s[me] = s_sum[...].astype(bf16)
    wq_a[me] = wq_s[w.chip]
    hid_s[w.chip, core] = hid[...]
    for one in loads:
        one.wait()
    per = PLANE // fold
    for chunk in range(fold):
        weights[1 + chunk, w.chip, core] = jnp.concatenate(
            [
                pair[0, shard // per, :, start : start + part]
                for shard in range(PLANE)
                for start in [(shard % per) * fold * part + chunk * part]
            ],
            axis=1,
        )

    @pl.when(edge)
    def _():
        pl.semaphore_wait(barrier, PLANE)

    @pl.when(jnp.logical_not(edge))
    def _():
        pl.semaphore_wait(barrier, PLANE + 1)

    smalls = [
        w.start(names_s.at[me], names_s.at[me], (me + step) % PLANE) for step in range(1, PLANE)
    ]
    q_mate = w.start(wq_s.at[w.chip], wq_a.at[me], w.mate)
    q_d = w.start(wq_s.at[w.cd], wq_a.at[me], w.dn)
    q_x = w.start(wq_s.at[w.cx], wq_a.at[me], w.xn)
    q_y = w.start(wq_s.at[w.cy], wq_a.at[me], w.yn)
    own_ids = [even + odd * (uneven - even) for even, uneven in PAIRED]
    far_ids = [uneven + odd * (even - uneven) for even, uneven in PAIRED]
    mine = [Gather(w, weights.at[one], far=far) for one in own_ids]
    theirs = [Passed(w, weights.at[one], source) for one, source in zip(far_ids, mine)]
    both = [Gather(w, weights.at[one]) for one in COMMON]
    first = Gather(w, hid_s)
    mine[0].begin()
    first.begin()
    q_on = []
    for came, source in ((q_x, w.xn), (q_y, w.yn), (q_d, w.dn)):
        came.wait_recv()
        q_on.append(w.start(wq_a.at[source], wq_a.at[source], w.mate))
    for made in smalls:
        made.wait_recv()
    for source in range(PLANE):
        ids = names_s[source].astype(f32)[seg_row : seg_row + tok // 128]
        segq[source] = jnp.concatenate([ids[one : one + 1] for one in range(tok // 128)], axis=1)
        for one in range(tok // 128):
            at = source * tok + one * 128
            segk[at : at + 128, :] = jnp.broadcast_to(ids[one : one + 1], (128, 128)).T
    names = [names_s[2 * w.chip + side].astype(f32).T for side in range(2)]
    bias_q = jnp.concatenate([one[:part, 0:1] for one in names], axis=0)
    bias_v = jnp.concatenate([one[:part, 1:2] for one in names], axis=0)
    spread = [
        jnp.concatenate(
            [names_s[source, 8 + row : 9 + row, :].astype(f32) for row in range(rows_in)], axis=1
        )
        for source in range(PLANE)
    ]
    for chunk in range(fold):
        bias_s[chunk] = jnp.concatenate(
            [one[:, chunk * part : (chunk + 1) * part] for one in spread], axis=1
        )
    for made in [q_mate] + q_on:
        made.wait_recv()

    def project(turn_no, carry):
        index = pick_turn(turn_no)
        for own in (True, False):
            side = core if own else 1 - core
            block = hid_s[index, side]
            weight = wq_a[...].reshape(width, 3 * wide)
            rows = pl.ds(pl.multiple_of((2 * index + side) * tok, tok), tok)
            kv = dot(block, weight if own else weight[:, : 2 * wide], 1, 0)
            kvt = kv.T
            low_v = (kvt[wide : 2 * wide] + bias_v).astype(bf16)
            kt[:, rows] = kvt[:wide].astype(bf16)
            vt[:, rows] = low_v
            back = turn(low_v)
            for head in range(heads):
                cols = slice(head * hd, (head + 1) * hd)
                kv_s[head, rows, :] = jnp.concatenate([kv[:, cols], back[:, cols]], axis=1).astype(bf16)
            if own:
                query = kvt[2 * wide :] + bias_q
                qt[index] = (query.astype(bf16).astype(f32) * scale_factor).astype(bf16)
                hidt[index] = turn(block).astype(bf16)
        return carry

    def pick_turn(turn_no):
        return (
            (turn_no == 0) * w.chip + (turn_no == 1) * w.cx + (turn_no == 2) * w.cy + (turn_no == 3) * w.cd
        )

    first.took("to_mate")
    lax.fori_loop(0, 1, project, 0)
    mine[0].relay()
    first.relay()
    for one in mine[1:] + theirs:
        one.begin()
    both[0].begin()
    first.took("x_mate", "y_mate")
    lax.fori_loop(1, 3, project, 0)
    first.finish()
    mine[0].finish()
    mine[1].relay()
    first.took("d_low", "d_high")
    lax.fori_loop(3, 4, project, 0)
    first.done()
    both[1].begin()
    mine[2].relay()
    ctx_made = []
    for turn_no, (index, who) in enumerate(
        ((w.cd, w.dn), (w.cx, w.xn), (w.cy, w.yn), (w.chip, None))
    ):
        context, logs = attend(qt[index], kv_s, vt, segk, segq[2 * index + core], hd)
        ctx32[index] = context
        log[index] = logs
        if who is None:
            ctxt[w.chip] = context.astype(bf16)
        else:
            ctx_s[index] = context.astype(bf16)
            ctx_made.append(w.start(ctx_s.at[index], ctxt.at[w.chip], who))
        if turn_no == 0:
            mine[1].finish()
            both[0].relay()
            both[2].begin()
        if turn_no == 1:
            theirs[0].relay()
            mine[2].finish()
            both[1].relay()
        if turn_no == 2:
            theirs[0].finish()
            both[0].finish()
            theirs[1].relay()
        if turn_no == 3:
            both[2].relay()
            both[1].finish()
    for made in ctx_made:
        made.wait()
    theirs[0].done()
    mine[0].done()

    wo_v = weights[0].reshape(width, width)
    bo, g1, s1, bb, g2, s2 = (vector(names_s, row, part) for row in range(2, 8))
    tiny_s[...] = jnp.zeros_like(tiny_s)
    acc_s[...] = dot(turn(ctxt[...].reshape(width, tok)).astype(bf16), wo_v, 1, 0)

    def open_one(at, carry):
        unit, scale = moments(hid[at, :].astype(f32) + acc_s[at, :] + bo)
        unit_s[at, :] = unit
        scale_s[at, :] = jnp.broadcast_to(scale, (BAND, 128))
        normed = unit * g1 + s1
        low_s[at, :] = normed.astype(bf16)
        acc_s[at, :] = normed + bb
        return carry

    each(tok, BAND, open_one, 0)
    lowt_s[...] = turn(low_s[...]).astype(bf16)
    theirs[1].finish()
    theirs[1].done()
    mine[1].done()
    both[0].done()

    def up(chunk, carry):
        bias = bias_s[chunk]
        wide_s[...] = dot(low_s[...], weights[1 + chunk].reshape(width, width), 1, 0)

        def gelu(at, carry):
            pre = wide_s[at, :] + bias
            phi = 0.5 * (1.0 + lax.erf(pre * math.sqrt(0.5)))
            act_s[chunk, at, :] = (pre * phi).astype(bf16)
            slope_s[chunk, at, :] = phi + pre * (
                jnp.exp(-0.5 * pre * pre) * (1.0 / math.sqrt(2.0 * math.pi))
            )
            return carry

        each(tok, BAND, gelu, 0)
        return carry

    lax.fori_loop(0, fold, up, 0)
    theirs[2].relay()
    both[2].finish()
    theirs[2].finish()
    for one in (mine[2], theirs[2], both[1], both[2]):
        one.done()

    def join_back(chunk, carry):
        acc_s[...] += dot(act_s[chunk], weights[1 + fold + chunk].reshape(width, width), 1, 0)
        return carry

    lax.fori_loop(0, fold, join_back, 0)

    zero = jnp.zeros((8, width), f32)

    def close(at, sums):
        unit, scale = moments(acc_s[at, :])
        out_o[at, :] = (unit * g2 + s2).astype(bf16)
        grad = cot[at, :]
        d_resid = norm_back(grad, g2, unit, scale)
        acc_s[at, :] = d_resid
        grad_s[at, :] = d_resid.astype(bf16)
        return (sums[0] + fold_rows(d_resid), sums[1] + fold_rows(grad * unit), sums[2] + fold_rows(grad))

    sums = each(tok, BAND, close, (zero, zero, zero))
    for row, value in zip((5, 6, 7), sums):
        put_vector(tiny_s, row, settle(value), part)

    picks = [(1 + fold + slot, db_o.at[pl.ds(slot * part, part)]) for slot in range(fold)]
    picks += [(1 + slot, di_o.at[:, pl.ds(slot * width, width)]) for slot in range(fold)]
    picks.append((0, do_o))
    count = len(picks)
    chunks = [
        Reduce(w, weights.at[which], pair.at[slot], land.at[slot]) for slot, (which, _) in enumerate(picks)
    ]
    lines = [
        Line(w, z, part_s.at[slot], z_land.at[slot], out) for slot, (_, out) in enumerate(picks)
    ]
    left = [op + str(slot) for slot in range(count) for op in "MFSTYZ"]

    def go(plan):
        for name in plan:
            left.remove(name)
            slot = int(name[1:])
            chunk, line = chunks[slot], lines[slot]
            if name[0] == "M":
                chunk.meet.start()
            elif name[0] == "F":
                chunk.first()
            elif name[0] == "S":
                chunk.second()
            elif name[0] == "T":
                chunk.third(part_s.at[slot])
                line.first()
            elif name[0] == "Y":
                line.second()
            else:
                line.third()

    for chunk in range(fold):
        grad = grad_s[...]
        wide_s[...] = dot(grad, weights[1 + fold + chunk].reshape(width, width), 1, 1)
        weights[1 + fold + chunk] = (
            dot(turn(act_s[chunk]).astype(bf16), grad, 1, 0).astype(bf16).reshape(CHIPS, 2, part, width)
        )
        go(("M" + str(chunk),))

        def through(at, sums):
            d_pre = wide_s[at, :] * slope_s[chunk, at, :]
            act_s[chunk, at, :] = d_pre.astype(bf16)
            return sums + fold_rows(d_pre)

        put_vector(tiny_s, 8 + chunk, settle(each(tok, BAND, through, zero)), part)
        acc_s[...] += dot(act_s[chunk], weights[1 + chunk].reshape(width, width), 1, 1)
        go(PLAN_DOWN[chunk])

    def finish(at, sums):
        unit = unit_s[at, :]
        grad = acc_s[at, :]
        d_resid = norm_back(grad, g1, unit, scale_s[at, 0:1])
        resid_s[at, :] = d_resid
        grad_s[at, :] = d_resid.astype(bf16)
        return (sums[0] + fold_rows(d_resid), sums[1] + fold_rows(grad * unit), sums[2] + fold_rows(grad))

    sums = each(tok, BAND, finish, (zero, zero, zero))
    grad = grad_s[...]
    ctx_s[...] = dot(weights[0].reshape(width, width), grad, 1, 1).astype(bf16).reshape(CHIPS, wide, tok)
    dctx_made = [
        w.start(ctx_s.at[chip], dctx_s.at[w.chip], who)
        for chip, who in ((w.cx, w.xn), (w.cy, w.yn), (w.cd, w.dn))
    ]
    dctx_s[w.chip] = ctx_s[w.chip]
    go(PLAN_OPEN)
    for chunk in range(fold):
        weights[1 + chunk] = dot(lowt_s[...], act_s[chunk], 1, 0).astype(bf16).reshape(CHIPS, 2, part, width)
        go(PLAN_IN[chunk])
    weights[0] = dot(ctxt[...].reshape(width, tok), grad, 1, 0).astype(bf16).reshape(CHIPS, 2, part, width)
    for row, value in zip((2, 3, 4), sums):
        put_vector(tiny_s, row, settle(value), part)
    go(PLAN_IN[fold])

    dq_s = slope_s.at[:, 0:wide, 0:tok]
    dkv_a[...] = jnp.zeros_like(dkv_a)
    steps = PLANE * tok // SPAN
    for turn_no, index in enumerate((w.chip, w.cx, w.cy, w.cd)):
        if turn_no:
            dctx_made[turn_no - 1].wait_recv()
        dt = dctx_s[index]
        product = dt.astype(f32) * ctx32[index]
        delta = [
            jnp.sum(product[head * hd : (head + 1) * hd], axis=0, keepdims=True) for head in range(heads)
        ]
        dq_s[index] = attend_back(
            qt[index], dt, log[index], delta, kv_s, kt, segk, segq[2 * index + core], dkv_a, 0, steps, hd
        )
        go(PLAN_BACK[turn_no])

    dkv_s = hid_s.at[:, 0, :, 0 : 2 * wide]
    dkv_land = hid_s.at[:, 1, :, 0 : 2 * wide]

    def away(index, carry):
        at = pl.ds(pl.multiple_of((2 * index + 1 - core) * tok, tok), tok)
        dkv_s[index] = dkv_a[at, :].astype(bf16)
        return carry

    lax.fori_loop(0, CHIPS, away, 0)
    meet = w.start(dkv_s, dkv_land, w.mate)
    go(PLAN_MEET)
    meet.wait_recv()

    def join(index, sums):
        at = pl.ds(pl.multiple_of((2 * index + core) * tok, tok), tok)
        dkv = dkv_a[at, :] + dkv_land[index].astype(f32)
        dqkv = jnp.concatenate([dkv, (dq_s[index] * scale_factor).T], axis=1)
        dqkv_s[index] = dqkv.astype(bf16)
        return sums + jnp.sum(dqkv, axis=0, keepdims=True)

    sums = lax.fori_loop(0, CHIPS, join, jnp.zeros((1, 3 * wide), f32))
    for half in range(2):
        at = slice(half * width // 2, (half + 1) * width // 2)
        total = sum(dot(hidt[index, at, :], dqkv_s[index], 1, 0) for index in range(CHIPS))
        gq_s[2 * half : 2 * half + 2] = total.astype(bf16).reshape(2, 2, part, 3 * wide)
    q_meet = w.start(gq_s.at[:, 1 - core], q_pair, w.mate)
    go(PLAN_GRAD)
    for side in range(2):
        slot = 2 * w.chip + side
        tiny_s[slot, 0:1, :part] = sums[:, 2 * wide + side * part : 2 * wide + (side + 1) * part]
        tiny_s[slot, 1:2, :part] = sums[:, wide + side * part : wide + (side + 1) * part]
    tinies = [
        w.start(tiny_s.at[(me + step) % PLANE], s_land.at[me], (me + step) % PLANE)
        for step in range(1, PLANE)
    ]
    s_land[me] = tiny_s[me]
    dh_s = act_s
    hidden = Reduce(w, None, dh_s, dh_land)

    q_meet.wait_recv()
    add_into(q_pair, gq_s.at[:, core])
    q_made = [
        w.start(q_pair.at[chip], q_all.at[w.chip], who)
        for chip, who in ((w.cx, w.xn), (w.cy, w.yn), (w.cd, w.dn))
    ]
    q_all[w.chip] = q_pair[w.chip]
    halves = [pl.ds(0, part // 2), pl.ds(part // 2, part // 2)]
    q_lines = [
        Line(w, z, q_all.at[chip, rows], zq_land.at[chip, :, rows], dq_o.at[chip, rows])
        for chip in (w.chip, w.cx, w.cy, w.cd)
        for rows in halves
    ]
    q_lines[0].first()
    q_lines[1].first()
    go(PLAN_SENT)

    def input_grad(index, carry):
        dh_s[index] = dot(dqkv_s[index], wq_a[...].reshape(width, 3 * wide), 1, 1).astype(bf16)
        return carry

    lax.fori_loop(0, CHIPS, input_grad, 0)
    hidden.first()
    for one in tinies:
        one.wait_recv()
    s_sum[...] = jnp.sum(s_land[...], axis=0)
    s_line = Line(w, z, s_sum, zs_land, small_o)
    s_line.first()
    go(PLAN_END[0])
    for slot in (1, 2, 3):
        q_made[slot - 1].wait_recv()
        for half in range(2):
            q_lines[2 * slot + half].first()
        for half in range(2):
            q_lines[2 * slot - 2 + half].second()
        if slot > 1:
            for half in range(2):
                q_lines[2 * slot - 4 + half].third()
        go(PLAN_END[slot])
    s_line.second()
    q_lines[4].third()
    q_lines[6].second()
    q_lines[5].third()
    q_lines[7].second()
    hidden.second()
    go(tuple(left))
    s_line.third()
    q_lines[6].third()
    q_lines[7].third()
    hidden.third(dh_o)
    for one in [q_mate, q_x, q_y, q_d] + q_on + smalls + tinies + q_made + [q_meet, meet] + dctx_made:
        one.wait_send()
    for one in chunks + [hidden]:
        one.done()
    for one in lines + q_lines + [s_line]:
        one.done()
    dh_o[...] = (resid_s[...] + dh_o[...].astype(f32)).astype(dh_o.dtype)


def layer_all(hid, wq, vectors, wo, wi, wb, cot, hd):
    tok, width = hid.shape
    wide = width // CHIPS
    part = wq.shape[0]
    ff = wi.shape[1]
    fold = ff // width
    seq = PLANE * tok
    rows, cols = wo.shape
    count = wb.shape[0] // rows + fold + 1
    q_block = (CHIPS, part, 3 * wide)
    shape = jax.ShapeDtypeStruct
    outs = [
        shape((tok, width), bf16),
        shape(q_block, bf16),
        shape(wb.shape, bf16),
        shape(wi.shape, bf16),
        shape(wo.shape, bf16),
        shape((tok, width), f32),
        shape((16, 128), f32),
    ]
    pairs = (CHIPS, 2)
    heads_block = (CHIPS, wide, tok)
    scratch = [
        VMEM((count,) + pairs + wo.shape, bf16),
        VMEM((PLANE, 16, 128), bf16),
        VMEM(q_block, bf16),
        VMEM((PLANE, part, 3 * wide), bf16),
        VMEM(pairs + (tok, width), bf16),
        VMEM((CHIPS, width, tok), bf16),
        VMEM(heads_block, bf16),
        VMEM((wide // hd, seq, 2 * hd), bf16),
        VMEM((wide, seq), bf16),
        VMEM((wide, seq), bf16),
        VMEM((seq, 128), f32),
        VMEM((PLANE, 1, tok), f32),
        VMEM(heads_block, f32),
        VMEM((CHIPS, wide // hd, tok), f32),
        VMEM(heads_block, bf16),
        VMEM(heads_block, bf16),
        VMEM((tok, width), f32),
        VMEM((fold, 1, width), f32),
        VMEM((tok, width), f32),
        VMEM((tok, 128), f32),
        VMEM((tok, width), bf16),
        VMEM((width, tok), bf16),
        VMEM((fold, tok, width), bf16),
        VMEM((fold, tok, width), f32),
        VMEM((tok, width), f32),
        VMEM((tok, width), bf16),
        VMEM((tok, width), f32),
        VMEM(heads_block, bf16),
        VMEM((seq, 2 * wide), f32),
        VMEM((CHIPS, tok, 3 * wide), bf16),
        VMEM(pairs + (part, 3 * wide), bf16),
        VMEM((PLANE, 16, 128), f32),
        VMEM(q_block, bf16),
        VMEM(q_block, bf16),
        VMEM((count, CHIPS, rows, cols), bf16),
        VMEM((count, 6, rows // 2, cols), bf16),
        VMEM((6, tok // 2, width), bf16),
        VMEM((count, rows, cols), bf16),
        VMEM((PLANE, 16, 128), f32),
        VMEM((16, 128), f32),
        VMEM((CHIPS, 2) + q_block[1:], bf16),
        VMEM((count, 2, rows, cols), bf16),
        VMEM((2, 16, 128), f32),
    ]
    return pl.pallas_call(
        functools.partial(layer_kernel, hd=hd),
        out_shape=outs,
        in_specs=[pl.BlockSpec(memory_space=space) for space in [VMEM] * 11 + [ANY] * 3 + [VMEM]],
        out_specs=[pl.BlockSpec(memory_space=VMEM)] * 7,
        scratch_shapes=scratch + dma_sems(count * 10 + 190) + [pltpu.SemaphoreType.DMA((count,))],
        compiler_params=pltpu.CompilerParams(
            collective_id=1, has_side_effects=True, vmem_limit_bytes=67043328
        ),
        name="layer_all",
    )(hid, wq, *vectors, wo, wi, wb, cot)


def finish_kernel(*refs):
    ins, rest = refs[:7], refs[7:]
    dq_o, db_o, di_o, do_o, dh_o, out_o, qv_o, bi_o = rest[:8]
    vectors, copies, sems = rest[8:14], rest[14:21], rest[21]
    made = [
        pltpu.make_async_copy(one, copy, sems.at[slot]) for slot, (one, copy) in enumerate(zip(ins, copies))
    ]
    for one in made:
        one.start()
    dq, db, di, do, dh, out, tiny = copies
    wide = dq.shape[2] // 3
    width = dh.shape[1]
    part = do.shape[0]
    made[0].wait()
    for chip in range(CHIPS):
        for place, section in enumerate((1, 2, 0)):
            start = section * width + chip * wide
            dq_o[:, start : start + wide] = dq[chip, :, place * wide : (place + 1) * wide].astype(f32)
    for one in made[1:]:
        one.wait()
    db_o[...] = db[...].astype(f32)
    fold = di.shape[1] // width
    for chunk in range(fold):
        for shard in range(PLANE):
            to, start = (shard * fold + chunk) * part, chunk * width + shard * part
            di_o[:, to : to + part] = di[:, start : start + part].astype(f32)
    do_o[...] = do[...].astype(f32)
    dh_o[...] = dh[...]
    out_o[...] = out[...]
    qv_o[...] = tiny[0:2, :part]
    for row, one in enumerate(vectors):
        one[...] = tiny[2 + row : 3 + row, :part]
    bi_o[...] = jnp.concatenate([tiny[8 + row : 9 + row, :part] for row in range(fold)], axis=1)


def finish_all(dq, db, di, do, dh, out, tiny):
    part, wide = dq.shape[1:]
    shape = jax.ShapeDtypeStruct
    ins = (dq, db, di, do, dh, out, tiny)
    outs = [shape((part, CHIPS * wide), f32)] + [shape(one.shape, f32) for one in (db, di, do, dh)]
    outs += [shape(out.shape, out.dtype), shape((2, part), f32), shape((1, db.shape[0]), f32)]
    outs += [shape((1, part), f32)] * 6
    return pl.pallas_call(
        finish_kernel,
        out_shape=outs,
        in_specs=[pl.BlockSpec(memory_space=ANY)] * 7,
        out_specs=[pl.BlockSpec(memory_space=VMEM)] * 14,
        scratch_shapes=[VMEM(one.shape, one.dtype) for one in ins] + [pltpu.SemaphoreType.DMA((7,))],
        compiler_params=pltpu.CompilerParams(vmem_limit_bytes=60 << 20),
        name="finish_all",
    )(*ins)


def fast_body(
    hidden,
    segment_ids,
    w_qkv,
    b_qv,
    w_out,
    b_out,
    gain1,
    shift1,
    w_in,
    b_in,
    w_back,
    b_back,
    gain2,
    shift2,
    cotangent,
):
    tok, width = hidden.shape
    hd = width // HEADS
    part = w_qkv.shape[0]
    ff = w_in.shape[1]
    vectors = (b_qv, b_out, gain1, shift1, b_back, gain2, shift2, b_in, segment_ids)
    output, dq, db, di, do, dh, tiny = layer_all(
        hidden, w_qkv, vectors, w_out, w_in, w_back, cotangent, hd
    )
    g_qkv, g_back, g_in, g_out, d_hidden, output, g_qv, g_bin, *sums = finish_all(
        dq, db, di, do, dh, output, tiny
    )
    g_bout, g_gain1, g_shift1, g_bback, g_gain2, g_shift2 = (one.reshape(part) for one in sums)
    return (
        output,
        d_hidden,
        g_qkv,
        g_qv,
        g_out,
        g_bout,
        g_gain1,
        g_shift1,
        g_in,
        g_bin.reshape(ff // PLANE),
        g_back,
        g_bback,
        g_gain2,
        g_shift2,
    )


def solution(mesh):
    in_specs = (
        P(("replica", "shard"), None),
        P(("replica", "shard")),
        P("shard", None),
        P(None, "shard"),
        P("shard", None),
        P("shard"),
        P("shard"),
        P("shard"),
        P("shard", None),
        P("shard"),
        P("shard", None),
        P("shard"),
        P("shard"),
        P("shard"),
        P(("replica", "shard"), None),
    )
    out_specs = (
        P(("replica", "shard"), None),
        P(("replica", "shard"), None),
        P("shard", None),
        P(None, "shard"),
        P("shard", None),
        P("shard"),
        P("shard"),
        P("shard"),
        P("shard", None),
        P("shard"),
        P("shard", None),
        P("shard"),
        P("shard"),
        P("shard"),
    )
    paired = mesh.shape["shard"] == PLANE and mesh.shape["replica"] == LINE
    body = fast_body if paired else plain_body
    return jax.shard_map(body, mesh=mesh, in_specs=in_specs, out_specs=out_specs, check_vma=False)
```
